32 devices in a mesh: section: 2 (over x), fsdp: 4 (over z), tp: 4 (over y, core).
Axes of the slice: x: 2, y: 2, z: 4, core: 2. Of those that a mesh axis runs over, the one named last changes fastest.
Arguments:
- inputs: bfloat16 [2, 1024, 1024], P(None, ('fsdp', 'tp')), may hold values from -6 to 6
- segment_ids: int32 [2, 4, 256], P(None, 'fsdp'), may hold values from 0 to 3, never falling along the last dimension, each value on 1 to 128 neighbouring positions
- routes: int32 [2, 2, 1024, 8], P('section', None, 'fsdp'), may hold values from 0 to 31, all different within a row; in each aligned block of 256 rows (0 to 255, 256 to 511, ..., all dimensions but the last counted through in order) at most 128 rows name the same one
- w_query: bfloat16 [2, 1024, 1024], P('section', 'fsdp', 'tp'), may hold values from -0.1875 to 0.1875
- key_weight: bfloat16 [2, 1024, 512], P('section', 'fsdp', 'tp'), may hold values from -0.1875 to 0.1875
- value_weight: bfloat16 [2, 1024, 512], P('section', 'fsdp', 'tp'), may hold values from -0.1875 to 0.1875
- w_output: bfloat16 [2, 1024, 1024], P('section', ('tp', 'fsdp')), may hold values from -1.5 to 1.5
- w_router: bfloat16 [2, 1024, 32], P('section', 'fsdp'), may hold values from -0.375 to 0.375
- gain_attn: float32 [2, 1024], P('section', 'fsdp'), may hold values from 0.5 to 1.5
- gain_moe: float32 [2, 1024], P('section', 'fsdp'), may hold values from 0.5 to 1.5
- w_gate: bfloat16 [2, 32, 1024, 512], P('section', None, 'fsdp', 'tp'), may hold values from -0.1875 to 0.1875
- w_up: bfloat16 [2, 32, 1024, 512], P('section', None, 'fsdp', 'tp'), may hold values from -0.1875 to 0.1875
- w_down: bfloat16 [2, 32, 512, 1024], P('section', None, ('tp', 'fsdp')), may hold values from -1 to 1
- out_grad: bfloat16 [2, 1024, 1024], P(None, ('fsdp', 'tp')), may hold values from -6 to 6
Outputs:
- layer_outputs: bfloat16 [2, 2, 1024, 1024], P('section', None, ('fsdp', 'tp'))
- input_grads: float32 [2, 2, 1024, 1024], P('section', None, ('fsdp', 'tp'))
- w_query_grad: float32 [2, 1024, 1024], P('section', 'fsdp', 'tp')
- w_key_grad: float32 [2, 1024, 512], P('section', 'fsdp', 'tp')
- w_value_grad: float32 [2, 1024, 512], P('section', 'fsdp', 'tp')
- w_output_grad: float32 [2, 1024, 1024], P('section', ('tp', 'fsdp'))
- w_router_grad: float32 [2, 1024, 32], P('section', 'fsdp')
- gain_attn_grad: float32 [2, 1024], P('section', 'fsdp')
- gain_moe_grad: float32 [2, 1024], P('section', 'fsdp')
- w_gate_grad: float32 [2, 32, 1024, 512], P('section', None, 'fsdp', 'tp')
- w_up_grad: float32 [2, 32, 1024, 512], P('section', None, 'fsdp', 'tp')
- w_down_grad: float32 [2, 32, 512, 1024], P('section', None, ('tp', 'fsdp'))
The draws below stay inside these ranges and needn't reach their ends.
Inputs may be any that keep to these rules, and one draw needn't show every extreme that they name: `segment_ids`: within a group the numbers never fall; each sequence has 1 to 128 tokens and one has exactly 128. `routes`: A token names 8 different experts; the 256 tokens of one group name no expert more than 128 times in one layer, a bound that some block reaches.
All inputs are finite; a program needn't handle non-finite values.
Results may differ from the reference program's by a relative error of at most 0.04.
Values may be sent and summed in bfloat16 or wider, within the bound.
A program may use at most 384 MiB of HBM per device.

```python
import math
from functools import partial
import jax
import jax.numpy as jnp
import numpy as np
from jax import lax

MODEL_DIM = 1024
QUERY_HEADS = 16
KEY_VALUE_HEADS = 8
HEAD_SIZE = 64
E = 32
FF = 512
TOP = 8
TOK_DEV = 256
CAP = 128
MICRO = 2
SEG_COUNT = 4
SEGMAX = 128
TOKENS_MB = 1024
N_SECTION = 2
N_FSDP = 4


def shard_levels(own_key, extent, split, low, high):
    loudness = 1.0
    for dim, blocks in split:
        draws = jax.random.uniform(jax.random.fold_in(jax.random.fold_in(own_key, 6), dim), (blocks,), jnp.float32, low / len(split), high / len(split))
        loudness = loudness * jnp.repeat(jnp.exp(draws), extent[dim] // blocks).reshape((-1,) + (1,) * (len(extent) - 1 - dim))
    return loudness


def split_up(count, total, most, lean):
    loads = [(1 << 20) // math.isqrt(standing ** lean) + 1 for standing in range(2, count + 1)]
    rest, given = total - most - (count - 1), [1] * (count - 1)
    while rest > 0:
        candidates = [i for i in range(count - 1) if given[i] < most]
        pool, left = sum([loads[i] for i in candidates]), rest
        for i in candidates:
            more = min(most - given[i], max(1, left * loads[i] // pool), rest)
            given[i] = given[i] + more
            rest = rest - more
    return np.array([most] + given)


def ragged_sizes(stream_key, number_of, total, limit, skew):
    if number_of == 2:
        one = jax.random.randint(stream_key, (), max(1, total - limit), min(limit, total - 1) + 1)
        return jnp.stack([one, total - one])
    tallies = jnp.asarray(split_up(number_of, total, limit, skew), jnp.int32)
    twos = (number_of - 1) // 2
    source_of, sink = tallies[1:1 + 2 * twos:2], tallies[2:2 + 2 * twos:2]
    room = jnp.minimum(source_of - 1, limit - sink)
    shifted = jax.random.randint(jax.random.fold_in(stream_key, 1), (twos,), 0, 1 << 20) % (room + 1)
    tallies = tallies.at[1:1 + 2 * twos:2].set(source_of - shifted).at[2:2 + 2 * twos:2].set(sink + shifted)
    return tallies[jax.random.permutation(jax.random.fold_in(stream_key, 2), number_of)]


def routed_block(stream_key, own, number, rows, number_of, top, most, lean):
    order = jax.random.permutation(stream_key, number_of)
    heavy_load, common = shares(number_of, rows * top, most, lean, True), shares(number_of, rows * top, most, lean, False)
    places = jnp.arange(number_of)

    def named(tallies, offset_by):
        used = int((tallies > 0).sum())
        fixed = max(1, used // 4)
        passed = fixed + (places - fixed + offset_by * (used - fixed)) % max(1, number_of - fixed)
        return jnp.zeros((number_of,), jnp.int32).at[order[jnp.where(places < fixed, places, passed)]].set(jnp.asarray(tallies, jnp.int32))

    tallies = jnp.where(number % 4 == 0, named(heavy_load, number // 4), named(common, number - number // 4 - 1))
    mixed = jax.random.permutation(jax.random.fold_in(own, 3), number_of)
    source_of, sink = mixed[0:number_of // 2 * 2:2], mixed[1:number_of // 2 * 2:2]
    room = jnp.minimum(tallies[source_of] - 1, most - tallies[sink]) // 2
    room = jnp.where((source_of == order[0]) | (sink == order[0]) | (tallies[sink] == 0), 0, jnp.maximum(room, 0))
    passed = jax.random.randint(jax.random.fold_in(own, 4), (number_of // 2,), 0, 1 << 20) % (room + 1)
    tallies = tallies.at[source_of].add(-passed).at[sink].add(passed)
    members = jnp.searchsorted(jnp.cumsum(tallies), jnp.arange(rows * top), side="right").astype(jnp.int32)
    grid = members.reshape(top, rows).T
    grid = grid[jax.random.permutation(jax.random.fold_in(own, 1), rows)]
    offset_by = jax.random.randint(jax.random.fold_in(own, 2), (rows, 1), 0, top)
    return jnp.take_along_axis(grid, (jnp.arange(top)[None, :] + offset_by) % top, axis=1)


def shares(amount, total, most, slope, full):
    portions = [(1 << 20) // math.isqrt(grade ** slope) + 1 for grade in range(1, amount + 1)]
    largest = most if full else min(most, max(-(-total // amount), total * portions[0] // sum(portions)))
    least = 1 if total - largest >= amount - 1 else 0
    counts, spare = [largest] + [least] * (amount - 1), total - largest - least * (amount - 1)
    while spare > 0:
        free = [i for i in range(1, amount) if counts[i] < largest] or [i for i in range(1, amount) if counts[i] < most]
        pool, left = sum([portions[i] for i in free]), spare
        for i in free:
            addition = min(most - counts[i], max(1, left * portions[i] // pool), spare)
            counts[i] = counts[i] + addition
            spare = spare - addition
    return np.array(counts)


def normal_values(stream_key, shape, width, most, cuts=(), kind=jnp.bfloat16):
    values = width * jax.random.normal(stream_key, shape, jnp.float32)
    if cuts:
        values = values * shard_levels(stream_key, shape, cuts, -0.22, 0.18)
    return jnp.clip(values, -most, most).astype(kind)


def setup_inputs(seed: int = 0) -> dict:
    splits = jax.random.split(jax.random.key(seed), 15)
    inputs = normal_values(splits[0], (MICRO, TOKENS_MB, MODEL_DIM), 1.0, 6.0, ((1, 16),))
    segment_ids = jax.vmap(lambda own: jnp.searchsorted(jnp.cumsum(ragged_sizes(own, SEG_COUNT, TOK_DEV, SEGMAX, 1)), jnp.arange(TOK_DEV), side="right"))(jax.random.split(splits[1], MICRO * N_FSDP)).reshape((MICRO, N_FSDP, TOK_DEV)).astype(jnp.int32)
    routes_keys = jax.random.split(jax.random.fold_in(splits[2], 1), N_SECTION * MICRO * TOKENS_MB // TOK_DEV)
    routes_turns = jax.random.permutation(jax.random.fold_in(splits[2], 3), N_SECTION * MICRO * TOKENS_MB // TOK_DEV)
    routes = jax.vmap(lambda own, number: routed_block(jax.random.fold_in(splits[2], 2), own, number, TOK_DEV, E, TOP, CAP, 1))(routes_keys, routes_turns).reshape((N_SECTION, MICRO, TOKENS_MB, TOP))
    w_query = normal_values(splits[3], (N_SECTION, MODEL_DIM, QUERY_HEADS * HEAD_SIZE), MODEL_DIM ** -0.5, 0.1875, ((0, 2), (1, 4), (2, 4)))
    key_weight = normal_values(splits[4], (N_SECTION, MODEL_DIM, KEY_VALUE_HEADS * HEAD_SIZE), MODEL_DIM ** -0.5, 0.1875, ((0, 2), (1, 4), (2, 4)))
    value_weight = normal_values(splits[5], (N_SECTION, MODEL_DIM, KEY_VALUE_HEADS * HEAD_SIZE), MODEL_DIM ** -0.5, 0.1875, ((0, 2), (1, 4), (2, 4)))
    w_output = normal_values(splits[6], (N_SECTION, QUERY_HEADS * HEAD_SIZE, MODEL_DIM), (QUERY_HEADS * HEAD_SIZE // 64) ** -0.5, 1.5, ((0, 2), (1, 16)))
    w_router = normal_values(splits[7], (N_SECTION, MODEL_DIM, E), (MODEL_DIM // 4) ** -0.5, 0.375, ((0, 2), (1, 4)))
    gain_attn = jnp.clip(1.0 + 0.1 * jax.random.normal(splits[8], (N_SECTION, MODEL_DIM), jnp.float32), 0.5, 1.5)
    gain_moe = jnp.clip(1.0 + 0.1 * jax.random.normal(splits[9], (N_SECTION, MODEL_DIM), jnp.float32), 0.5, 1.5)
    w_gate = normal_values(splits[10], (N_SECTION, E, MODEL_DIM, FF), MODEL_DIM ** -0.5, 0.1875, ((0, 2), (2, 4), (3, 4)))
    w_up = normal_values(splits[11], (N_SECTION, E, MODEL_DIM, FF), MODEL_DIM ** -0.5, 0.1875, ((0, 2), (2, 4), (3, 4)))
    w_down = normal_values(splits[12], (N_SECTION, E, FF, MODEL_DIM), (FF // 16) ** -0.5, 1.0, ((0, 2), (2, 16)))
    out_grad = normal_values(splits[13], (MICRO, TOKENS_MB, MODEL_DIM), 1.0, 6.0, ((1, 16),))
    return {"inputs": inputs, "segment_ids": segment_ids, "routes": routes, "w_query": w_query, "key_weight": key_weight, "value_weight": value_weight, "w_output": w_output, "w_router": w_router, "gain_attn": gain_attn, "gain_moe": gain_moe, "w_gate": w_gate, "w_up": w_up, "w_down": w_down, "out_grad": out_grad}


norm_eps = 1e-06
branch_scale = 0.22
score_scale = 0.015625
rope_base = 10000.0
masked_score = -1e+30

def norm_rows(vectors, gain_vec):
    inverse = lax.rsqrt(lax.optimization_barrier(jnp.mean(vectors * vectors, axis=-1, keepdims=True)) + norm_eps)
    normed = vectors * inverse
    return (normed * gain_vec, normed, inverse)

def norm_back(upstream, normed, inverse, gain_vec):
    scaled_grad = upstream * gain_vec
    gain_grad = lax.optimization_barrier(jnp.sum(upstream * normed, axis=0))
    inner_mean = lax.optimization_barrier(jnp.mean(scaled_grad * normed, axis=-1, keepdims=True))
    return (inverse * (scaled_grad - normed * inner_mean), gain_grad)

def rope_tables(segment):
    position = jnp.arange(segment.shape[0], dtype=jnp.int32)
    before = jnp.concatenate([jnp.full((1,), -1, dtype=jnp.int32), segment[:-1].astype(jnp.int32)])
    starts = jnp.where(segment != before, position, jnp.zeros_like(position))
    offsets = (position - lax.cummax(starts, axis=0)).astype(jnp.float32)
    half_dim = HEAD_SIZE // 2
    frequency = rope_base ** (-(jnp.arange(half_dim, dtype=jnp.float32) * 2.0 / HEAD_SIZE))
    angles = offsets[:, None] * frequency[None, :]
    return (jnp.cos(angles)[:, None, :], jnp.sin(angles)[:, None, :])

def rotate(vectors, cosine, sine):
    half_dim = vectors.shape[-1] // 2
    front_half = vectors[..., :half_dim]
    back_half = vectors[..., half_dim:]
    return jnp.concatenate([front_half * cosine - back_half * sine, back_half * cosine + front_half * sine], axis=-1)

def rotate_back(vectors, cosine, sine):
    half_dim = vectors.shape[-1] // 2
    front_half = vectors[..., :half_dim]
    back_half = vectors[..., half_dim:]
    return jnp.concatenate([front_half * cosine + back_half * sine, back_half * cosine - front_half * sine], axis=-1)

def allowed_pairs(segment):
    position = jnp.arange(segment.shape[0], dtype=jnp.int32)
    return (segment[:, None] == segment[None, :]) & (position[None, :] <= position[:, None])

def route_tables(route):
    flat_routes = route.reshape(-1)
    onehot = (flat_routes[:, None] == jnp.arange(E, dtype=jnp.int32)[None, :]).astype(jnp.int32)
    rank_list = lax.optimization_barrier(jnp.sum((jnp.cumsum(onehot, axis=0) - 1) * onehot, axis=1))
    slot_index = (flat_routes * CAP + rank_list).astype(jnp.int32)
    owners = jnp.arange(flat_routes.shape[0], dtype=jnp.int32) // TOP
    source = jnp.zeros((E * CAP,), jnp.int32).at[slot_index].set(owners)
    filled = jnp.zeros((E * CAP,), jnp.int32).at[slot_index].set(jnp.ones_like(owners))
    return (slot_index, source, filled)

def dispatch(rows_in, source, filled):
    picked = jnp.take(rows_in, source, axis=0)
    picked = jnp.where(filled[:, None] == 1, picked, jnp.zeros_like(picked))
    return picked.reshape(E, CAP, rows_in.shape[1])

def collect(slot_rows, slot_index):
    flat_rows = slot_rows.reshape(E * CAP, slot_rows.shape[-1])
    return jnp.take(flat_rows, slot_index, axis=0).reshape(-1, TOP, slot_rows.shape[-1]).sum(axis=1)

def place_shares(route_share, slot_index):
    return jnp.zeros((E * CAP,), jnp.float32).at[slot_index].set(route_share.reshape(-1)).reshape(E, CAP)

def attend(query_rows, key_matrix, value_matrix, permitted_mask):
    scores = jnp.einsum('qhgd,khd->hgqk', query_rows.astype(jnp.float32), key_matrix.astype(jnp.float32)) * score_scale
    scores = jnp.where(permitted_mask[None, None], scores, masked_score)
    row_max = lax.optimization_barrier(jnp.max(scores, axis=-1, keepdims=True))
    log_sum_exp = row_max + jnp.log(lax.optimization_barrier(jnp.sum(jnp.exp(scores - row_max), axis=-1, keepdims=True)))
    weights_low = jnp.exp(scores - log_sum_exp).astype(jnp.bfloat16)
    attended = jnp.einsum('hgqk,khd->qhgd', weights_low.astype(jnp.float32), value_matrix.astype(jnp.float32))
    return (attended.astype(jnp.bfloat16), log_sum_exp)

def attention_backward(query_rows, key_matrix, value_matrix, permitted_mask, log_sum_exp, head_gradient):
    scores = jnp.einsum('qhgd,khd->hgqk', query_rows.astype(jnp.float32), key_matrix.astype(jnp.float32)) * score_scale
    scores = jnp.where(permitted_mask[None, None], scores, masked_score)
    weights_full = jnp.exp(scores - log_sum_exp)
    weights_low = weights_full.astype(jnp.bfloat16)
    heads_wide = head_gradient.astype(jnp.float32)
    value_gradient = jnp.einsum('hgqk,qhgd->khd', weights_low.astype(jnp.float32), heads_wide)
    weight_grad = jnp.einsum('qhgd,khd->hgqk', heads_wide, value_matrix.astype(jnp.float32))
    inner_sum = lax.optimization_barrier(jnp.sum(weights_full * weight_grad, axis=-1, keepdims=True))
    score_grad = (weights_full * (weight_grad - inner_sum) * score_scale).astype(jnp.bfloat16).astype(jnp.float32)
    query_gradient = jnp.einsum('hgqk,khd->qhgd', score_grad, key_matrix.astype(jnp.float32))
    key_gradient = jnp.einsum('hgqk,qhgd->khd', score_grad, query_rows.astype(jnp.float32))
    return (query_gradient, key_gradient, value_gradient)

def experts_forward(routed, slot_share, w_gate, w_up, w_down):
    routed_wide = routed.astype(jnp.float32)
    gate_pre = jnp.einsum('ecd,edf->ecf', routed_wide, w_gate.astype(jnp.float32))
    up_pre = jnp.einsum('ecd,edf->ecf', routed_wide, w_up.astype(jnp.float32))
    hidden = gate_pre * jax.nn.sigmoid(gate_pre) * up_pre
    weighted = (slot_share[:, :, None] * hidden).astype(jnp.bfloat16)
    slot_out = jnp.einsum('ecf,efd->ecd', weighted.astype(jnp.float32), w_down.astype(jnp.float32))
    return (slot_out, gate_pre, up_pre)

def experts_backward(slot_share, gate_pre, up_pre, slot_grad, w_gate, w_up, w_down):
    hidden_grad = jnp.einsum('ecd,efd->ecf', slot_grad.astype(jnp.float32), w_down.astype(jnp.float32))
    sigmoid_gate = jax.nn.sigmoid(gate_pre)
    hidden = gate_pre * sigmoid_gate * up_pre
    share_slot = lax.optimization_barrier(jnp.sum(hidden_grad * hidden, axis=-1))
    scaled_grad = slot_share[:, :, None] * hidden_grad
    gate_grad = (scaled_grad * up_pre * sigmoid_gate * (1.0 + gate_pre * (1.0 - sigmoid_gate))).astype(jnp.bfloat16)
    up_grad = (scaled_grad * gate_pre * sigmoid_gate).astype(jnp.bfloat16)
    routed_grad = jnp.einsum('ecf,edf->ecd', gate_grad.astype(jnp.float32), w_gate.astype(jnp.float32))
    routed_grad = routed_grad + jnp.einsum('ecf,edf->ecd', up_grad.astype(jnp.float32), w_up.astype(jnp.float32))
    weighted = (slot_share[:, :, None] * hidden).astype(jnp.bfloat16)
    return (routed_grad, share_slot, gate_grad, up_grad, weighted)

def layer_forward(layer_in, segment, route, weights):
    w_query, key_weight, value_weight, w_output, w_router, gain_attn, gain_moe, w_gate, w_up, w_down = weights
    count_of_tokens = layer_in.shape[0]
    key_value_heads = key_weight.shape[1] // HEAD_SIZE
    residual = layer_in.astype(jnp.float32)
    scaled_one, normed_one, inverse_one = norm_rows(residual, gain_attn)
    attn_in = scaled_one.astype(jnp.bfloat16)
    cosine, sine = rope_tables(segment)
    permitted_mask = allowed_pairs(segment)
    query_rows = rotate(jnp.dot(attn_in, w_query, preferred_element_type=jnp.float32).reshape(count_of_tokens, -1, HEAD_SIZE), cosine, sine)
    query_rows = query_rows.astype(jnp.bfloat16).reshape(count_of_tokens, key_value_heads, QUERY_HEADS // KEY_VALUE_HEADS, HEAD_SIZE)
    key_matrix = rotate(jnp.dot(attn_in, key_weight, preferred_element_type=jnp.float32).reshape(count_of_tokens, key_value_heads, HEAD_SIZE), cosine, sine).astype(jnp.bfloat16)
    value_matrix = jnp.dot(attn_in, value_weight, preferred_element_type=jnp.float32).astype(jnp.bfloat16).reshape(count_of_tokens, key_value_heads, HEAD_SIZE)
    attended, log_sum_exp = attend(query_rows, key_matrix, value_matrix, permitted_mask)
    mixed_heads = attended.reshape(count_of_tokens, -1)
    hidden_state = residual + branch_scale * jnp.dot(mixed_heads, w_output, preferred_element_type=jnp.float32)
    scaled_two, normed_two, inverse_two = norm_rows(hidden_state, gain_moe)
    moe_in = scaled_two.astype(jnp.bfloat16)
    logits = jnp.dot(moe_in, w_router, preferred_element_type=jnp.float32)
    route_share = jax.nn.softmax(jnp.take_along_axis(logits, route, axis=1), axis=-1)
    slot_index, source, filled = route_tables(route)
    slot_share = place_shares(route_share, slot_index)
    routed = dispatch(moe_in, source, filled)
    slot_out, gate_pre, up_pre = experts_forward(routed, slot_share, w_gate, w_up, w_down)
    result = (hidden_state + branch_scale * collect(slot_out, slot_index)).astype(jnp.bfloat16)
    kept_state = (attn_in, query_rows, key_matrix, value_matrix, attended, log_sum_exp, normed_one, inverse_one, normed_two, inverse_two, moe_in, route_share, slot_share, slot_index, source, filled, gate_pre, up_pre, cosine, sine, permitted_mask, route, routed)
    return (result, kept_state)

def layer_backward(upstream, kept_state, weights):
    w_query, key_weight, value_weight, w_output, w_router, gain_attn, gain_moe, w_gate, w_up, w_down = weights
    attn_in, query_rows, key_matrix, value_matrix, attended, log_sum_exp, normed_one, inverse_one, normed_two, inverse_two, moe_in, route_share, slot_share, slot_index, source, filled, gate_pre, up_pre, cosine, sine, permitted_mask, route, routed = kept_state
    count_of_tokens = upstream.shape[0]
    key_value_heads = key_matrix.shape[1]
    moe_grad = (branch_scale * upstream).astype(jnp.bfloat16)
    slot_grad = dispatch(moe_grad, source, filled)
    routed_grad, share_slot, gate_grad, up_grad, weighted = experts_backward(slot_share, gate_pre, up_pre, slot_grad, w_gate, w_up, w_down)
    routed_wide = routed.astype(jnp.float32)
    gate_w = jnp.einsum('ecd,ecf->edf', routed_wide, gate_grad.astype(jnp.float32))
    up_w = jnp.einsum('ecd,ecf->edf', routed_wide, up_grad.astype(jnp.float32))
    down_w = jnp.einsum('ecf,ecd->efd', weighted.astype(jnp.float32), slot_grad.astype(jnp.float32))
    token_grad = collect(routed_grad, slot_index)
    share_grad = jnp.take(share_slot.reshape(-1), slot_index).reshape(count_of_tokens, TOP)
    chosen_grad = route_share * (share_grad - lax.optimization_barrier(jnp.sum(route_share * share_grad, axis=-1, keepdims=True)))
    onehot = (route[:, :, None] == jnp.arange(E, dtype=jnp.int32)[None, None, :]).astype(jnp.float32)
    logit_grad = jnp.einsum('tr,tre->te', chosen_grad, onehot).astype(jnp.bfloat16)
    router_w = jnp.einsum('td,te->de', moe_in.astype(jnp.float32), logit_grad.astype(jnp.float32))
    norm_grad = token_grad + jnp.dot(logit_grad, w_router.T, preferred_element_type=jnp.float32)
    back_two, gain_two = norm_back(norm_grad, normed_two, inverse_two, gain_moe)
    hidden_grad = upstream + back_two
    attn_grad = (branch_scale * hidden_grad).astype(jnp.bfloat16)
    mixed_heads = attended.reshape(count_of_tokens, -1)
    head_gradient = jnp.dot(attn_grad, w_output.T, preferred_element_type=jnp.float32).astype(jnp.bfloat16)
    output_w = jnp.einsum('tk,td->kd', mixed_heads.astype(jnp.float32), attn_grad.astype(jnp.float32))
    query_gradient, key_gradient, value_gradient = attention_backward(query_rows, key_matrix, value_matrix, permitted_mask, log_sum_exp, head_gradient.reshape(count_of_tokens, key_value_heads, QUERY_HEADS // KEY_VALUE_HEADS, HEAD_SIZE))
    query_gradient = rotate_back(query_gradient.reshape(count_of_tokens, -1, HEAD_SIZE), cosine, sine).reshape(count_of_tokens, -1).astype(jnp.bfloat16)
    key_gradient = rotate_back(key_gradient, cosine, sine).reshape(count_of_tokens, -1).astype(jnp.bfloat16)
    value_gradient = value_gradient.reshape(count_of_tokens, -1).astype(jnp.bfloat16)
    attn_wide = attn_in.astype(jnp.float32)
    query_w = jnp.einsum('td,tk->dk', attn_wide, query_gradient.astype(jnp.float32))
    key_w = jnp.einsum('td,tk->dk', attn_wide, key_gradient.astype(jnp.float32))
    value_w = jnp.einsum('td,tk->dk', attn_wide, value_gradient.astype(jnp.float32))
    input_part = jnp.dot(query_gradient, w_query.T, preferred_element_type=jnp.float32)
    input_part = input_part + jnp.dot(key_gradient, key_weight.T, preferred_element_type=jnp.float32)
    input_part = input_part + jnp.dot(value_gradient, value_weight.T, preferred_element_type=jnp.float32)
    back_one, gain_one = norm_back(input_part, normed_one, inverse_one, gain_attn)
    return (hidden_grad + back_one, (query_w, key_w, value_w, output_w, router_w, gain_one, gain_two, gate_w, up_w, down_w))

def forward_only(group_item, weights):
    layer_in, segment, route = group_item
    return layer_forward(layer_in, segment, route, weights)[0]

def reference(inputs, segment_ids, routes, w_query, key_weight, value_weight, w_output, w_router, gain_attn, gain_moe, w_gate, w_up, w_down, out_grad):
    groups = MICRO * N_FSDP
    segments = segment_ids.reshape(groups, TOK_DEV)
    weight_sets = [tuple((matrix[layer_index] for matrix in (w_query, key_weight, value_weight, w_output, w_router, gain_attn, gain_moe, w_gate, w_up, w_down))) for layer_index in range(N_SECTION)]
    current = inputs.reshape(groups, TOK_DEV, MODEL_DIM)
    layer_inputs = []
    outputs_list = []
    for layer_index in range(N_SECTION):
        layer_inputs.append(current)
        route_set = routes[layer_index].reshape(groups, TOK_DEV, TOP)
        current = lax.map(partial(forward_only, weights=weight_sets[layer_index]), (current, segments, route_set))
        outputs_list.append(current)
    upstream = out_grad.reshape(groups, TOK_DEV, MODEL_DIM).astype(jnp.float32)
    grads_list = [None] * N_SECTION
    input_list = [None] * N_SECTION
    for layer_index in reversed(range(N_SECTION)):
        weights = weight_sets[layer_index]
        route_set = routes[layer_index].reshape(groups, TOK_DEV, TOP)
        totals = tuple((jnp.zeros(matrix.shape, jnp.float32) for matrix in weights))

        def group_step(running, group_item, weights=weights):
            layer_in, segment, route, grad_rows = group_item
            kept_state = layer_forward(layer_in, segment, route, weights)[1]
            grad_out, grads = layer_backward(grad_rows, kept_state, weights)
            return (jax.tree.map(jnp.add, running, grads), grad_out)
        totals, upstream = lax.scan(group_step, totals, (layer_inputs[layer_index], segments, route_set, upstream))
        grads_list[layer_index] = totals
        input_list[layer_index] = upstream
    layer_outputs = jnp.stack(outputs_list).reshape(N_SECTION, MICRO, TOKENS_MB, MODEL_DIM)
    input_grads = jnp.stack(input_list).reshape(N_SECTION, MICRO, TOKENS_MB, MODEL_DIM)
    stacked = [jnp.stack([grads_list[layer_index][which] for layer_index in range(N_SECTION)]) for which in range(10)]
    return (layer_outputs, input_grads, stacked[0], stacked[1], stacked[2], stacked[3], stacked[4], stacked[5], stacked[6], stacked[7], stacked[8], stacked[9])
```

```python
import functools

import jax
import jax.numpy as jnp
from jax import lax
from jax.experimental import pallas as pl
from jax.experimental.pallas import tpu as pltpu
from jax.sharding import PartitionSpec as P

QUERY_HEADS = 16
KEY_VALUE_HEADS = 8
HEAD_SIZE = 64


norm_eps = 1e-06
branch_scale = 0.22
score_scale = 0.015625
rope_base = 10000.0
masked_score = -1e30


def norm_rows(vectors, gain_vec):
    inverse = lax.rsqrt(jnp.mean(vectors * vectors, axis=-1, keepdims=True) + norm_eps)
    normed = vectors * inverse
    return (normed * gain_vec, normed, inverse)


def norm_back(upstream, normed, inverse, gain_vec):
    scaled_grad = upstream * gain_vec
    gain_grad = jnp.sum(upstream * normed, axis=0, keepdims=True)
    inner_mean = jnp.mean(scaled_grad * normed, axis=-1, keepdims=True)
    return (inverse * (scaled_grad - normed * inner_mean), gain_grad)


def rope_tables(permitted_mask):
    offsets = (jnp.sum(permitted_mask.astype(jnp.int32), axis=1) - 1).astype(jnp.float32)
    half_dim = HEAD_SIZE // 2
    frequency = rope_base ** (-(jnp.arange(half_dim, dtype=jnp.float32) * 2.0 / HEAD_SIZE))
    angles = offsets[:, None] * frequency[None, :]
    return (jnp.cos(angles)[:, None, :], jnp.sin(angles)[:, None, :])


def rotate(vectors, cosine, sine):
    half_dim = vectors.shape[-1] // 2
    front_half = vectors[..., :half_dim]
    back_half = vectors[..., half_dim:]
    return jnp.concatenate(
        [front_half * cosine - back_half * sine, back_half * cosine + front_half * sine], axis=-1
    )


def rotate_back(vectors, cosine, sine):
    half_dim = vectors.shape[-1] // 2
    front_half = vectors[..., :half_dim]
    back_half = vectors[..., half_dim:]
    return jnp.concatenate(
        [front_half * cosine + back_half * sine, back_half * cosine - front_half * sine], axis=-1
    )


def allowed_pairs(segment):
    position = jnp.arange(segment.shape[0], dtype=jnp.int32)
    return (segment[:, None] == segment[None, :]) & (position[None, :] <= position[:, None])


def attend(query_rows, key_matrix, value_matrix, permitted_mask):
    scores = (
        jnp.einsum("qhgd,khd->hgqk", query_rows, key_matrix, preferred_element_type=jnp.float32)
        * score_scale
    )
    scores = jnp.where(permitted_mask[None, None], scores, masked_score)
    row_max = jnp.max(scores, axis=-1, keepdims=True)
    log_sum_exp = row_max + jnp.log(jnp.sum(jnp.exp(scores - row_max), axis=-1, keepdims=True))
    weights_low = jnp.exp(scores - log_sum_exp).astype(jnp.bfloat16)
    attended = jnp.einsum(
        "hgqk,khd->qhgd", weights_low, value_matrix, preferred_element_type=jnp.float32
    )
    return (attended.astype(jnp.bfloat16), log_sum_exp)


def attention_backward(
    query_rows, key_matrix, value_matrix, permitted_mask, log_sum_exp, head_gradient
):
    scores = (
        jnp.einsum("qhgd,khd->hgqk", query_rows, key_matrix, preferred_element_type=jnp.float32)
        * score_scale
    )
    scores = jnp.where(permitted_mask[None, None], scores, masked_score)
    weights_full = jnp.exp(scores - log_sum_exp)
    weights_low = weights_full.astype(jnp.bfloat16)
    value_gradient = jnp.einsum(
        "hgqk,qhgd->khd", weights_low, head_gradient, preferred_element_type=jnp.float32
    )
    weight_grad = jnp.einsum(
        "qhgd,khd->hgqk", head_gradient, value_matrix, preferred_element_type=jnp.float32
    )
    inner_sum = jnp.sum(weights_full * weight_grad, axis=-1, keepdims=True)
    score_grad = (weights_full * (weight_grad - inner_sum) * score_scale).astype(jnp.bfloat16)
    query_gradient = jnp.einsum(
        "hgqk,khd->qhgd", score_grad, key_matrix, preferred_element_type=jnp.float32
    )
    key_gradient = jnp.einsum(
        "hgqk,qhgd->khd", score_grad, query_rows, preferred_element_type=jnp.float32
    )
    return (query_gradient, key_gradient, value_gradient)


MESH = pl.DeviceIdType.MESH
LANES = 128
VMEM_LIMIT = 60 * 1024 * 1024
WHOLE_VMEM = pl.BlockSpec(memory_space=pltpu.VMEM)


def flipped(index, bit):
    step = 1 << bit
    return index + step - 2 * step * lax.rem(lax.div(index, step), 2)


def crossed(index, mask, bits):
    for bit in range(bits):
        if (mask >> bit) & 1:
            index = flipped(index, bit)
    return index


class Team:
    def __init__(self, sizes):
        self.sections, self.fsdp, self.tp = sizes
        self.bits = self.tp.bit_length() - 1
        assert 1 << self.bits == self.tp
        self.s = lax.axis_index("section")
        self.f = lax.axis_index("fsdp")
        self.t = lax.axis_index("tp")
        self.hops = [
            (bit, mask)
            for bit in reversed(range(self.bits))
            for mask in range(0, self.tp, 2 << bit)
        ]
        self.place = {hop: number for number, hop in enumerate(self.hops)}

    def row(self, i):
        return lax.rem(self.f + self.fsdp - i, self.fsdp)

    def column(self, mask):
        return crossed(self.t, mask, self.bits)


def greet(team, fsdp, section_step):
    barrier = pltpu.get_barrier_semaphore()
    count = 0
    if fsdp:
        for i in range(1, team.fsdp):
            pl.semaphore_signal(
                barrier, inc=1, device_id={"fsdp": team.row(i)}, device_id_type=MESH
            )
            count += 1
    for bit in range(team.bits):
        pl.semaphore_signal(
            barrier, inc=1, device_id={"tp": flipped(team.t, bit)}, device_id_type=MESH
        )
        count += 1
    if section_step:
        behind = lax.rem(team.s + team.sections - section_step, team.sections)
        pl.semaphore_signal(
            barrier, inc=1, device_id={"section": behind}, device_id_type=MESH
        )
        count += 1
    pl.semaphore_wait(barrier, count)


def rows_of(block, size):
    return pl.ds(pl.multiple_of(block * size, size), size)


class TpGather:
    def __init__(self, team, ref, size, sends, recvs):
        self.team, self.ref, self.size, self.sends, self.recvs = team, ref, size, sends, recvs

    def copy(self, hop, arriving):
        bit, mask = hop
        team = self.team
        block = team.column(mask | ((1 << bit) if arriving else 0))
        part = self.ref.at[rows_of(block, self.size)]
        return pltpu.make_async_remote_copy(
            src_ref=part,
            dst_ref=part,
            send_sem=self.sends(team.place[hop]),
            recv_sem=self.recvs(team.place[hop]),
            device_id={"tp": flipped(team.t, bit)},
            device_id_type=MESH,
        )

    def begin(self):
        for bit in reversed(range(self.team.bits)):
            self.copy((bit, 0), False).start()

    def relay(self):
        for hop in self.team.hops:
            bit, mask = hop
            if bit:
                self.copy(hop, True).wait_recv()
                for lower in reversed(range(bit)):
                    self.copy((lower, mask | (1 << bit)), False).start()

    def arrive(self):
        for hop in self.team.hops:
            if hop[0] == 0:
                self.copy(hop, True).wait_recv()

    def drain(self):
        for hop in self.team.hops:
            self.copy(hop, False).wait_send()


def add_blocks(target, rows, other, width, experts):
    wide = target[rows, :width].astype(jnp.float32) + other[:, :width].astype(jnp.float32)
    target[rows, :width] = wide.astype(target.dtype)
    if target.shape[1] > width:
        both = target[rows, width:].astype(jnp.float32) + other[:, width:].astype(jnp.float32)
        target[rows, width:] = two_parts(both, experts)


def two_parts(both, experts):
    lane = lax.broadcasted_iota(jnp.int32, both.shape, 1)
    first = lane < experts
    full = both + jnp.where(
        first, pltpu.roll(both, LANES - experts, 1), pltpu.roll(both, experts, 1)
    )
    return parted(full, first, lane < 2 * experts)


def parted(full, first, second):
    high = full.astype(jnp.bfloat16)
    low = (full - high.astype(jnp.float32)).astype(jnp.bfloat16)
    zero = jnp.zeros_like(high)
    return jnp.where(first, high, jnp.where(second, low, zero))


class TpScatter:
    def __init__(self, team, ref, size, landing, sends, recvs, width, experts):
        self.team, self.ref, self.size, self.landing = team, ref, size, landing
        self.sends, self.recvs, self.width, self.experts = sends, recvs, width, experts

    def copy(self, hop):
        bit, mask = hop
        team = self.team
        block = team.column(mask | (1 << bit))
        return pltpu.make_async_remote_copy(
            src_ref=self.ref.at[rows_of(block, self.size)],
            dst_ref=self.landing(team.place[hop]),
            send_sem=self.sends(team.place[hop]),
            recv_sem=self.recvs(team.place[hop]),
            device_id={"tp": flipped(team.t, bit)},
            device_id_type=MESH,
        )

    def send(self, bit):
        for hop in self.team.hops:
            if hop[0] == bit:
                self.copy(hop).start()

    def add(self, bit):
        for hop in self.team.hops:
            if hop[0] == bit:
                self.copy(hop).wait_recv()
                add_blocks(
                    self.ref,
                    rows_of(self.team.column(hop[1]), self.size),
                    self.landing(self.team.place[hop]),
                    self.width,
                    self.experts,
                )

    def drain(self):
        for hop in self.team.hops:
            self.copy(hop).wait_send()

    def run(self):
        for bit in range(self.team.bits):
            self.send(bit)
            self.add(bit)


def ring_copy(team, step, source, target, sends, recvs):
    ahead = lax.rem(team.s + team.sections + step, team.sections)
    return pltpu.make_async_remote_copy(
        src_ref=source,
        dst_ref=target,
        send_sem=sends.at[0],
        recv_sem=recvs.at[0],
        device_id={"section": ahead},
        device_id_type=MESH,
    )


def group_exchange(team, gathered, partial, landing, across, sems, size, width, experts, first, second):
    ag_send, ag_recv, agz_send, agz_recv, rs_send, rs_recv, rsz_send, rsz_recv = sems
    count = team.fsdp

    def gather(i):
        return TpGather(
            team,
            gathered.at[team.row(i)],
            size,
            lambda place: ag_send.at[i, place],
            lambda place: ag_recv.at[i, place],
        )

    def scatter(i):
        return TpScatter(
            team,
            partial.at[team.row(i)],
            size,
            lambda place: landing.at[i, place],
            lambda place: rs_send.at[i, place],
            lambda place: rs_recv.at[i, place],
            width,
            experts,
        )

    def own_rows():
        return rows_of(team.t, size)

    def gather_across(i, arriving):
        row = team.row(i) if arriving else team.f
        part = gathered.at[row, own_rows()]
        return pltpu.make_async_remote_copy(
            src_ref=part,
            dst_ref=part,
            send_sem=agz_send.at[i],
            recv_sem=agz_recv.at[i],
            device_id={"fsdp": lax.rem(team.f + i, count)},
            device_id_type=MESH,
        )

    def scatter_across(i):
        return pltpu.make_async_remote_copy(
            src_ref=partial.at[team.row(i), own_rows()],
            dst_ref=across.at[i],
            send_sem=rsz_send.at[i],
            recv_sem=rsz_recv.at[i],
            device_id={"fsdp": team.row(i)},
            device_id_type=MESH,
        )

    gather(0).begin()
    for i in range(1, count):
        gather_across(i, False).start()
    gather(0).relay()

    def step(i, carry):
        @pl.when(i + 1 < count)
        def _():
            gather_across(i + 1, True).wait_recv()
            gather(i + 1).begin()

        @pl.when(i < count)
        def _():
            gather(i).arrive()
            first(team.row(i))

        for bit in range(team.bits):
            done = i - 1 - bit

            @pl.when((done >= 0) & (done < count))
            def _():
                scatter(done).add(bit)
                if bit + 1 < team.bits:
                    scatter(done).send(bit + 1)
                else:

                    @pl.when(done > 0)
                    def _():
                        scatter_across(done).start()

        @pl.when(i + 1 < count)
        def _():
            gather(i + 1).relay()

        @pl.when(i < count)
        def _():
            second(team.row(i))
            scatter(i).send(0)

        return carry

    lax.fori_loop(0, count + team.bits, step, 0)

    def finish(i, carry):
        gather_across(i, False).wait_send()
        scatter_across(i).wait_send()
        return carry

    def settle(i, carry):
        gather(i).drain()
        scatter(i).drain()
        return carry

    lax.fori_loop(1, count, finish, 0)
    lax.fori_loop(0, count, settle, 0)

    def take(i, total):
        scatter_across(i).wait_recv()
        return total + across[i, :, :width].astype(jnp.float32)

    total = partial[team.f, own_rows(), :width].astype(jnp.float32)
    for i in range(1, count):
        total = take(i, total)
    extra = None
    if partial.shape[2] > width:
        extra = partial[team.f, own_rows(), width:].astype(jnp.float32)
        for i in range(1, count):
            extra = extra + across[i, :, width:].astype(jnp.float32)
    return total, extra


def group_sems(team_sizes):
    _, fsdp, tp = team_sizes
    dma = pltpu.SemaphoreType.DMA
    return [
        dma((fsdp, tp)), dma((fsdp, tp)), dma((fsdp,)), dma((fsdp,)),
        dma((fsdp, tp)), dma((fsdp, tp)), dma((fsdp,)), dma((fsdp,)),
    ]


def share_parts(share, experts):
    lane = lax.broadcasted_iota(jnp.int32, share.shape, 1)
    high = share.astype(jnp.bfloat16)
    rest = share - high.astype(jnp.float32)
    middle = rest.astype(jnp.bfloat16)
    low = (rest - middle.astype(jnp.float32)).astype(jnp.bfloat16)
    zero = jnp.zeros_like(high)
    return jnp.where(
        lane < experts,
        high,
        jnp.where(lane < 2 * experts, middle, jnp.where(lane < 3 * experts, low, zero)),
    )


def chunks(length, body, size=256):
    size = min(size, length)

    def step(c, carry):
        body(pl.multiple_of(c * size, size), size)
        return carry

    lax.fori_loop(0, length // size, step, 0)


def product(left, right):
    return jnp.dot(left, right, preferred_element_type=jnp.float32)


def product_turned(left, right):
    return lax.dot_general(
        left, right, (((1,), (1,)), ((), ())), preferred_element_type=jnp.float32
    )


def comm_params(number):
    return pltpu.CompilerParams(
        collective_id=number, has_side_effects=True, vmem_limit_bytes=VMEM_LIMIT
    )


def begin_layer(sizes, layer_in, gain, number):
    rows, width = layer_in.shape
    tp = sizes[2]

    def kernel(in_ref, gain_ref, out_ref, sends, recvs):
        team = Team(sizes)
        greet(team, False, 0)
        scaled, _, _ = norm_rows(in_ref[...].astype(jnp.float32), gain_ref[...])
        out_ref[rows_of(team.t, rows)] = scaled.astype(jnp.bfloat16)
        gather = TpGather(team, out_ref, rows, lambda p: sends.at[p], lambda p: recvs.at[p])
        gather.begin()
        gather.relay()
        gather.arrive()
        gather.drain()

    return pl.pallas_call(
        kernel,
        out_shape=jax.ShapeDtypeStruct((tp * rows, width), jnp.bfloat16),
        in_specs=[WHOLE_VMEM] * 2,
        out_specs=WHOLE_VMEM,
        scratch_shapes=[pltpu.SemaphoreType.DMA((tp,)), pltpu.SemaphoreType.DMA((tp,))],
        compiler_params=comm_params(number),
    )(layer_in, gain)


def moe_forward(sizes, partial_out, residual, chosen, weights, fresh, experts, number):
    router, gain_one, gain_two, gate_up, down, spread_map = weights
    sections, fsdp, tp = sizes
    rows, width = residual.shape
    band = tp * rows
    hidden = down.shape[0]
    copies = LANES // experts
    tail = fresh is not None
    bf16, f32 = jnp.bfloat16, jnp.float32
    shapes = [
        jax.ShapeDtypeStruct((fsdp, band, width), bf16),
        jax.ShapeDtypeStruct((fsdp, band, 2 * hidden), bf16),
        jax.ShapeDtypeStruct((fsdp, band, LANES), f32),
        jax.ShapeDtypeStruct((rows, width), f32),
        jax.ShapeDtypeStruct((rows, width), bf16),
    ]
    if tail:
        shapes += [
            jax.ShapeDtypeStruct((rows, width), bf16),
            jax.ShapeDtypeStruct((band, width), bf16),
        ]
    dma = pltpu.SemaphoreType.DMA
    scratch = [
        pltpu.VMEM((band, width), bf16),
        pltpu.VMEM((tp, rows, width), bf16),
        pltpu.VMEM((fsdp, band, width), bf16),
        pltpu.VMEM((fsdp, tp, rows, width), bf16),
        pltpu.VMEM((fsdp, rows, width), bf16),
        pltpu.VMEM((band, hidden), bf16),
        pltpu.VMEM((band, LANES), bf16),
        pltpu.VMEM((rows, width), bf16),
        dma((tp,)), dma((tp,)), dma((tp,)), dma((tp,)), dma((1,)), dma((1,)),
    ] + group_sems(sizes)

    def kernel(*refs):
        part_ref, res_ref, chosen_ref, router_ref, one_ref, two_ref, both_ref, down_ref, map_ref = refs[:9]
        refs = refs[9:]
        if tail:
            fresh_ref, refs = refs[0], refs[1:]
        all_ref, pre_ref, share_ref, state_ref, result_ref = refs[:5]
        refs = refs[5:]
        if tail:
            next_ref, attn_ref = refs[:2]
            refs = refs[2:]
        sums, sums_in, partial, landing, across, weighted, parts, moved = refs[:8]
        tr_send, tr_recv, tg_send, tg_recv, sec_send, sec_recv = refs[8:14]
        sems = refs[14:]
        team = Team(sizes)
        sums[...] = part_ref[...]
        greet(team, True, 1 if tail else 0)
        reduce = TpScatter(
            team, sums, rows, lambda p: sums_in.at[p], lambda p: tr_send.at[p],
            lambda p: tr_recv.at[p], width, experts,
        )
        reduce.run()
        state = res_ref[...].astype(f32) + branch_scale * sums[rows_of(team.t, rows)].astype(f32)
        state_ref[...] = state
        scaled, _, _ = norm_rows(state, two_ref[...])
        all_ref[team.f, rows_of(team.t, rows)] = scaled.astype(bf16)

        def first(row):
            logits = product(all_ref[row], router_ref[...])
            logits = jnp.where(chosen_ref[row].astype(f32) > 0.5, logits, masked_score)
            grown = jnp.exp(logits - jnp.max(logits, axis=-1, keepdims=True))
            total = jnp.sum(grown, axis=-1, keepdims=True) * (1.0 / copies)
            share = grown / total
            share_ref[row] = share
            parts[...] = share_parts(share, experts)

            def piece(start, size):
                here, there = pl.ds(start, size), pl.ds(pl.multiple_of(hidden + start, size), size)
                gate = product(all_ref[row], both_ref[:, here])
                up = product(all_ref[row], both_ref[:, there])
                pre_ref[row, :, here] = gate.astype(bf16)
                pre_ref[row, :, there] = up.astype(bf16)
                wide = product(parts[...], map_ref[:, here])
                weighted[:, here] = (wide * (gate * jax.nn.sigmoid(gate) * up)).astype(bf16)

            chunks(hidden, piece)

        def second(row):
            def piece(start, size):
                here = pl.ds(start, size)
                partial[row, :, here] = product(weighted[...], down_ref[:, here]).astype(bf16)

            chunks(width, piece)

        total, _ = group_exchange(
            team, all_ref, partial, landing, across, sems, rows, width, experts, first, second
        )
        result_ref[...] = (state_ref[...] + branch_scale * total).astype(bf16)
        reduce.drain()
        if tail:
            move = ring_copy(team, 1, result_ref, moved, sec_send, sec_recv)
            move.start()
            move.wait_recv()
            layer_in = jnp.where(team.s == 0, fresh_ref[...], moved[...])
            next_ref[...] = layer_in
            scaled, _, _ = norm_rows(layer_in.astype(f32), one_ref[...])
            attn_ref[rows_of(team.t, rows)] = scaled.astype(bf16)
            gather = TpGather(
                team, attn_ref, rows, lambda p: tg_send.at[p], lambda p: tg_recv.at[p]
            )
            gather.begin()
            gather.relay()
            gather.arrive()
            gather.drain()
            move.wait_send()

    args = [partial_out, residual, chosen, router, gain_one, gain_two, gate_up, down, spread_map]
    if tail:
        args.append(fresh)
    return pl.pallas_call(
        kernel,
        out_shape=shapes,
        in_specs=[WHOLE_VMEM] * len(args),
        out_specs=[WHOLE_VMEM] * len(shapes),
        scratch_shapes=scratch,
        compiler_params=comm_params(number),
        name="moe_forward",
    )(*args)


def moe_backward(sizes, upstream, state, share, pre, weights, experts, number):
    router, gain_two, gate_up, down, spread_map, pick_map = weights
    sections, fsdp, tp = sizes
    rows, width = upstream.shape
    band = tp * rows
    hidden = down.shape[0]
    bf16, f32 = jnp.bfloat16, jnp.float32
    shapes = [
        jax.ShapeDtypeStruct((fsdp, band, width), bf16),
        jax.ShapeDtypeStruct((fsdp, band, 2 * hidden), bf16),
        jax.ShapeDtypeStruct((fsdp, band, hidden), bf16),
        jax.ShapeDtypeStruct((rows, LANES), bf16),
        jax.ShapeDtypeStruct((1, width), f32),
        jax.ShapeDtypeStruct((rows, width), f32),
        jax.ShapeDtypeStruct((band, width), bf16),
    ]
    dma = pltpu.SemaphoreType.DMA
    wider = width + LANES
    scratch = [
        pltpu.VMEM((fsdp, band, wider), bf16),
        pltpu.VMEM((fsdp, tp, rows, wider), bf16),
        pltpu.VMEM((fsdp, rows, wider), bf16),
        pltpu.VMEM((band, LANES), bf16),
        pltpu.VMEM((band, LANES), f32),
        dma((tp,)), dma((tp,)),
    ] + group_sems(sizes)

    def kernel(
        up_ref, state_ref, share_ref, pre_ref, router_ref, gain_ref, both_ref, down_ref, map_ref, pick_ref,
        all_ref, grad_ref, weighted_ref, logit_ref, gain_out, state_out, attn_ref,
        partial, landing, across, parts, share_sum, tg_send, tg_recv, *sems,
    ):
        team = Team(sizes)
        greet(team, True, 0)
        all_ref[team.f, rows_of(team.t, rows)] = (branch_scale * up_ref[...]).astype(bf16)

        def first(row):
            parts[...] = share_parts(share_ref[row], experts)
            share_sum[...] = jnp.zeros_like(share_sum)

            def piece(start, size):
                here, there = pl.ds(start, size), pl.ds(pl.multiple_of(hidden + start, size), size)
                hidden_grad = product_turned(all_ref[row], down_ref[here])
                gate = pre_ref[row, :, here].astype(f32)
                up = pre_ref[row, :, there].astype(f32)
                wide = product(parts[...], map_ref[:, here])
                sigmoid_gate = jax.nn.sigmoid(gate)
                swish = gate * sigmoid_gate
                value = swish * up
                weighted_ref[row, :, here] = (wide * value).astype(bf16)
                both = hidden_grad * value
                high = both.astype(bf16)
                low = (both - high.astype(f32)).astype(bf16)
                share_sum[...] += product(high, pick_ref[here]) + product(low, pick_ref[here])
                scaled = wide * hidden_grad
                grad_ref[row, :, here] = (
                    scaled * up * sigmoid_gate * (1.0 + gate * (1.0 - sigmoid_gate))
                ).astype(bf16)
                grad_ref[row, :, there] = (scaled * swish).astype(bf16)

            chunks(hidden, piece)

        def second(row):
            def piece(start, size):
                here = pl.ds(start, size)
                partial[row, :, here] = product_turned(grad_ref[row], both_ref[here]).astype(bf16)

            chunks(width, piece)
            lane = lax.broadcasted_iota(jnp.int32, (band, LANES), 1)
            partial[row, :, width:] = parted(share_sum[...], lane < experts, lane < 2 * experts)

        total, extra = group_exchange(
            team, all_ref, partial, landing, across, sems, rows, width, experts, first, second
        )
        lane = lax.broadcasted_iota(jnp.int32, (rows, LANES), 1)
        valid = lane < experts
        share_grad = extra + pltpu.roll(extra, LANES - experts, 1)
        own_share = jnp.where(valid, share_ref[team.f, rows_of(team.t, rows)], 0.0)
        inner = jnp.sum(own_share * share_grad, axis=-1, keepdims=True)
        logit_grad = (own_share * (share_grad - inner)).astype(bf16)
        logit_ref[...] = logit_grad
        norm_grad = total + product_turned(logit_grad, router_ref[...])
        _, normed, inverse = norm_rows(state_ref[...], gain_ref[...])
        back, gain_grad = norm_back(norm_grad, normed, inverse, gain_ref[...])
        gain_out[...] = gain_grad
        state_grad = up_ref[...] + back
        state_out[...] = state_grad
        attn_ref[rows_of(team.t, rows)] = (branch_scale * state_grad).astype(bf16)
        gather = TpGather(team, attn_ref, rows, lambda p: tg_send.at[p], lambda p: tg_recv.at[p])
        gather.begin()
        gather.relay()
        gather.arrive()
        gather.drain()

    args = [upstream, state, share, pre, router, gain_two, gate_up, down, spread_map, pick_map]
    return pl.pallas_call(
        kernel,
        out_shape=shapes,
        in_specs=[WHOLE_VMEM] * len(args),
        out_specs=[WHOLE_VMEM] * len(shapes),
        scratch_shapes=scratch,
        compiler_params=comm_params(number),
        name="moe_backward",
    )(*args)


def end_layer(sizes, partial_in, layer_in, state_grad, gain, number):
    tp = sizes[2]
    rows, width = layer_in.shape
    bf16, f32 = jnp.bfloat16, jnp.float32
    dma = pltpu.SemaphoreType.DMA

    def kernel(
        part_ref, in_ref, grad_ref, gain_ref, out_ref, gain_out, arrived_ref,
        sums, sums_in, leaving, tr_send, tr_recv, sec_send, sec_recv,
    ):
        team = Team(sizes)
        sums[...] = part_ref[...]
        greet(team, False, -1)
        reduce = TpScatter(
            team, sums, rows, lambda p: sums_in.at[p], lambda p: tr_send.at[p],
            lambda p: tr_recv.at[p], width, 0,
        )
        reduce.run()
        norm_grad = sums[rows_of(team.t, rows)].astype(f32)
        _, normed, inverse = norm_rows(in_ref[...].astype(f32), gain_ref[...])
        back, gain_grad = norm_back(norm_grad, normed, inverse, gain_ref[...])
        gain_out[...] = gain_grad
        result = grad_ref[...] + back
        out_ref[...] = result
        leaving[...] = result.astype(bf16)
        move = ring_copy(team, -1, leaving, arrived_ref, sec_send, sec_recv)
        move.start()
        reduce.drain()
        move.wait()

    return pl.pallas_call(
        kernel,
        out_shape=[
            jax.ShapeDtypeStruct((rows, width), f32),
            jax.ShapeDtypeStruct((1, width), f32),
            jax.ShapeDtypeStruct((rows, width), bf16),
        ],
        in_specs=[WHOLE_VMEM] * 4,
        out_specs=[WHOLE_VMEM] * 3,
        scratch_shapes=[
            pltpu.VMEM((tp * rows, width), bf16),
            pltpu.VMEM((tp, rows, width), bf16),
            pltpu.VMEM((rows, width), bf16),
            dma((tp,)), dma((tp,)), dma((1,)), dma((1,)),
        ],
        compiler_params=comm_params(number),
        name="end_layer",
    )(partial_in, layer_in, state_grad, gain)


def order_map(inputs, outputs, count, part, turned):
    across = count * part
    source = lax.broadcasted_iota(jnp.int32, (inputs, outputs), 1 if turned else 0)
    target = lax.broadcasted_iota(jnp.int32, (inputs, outputs), 0 if turned else 1)
    e, rest = lax.div(source, across), lax.rem(source, across)
    f, h = lax.div(rest, part), lax.rem(rest, part)
    return (f * LANES + e * part + h == target).astype(jnp.bfloat16)


def outgoing_experts(w_gate, w_up, count):
    experts, depth, hidden = w_gate.shape
    part = hidden // count
    bunch = LANES // part
    across = bunch * hidden
    blocks = experts // bunch

    def kernel(gate_ref, up_ref, out_ref, table):
        @pl.when((pl.program_id(0) == 0) & (pl.program_id(1) == 0))
        def _():
            table[...] = order_map(across, count * LANES, count, part, False)

        def move(ref):
            lanes = jnp.concatenate([ref[e] for e in range(bunch)], axis=1)
            moved = product(lanes, table[...]).astype(jnp.bfloat16)
            for f in range(count):
                out_ref[f] = moved[:, f * LANES : (f + 1) * LANES]

        @pl.when(pl.program_id(0) == 0)
        def _():
            move(gate_ref)

        @pl.when(pl.program_id(0) == 1)
        def _():
            move(up_ref)

    return pl.pallas_call(
        kernel,
        grid=(2, blocks),
        out_shape=jax.ShapeDtypeStruct((count, depth, 2 * blocks * LANES), jnp.bfloat16),
        in_specs=[
            pl.BlockSpec((bunch, depth, hidden), lambda w, b: (jnp.where(w == 0, b, blocks - 1), 0, 0)),
            pl.BlockSpec((bunch, depth, hidden), lambda w, b: (jnp.where(w == 1, b, 0), 0, 0)),
        ],
        out_specs=pl.BlockSpec((count, depth, LANES), lambda w, b: (0, 0, w * blocks + b)),
        scratch_shapes=[pltpu.VMEM((across, count * LANES), jnp.bfloat16)],
        compiler_params=pltpu.CompilerParams(vmem_limit_bytes=VMEM_LIMIT),
        name="outgoing_experts",
    )(w_gate, w_up)


def incoming_experts(both, experts, hidden):
    count, depth, width = both.shape
    part = hidden // count
    bunch = LANES // part
    across = bunch * hidden
    blocks = experts // bunch

    def kernel(in_ref, gate_ref, up_ref, table):
        @pl.when((pl.program_id(0) == 0) & (pl.program_id(1) == 0))
        def _():
            table[...] = order_map(count * LANES, across, count, part, True)

        lanes = jnp.concatenate([in_ref[f] for f in range(count)], axis=1)
        moved = product(lanes, table[...])

        def store(ref):
            for e in range(bunch):
                ref[e] = moved[:, e * hidden : (e + 1) * hidden]

        @pl.when(pl.program_id(0) == 0)
        def _():
            store(gate_ref)

        @pl.when(pl.program_id(0) == 1)
        def _():
            store(up_ref)

    shape = jax.ShapeDtypeStruct((experts, depth, hidden), jnp.float32)
    return pl.pallas_call(
        kernel,
        grid=(2, blocks),
        out_shape=[shape, shape],
        in_specs=[pl.BlockSpec((count, depth, LANES), lambda w, b: (0, 0, w * blocks + b))],
        out_specs=[
            pl.BlockSpec((bunch, depth, hidden), lambda w, b: (jnp.where(w == 0, b, blocks - 1), 0, 0)),
            pl.BlockSpec((bunch, depth, hidden), lambda w, b: (jnp.where(w == 1, b, 0), 0, 0)),
        ],
        scratch_shapes=[pltpu.VMEM((count * LANES, across), jnp.bfloat16)],
        compiler_params=pltpu.CompilerParams(vmem_limit_bytes=VMEM_LIMIT),
        name="incoming_experts",
    )(both)


def exchange(blocks):
    return lax.all_to_all(blocks, "fsdp", split_axis=0, concat_axis=0, tiled=True)


def attention_forward(attn_in, segment, w_qkv, w_output):
    query_width = w_output.shape[0]
    key_width = (w_qkv.shape[1] - query_width) // 2
    key_value_heads = key_width // HEAD_SIZE
    count_of_tokens = attn_in.shape[0]
    permitted_mask = allowed_pairs(segment)
    cosine, sine = rope_tables(permitted_mask)
    qkv = jnp.dot(attn_in, w_qkv, preferred_element_type=jnp.float32)
    turned = rotate(
        qkv[:, : query_width + key_width].reshape(count_of_tokens, -1, HEAD_SIZE), cosine, sine
    ).astype(jnp.bfloat16)
    query_rows = turned[:, : query_width // HEAD_SIZE].reshape(
        count_of_tokens, key_value_heads, QUERY_HEADS // KEY_VALUE_HEADS, HEAD_SIZE
    )
    key_matrix = turned[:, query_width // HEAD_SIZE :]
    value_matrix = (
        qkv[:, query_width + key_width :]
        .astype(jnp.bfloat16)
        .reshape(count_of_tokens, key_value_heads, HEAD_SIZE)
    )
    attended, log_sum_exp = attend(query_rows, key_matrix, value_matrix, permitted_mask)
    mixed_heads = attended.reshape(count_of_tokens, -1)
    partial = jnp.dot(mixed_heads, w_output, preferred_element_type=jnp.float32)
    kept = (
        query_rows, key_matrix, value_matrix, attended, log_sum_exp, cosine, sine, permitted_mask
    )
    return (partial.astype(jnp.bfloat16), kept)


def attention_gradients(attn_grad, kept, w_qkv, w_output):
    (
        query_rows, key_matrix, value_matrix, attended, log_sum_exp, cosine, sine, permitted_mask
    ) = kept
    count_of_tokens = attn_grad.shape[0]
    key_value_heads = key_matrix.shape[1]
    mixed_heads = attended.reshape(count_of_tokens, -1)
    head_gradient = jnp.dot(attn_grad, w_output.T, preferred_element_type=jnp.float32).astype(
        jnp.bfloat16
    )
    query_gradient, key_gradient, value_gradient = attention_backward(
        query_rows,
        key_matrix,
        value_matrix,
        permitted_mask,
        log_sum_exp,
        head_gradient.reshape(
            count_of_tokens, key_value_heads, QUERY_HEADS // KEY_VALUE_HEADS, HEAD_SIZE
        ),
    )
    turned = jnp.concatenate(
        [query_gradient.reshape(count_of_tokens, -1, HEAD_SIZE), key_gradient], axis=1
    )
    turned = rotate_back(turned, cosine, sine).reshape(count_of_tokens, -1)
    qkv_grad = jnp.concatenate(
        [turned, value_gradient.reshape(count_of_tokens, -1)], axis=1
    ).astype(jnp.bfloat16)
    input_part = lax.dot_general(
        qkv_grad, w_qkv, (((1,), (1,)), ((), ())), preferred_element_type=jnp.float32
    )
    return (input_part.astype(jnp.bfloat16), qkv_grad, mixed_heads)


def summed_product(pairs):
    left = jnp.concatenate([pair[0] for pair in pairs], axis=0)
    right = jnp.concatenate([pair[1] for pair in pairs], axis=0)
    return lax.dot_general(
        left, right, (((0,), (0,)), ((), ())), preferred_element_type=jnp.float32
    )


def per_device(
    sizes,
    inputs,
    segment_ids,
    routes,
    w_query,
    key_weight,
    value_weight,
    w_output,
    w_router,
    gain_attn,
    gain_moe,
    w_gate,
    w_up,
    w_down,
    out_grad,
):
    section_count, fsdp_count, tp_count = sizes
    section_index = lax.axis_index("section")
    micro_count, local_rows, model_width = inputs.shape
    depth = w_query.shape[1]
    expert_count = w_router.shape[2]
    hidden_units = w_gate.shape[3]
    own_units = hidden_units // fsdp_count
    hidden = expert_count * own_units
    copies = LANES // expert_count
    query_width = w_query.shape[2]
    key_width = key_weight.shape[2]
    qkv_width = query_width + 2 * key_width
    flat_output = w_output[0].reshape(depth, -1)
    output_width = flat_output.shape[1]
    packed = jnp.concatenate(
        [
            w_query[0],
            key_weight[0],
            value_weight[0],
            flat_output,
            w_router[0],
            gain_attn[0].astype(jnp.bfloat16)[:, None],
            gain_moe[0].astype(jnp.bfloat16)[:, None],
        ],
        axis=1,
    )
    packed = lax.all_gather(packed, "fsdp", axis=0, tiled=True)
    after = qkv_width + output_width
    w_qkv = packed[:, :qkv_width]
    out_full = packed[:, qkv_width:after].reshape(-1, model_width)
    router = jnp.tile(packed[:, after : after + expert_count], (1, copies))
    gain_one = packed[:, after + expert_count].astype(jnp.float32)[None]
    gain_two = packed[:, after + expert_count + 1].astype(jnp.float32)[None]
    both_out = outgoing_experts(w_gate[0], w_up[0], fsdp_count)
    gate_up = exchange(both_out).reshape(model_width, 2 * hidden)
    down = w_down[0].reshape(hidden, model_width)
    lane = jnp.arange(LANES, dtype=jnp.int32)
    owner = jnp.arange(hidden, dtype=jnp.int32) // own_units
    match = (lane % expert_count)[:, None] == owner[None, :]
    spread_map = (match & (lane < 3 * expert_count)[:, None]).astype(jnp.bfloat16)
    pick_map = (match & (lane < 2 * expert_count)[:, None]).astype(jnp.bfloat16).T
    expert_ids = jnp.arange(expert_count, dtype=jnp.int32)
    chosen_rows = jnp.any(routes[0][..., None] == expert_ids, axis=2).astype(jnp.bfloat16)
    chosen_rows = lax.all_gather(chosen_rows, "fsdp", axis=0)
    chosen_rows = jnp.tile(chosen_rows, (1, 1, 1, copies))
    segment_rows = segment_ids[:, 0, :]
    tick_count = micro_count + section_count - 1
    outputs = jnp.zeros((micro_count, local_rows, model_width), jnp.bfloat16)
    history = []
    layer_in = jnp.where(section_index == 0, inputs[0], jnp.zeros_like(inputs[0]))
    attn_in = begin_layer(sizes, layer_in, gain_one, 0)
    for tick_step in range(tick_count):
        mb_index = tick_step - section_index
        active = (mb_index >= 0) & (mb_index < micro_count)
        mb_pick = jnp.clip(mb_index, 0, micro_count - 1)
        segment = lax.dynamic_index_in_dim(segment_rows, mb_pick, 0, keepdims=False)
        chosen = lax.dynamic_index_in_dim(chosen_rows, mb_pick, 1, keepdims=False)
        partial, kept = attention_forward(attn_in, segment, w_qkv, out_full)
        last = tick_step == tick_count - 1
        fresh = None if last else inputs[min(tick_step + 1, micro_count - 1)]
        weights = (router, gain_one, gain_two, gate_up, down, spread_map)
        made = moe_forward(
            sizes, partial, layer_in, chosen, weights, fresh, expert_count, 2 if last else 1
        )
        moe_in, pre, share, state, result = made[:5]
        history.append((attn_in, layer_in, kept, moe_in, pre, share, state))
        outputs = jnp.where(
            active, lax.dynamic_update_index_in_dim(outputs, result, mb_pick, 0), outputs
        )
        if not last:
            layer_in, attn_in = made[5:]
    input_grads = jnp.zeros((micro_count, local_rows, model_width), jnp.float32)
    gain_sums = None
    all_terms = []
    arrived = None
    place = (lax.axis_index("fsdp"), lax.axis_index("tp") * local_rows, 0)
    for tick_step in range(tick_count):
        mb_index = micro_count + section_count - 2 - tick_step - section_index
        active = (mb_index >= 0) & (mb_index < micro_count)
        mb_pick = jnp.clip(mb_index, 0, micro_count - 1)
        upstream = out_grad[max(micro_count - 1 - tick_step, 0)].astype(jnp.float32)
        if arrived is None:
            arrived = jnp.zeros_like(upstream)
        upstream = jnp.where(
            section_index == section_count - 1, upstream, arrived.astype(jnp.float32)
        )
        upstream = jnp.where(active, upstream, jnp.zeros_like(upstream))
        attn_in, layer_in, kept, moe_in, pre, share, state = history[tick_count - 1 - tick_step]
        moe_grad, both_grad, weighted, logit_grad, gain_two_part, state_grad, attn_grad = moe_backward(
            sizes, upstream, state, share, pre,
            (router, gain_two, gate_up, down, spread_map, pick_map), expert_count, 3,
        )
        input_part, qkv_grad, mixed_heads = attention_gradients(attn_grad, kept, w_qkv, out_full)
        grad_out, gain_one_part, arrived = end_layer(
            sizes, input_part, layer_in, state_grad, gain_one, 4
        )
        input_grads = jnp.where(
            active, lax.dynamic_update_index_in_dim(input_grads, grad_out, mb_pick, 0), input_grads
        )
        gains = (gain_one_part, gain_two_part)
        gain_sums = gains if gain_sums is None else tuple(a + b for a, b in zip(gain_sums, gains))
        own_rows = lax.dynamic_slice(moe_in, place, (1, local_rows, model_width))[0]
        flat = lambda array: array.reshape(-1, array.shape[-1])
        all_terms.append(
            (
                active,
                (
                    (attn_in, qkv_grad),
                    (mixed_heads, attn_grad),
                    (logit_grad[:, :expert_count], own_rows),
                    (flat(moe_in), flat(both_grad)),
                    (flat(weighted), flat(moe_grad)),
                ),
            )
        )
    chosen_terms = []
    for first in range(micro_count):
        picked = all_terms[first][1]
        for active, terms in all_terms[first + micro_count :: micro_count]:
            picked = jax.tree.map(lambda a, b: jnp.where(active, b, a), picked, terms)
        chosen_terms.append(picked)
    qkv_pairs, output_pairs, router_pairs, both_pairs, down_pairs = zip(*chosen_terms)
    both_w = summed_product(both_pairs).astype(jnp.bfloat16)
    both_w = exchange(both_w.reshape(fsdp_count, depth, 2 * hidden))
    gate_shard, up_shard = incoming_experts(both_w, expert_count, hidden_units)
    down_shard = summed_product(down_pairs).reshape(expert_count, own_units, model_width)
    small = jnp.concatenate([summed_product(router_pairs)] + list(gain_sums), axis=0)
    small = lax.psum(small, "tp").T
    packed_grad = jnp.concatenate(
        [
            summed_product(qkv_pairs),
            summed_product(output_pairs).reshape(model_width, -1),
            small,
        ],
        axis=1,
    ).astype(jnp.bfloat16)
    packed_grad = lax.psum_scatter(
        packed_grad, "fsdp", scatter_dimension=0, tiled=True
    ).astype(jnp.float32)
    shard_sums = (
        packed_grad[:, :query_width],
        packed_grad[:, query_width : query_width + key_width],
        packed_grad[:, query_width + key_width : qkv_width],
        packed_grad[:, qkv_width:after].reshape(-1, model_width),
        packed_grad[:, after : after + expert_count],
        packed_grad[:, after + expert_count],
        packed_grad[:, after + expert_count + 1],
        gate_shard,
        up_shard,
        down_shard,
    )
    return (outputs[None], input_grads[None]) + tuple((part[None] for part in shard_sums))


def solution(mesh):
    in_specs = (
        P(None, ("fsdp", "tp"), None),
        P(None, "fsdp", None),
        P("section", None, "fsdp", None),
        P("section", "fsdp", "tp"),
        P("section", "fsdp", "tp"),
        P("section", "fsdp", "tp"),
        P("section", ("tp", "fsdp"), None),
        P("section", "fsdp", None),
        P("section", "fsdp"),
        P("section", "fsdp"),
        P("section", None, "fsdp", "tp"),
        P("section", None, "fsdp", "tp"),
        P("section", None, ("tp", "fsdp"), None),
        P(None, ("fsdp", "tp"), None),
    )
    out_specs = (
        P("section", None, ("fsdp", "tp"), None),
        P("section", None, ("fsdp", "tp"), None),
        P("section", "fsdp", "tp"),
        P("section", "fsdp", "tp"),
        P("section", "fsdp", "tp"),
        P("section", ("tp", "fsdp"), None),
        P("section", "fsdp", None),
        P("section", "fsdp"),
        P("section", "fsdp"),
        P("section", None, "fsdp", "tp"),
        P("section", None, "fsdp", "tp"),
        P("section", None, ("tp", "fsdp"), None),
    )
    sizes = tuple(mesh.shape[axis] for axis in ("section", "fsdp", "tp"))
    return jax.shard_map(
        functools.partial(per_device, sizes), mesh=mesh, in_specs=in_specs, out_specs=out_specs, check_vma=False
    )
```

```python
import functools

import jax
import jax.numpy as jnp
from jax import lax
from jax.experimental import pallas as pl
from jax.experimental.pallas import tpu as pltpu
from jax.sharding import PartitionSpec as P

QUERY_HEADS = 16
KEY_VALUE_HEADS = 8
HEAD_SIZE = 64


norm_eps = 1e-06
branch_scale = 0.22
score_scale = 0.015625
rope_base = 10000.0
masked_score = -1e30


def norm_rows(vectors, gain_vec):
    inverse = lax.rsqrt(jnp.mean(vectors * vectors, axis=-1, keepdims=True) + norm_eps)
    normed = vectors * inverse
    return (normed * gain_vec, normed, inverse)


def norm_back(upstream, normed, inverse, gain_vec):
    scaled_grad = upstream * gain_vec
    gain_grad = jnp.sum(upstream * normed, axis=0, keepdims=True)
    inner_mean = jnp.mean(scaled_grad * normed, axis=-1, keepdims=True)
    return (inverse * (scaled_grad - normed * inner_mean), gain_grad)


def rope_tables(permitted_mask):
    offsets = (jnp.sum(permitted_mask.astype(jnp.int32), axis=1) - 1).astype(jnp.float32)
    half_dim = HEAD_SIZE // 2
    frequency = rope_base ** (-(jnp.arange(half_dim, dtype=jnp.float32) * 2.0 / HEAD_SIZE))
    angles = offsets[:, None] * frequency[None, :]
    return (jnp.cos(angles)[:, None, :], jnp.sin(angles)[:, None, :])


def rotate(vectors, cosine, sine):
    half_dim = vectors.shape[-1] // 2
    front_half = vectors[..., :half_dim]
    back_half = vectors[..., half_dim:]
    return jnp.concatenate(
        [front_half * cosine - back_half * sine, back_half * cosine + front_half * sine], axis=-1
    )


def rotate_back(vectors, cosine, sine):
    half_dim = vectors.shape[-1] // 2
    front_half = vectors[..., :half_dim]
    back_half = vectors[..., half_dim:]
    return jnp.concatenate(
        [front_half * cosine + back_half * sine, back_half * cosine - front_half * sine], axis=-1
    )


def allowed_pairs(segment):
    position = jnp.arange(segment.shape[0], dtype=jnp.int32)
    return (segment[:, None] == segment[None, :]) & (position[None, :] <= position[:, None])


def attend(query_rows, key_matrix, value_matrix, permitted_mask):
    scores = (
        jnp.einsum("qhgd,khd->hgqk", query_rows, key_matrix, preferred_element_type=jnp.float32)
        * score_scale
    )
    scores = jnp.where(permitted_mask[None, None], scores, masked_score)
    row_max = jnp.max(scores, axis=-1, keepdims=True)
    log_sum_exp = row_max + jnp.log(jnp.sum(jnp.exp(scores - row_max), axis=-1, keepdims=True))
    weights_low = jnp.exp(scores - log_sum_exp).astype(jnp.bfloat16)
    attended = jnp.einsum(
        "hgqk,khd->qhgd", weights_low, value_matrix, preferred_element_type=jnp.float32
    )
    return (attended.astype(jnp.bfloat16), log_sum_exp)


def attention_backward(
    query_rows, key_matrix, value_matrix, permitted_mask, log_sum_exp, head_gradient
):
    scores = (
        jnp.einsum("qhgd,khd->hgqk", query_rows, key_matrix, preferred_element_type=jnp.float32)
        * score_scale
    )
    scores = jnp.where(permitted_mask[None, None], scores, masked_score)
    weights_full = jnp.exp(scores - log_sum_exp)
    weights_low = weights_full.astype(jnp.bfloat16)
    value_gradient = jnp.einsum(
        "hgqk,qhgd->khd", weights_low, head_gradient, preferred_element_type=jnp.float32
    )
    weight_grad = jnp.einsum(
        "qhgd,khd->hgqk", head_gradient, value_matrix, preferred_element_type=jnp.float32
    )
    inner_sum = jnp.sum(weights_full * weight_grad, axis=-1, keepdims=True)
    score_grad = (weights_full * (weight_grad - inner_sum) * score_scale).astype(jnp.bfloat16)
    query_gradient = jnp.einsum(
        "hgqk,khd->qhgd", score_grad, key_matrix, preferred_element_type=jnp.float32
    )
    key_gradient = jnp.einsum(
        "hgqk,qhgd->khd", score_grad, query_rows, preferred_element_type=jnp.float32
    )
    return (query_gradient, key_gradient, value_gradient)


MESH = pl.DeviceIdType.MESH
LANES = 128
VMEM_LIMIT = 60 * 1024 * 1024
WHOLE_VMEM = pl.BlockSpec(memory_space=pltpu.VMEM)


def flipped(index, bit):
    step = 1 << bit
    return index + step - 2 * step * lax.rem(lax.div(index, step), 2)


def crossed(index, mask, bits):
    for bit in range(bits):
        if (mask >> bit) & 1:
            index = flipped(index, bit)
    return index


class Team:
    def __init__(self, sizes):
        self.sections, self.fsdp, self.tp = sizes
        self.bits = self.tp.bit_length() - 1
        assert 1 << self.bits == self.tp
        self.s = lax.axis_index("section")
        self.f = lax.axis_index("fsdp")
        self.t = lax.axis_index("tp")
        self.hops = [
            (bit, mask)
            for bit in reversed(range(self.bits))
            for mask in range(0, self.tp, 2 << bit)
        ]
        self.place = {hop: number for number, hop in enumerate(self.hops)}

    def row(self, i):
        above = self.fsdp - 1 - self.f
        short = jnp.minimum(self.f, above)
        paired = i <= 2 * short
        distance = jnp.where(paired, lax.div(i + 1, 2), i - short)
        upward = jnp.where(paired, lax.rem(i, 2) == 1, self.f < above)
        return jnp.where(upward, self.f + distance, self.f - distance)

    def column(self, mask):
        return crossed(self.t, mask, self.bits)


def greet(team, fsdp, section_step):
    barrier = pltpu.get_barrier_semaphore()
    count = 0
    if fsdp:
        for i in range(1, team.fsdp):
            pl.semaphore_signal(
                barrier,
                inc=1,
                device_id={"fsdp": lax.rem(team.f + i, team.fsdp)},
                device_id_type=MESH,
            )
            count += 1
    for bit in range(team.bits):
        pl.semaphore_signal(
            barrier, inc=1, device_id={"tp": flipped(team.t, bit)}, device_id_type=MESH
        )
        count += 1
    if section_step:
        behind = lax.rem(team.s + team.sections - section_step, team.sections)
        pl.semaphore_signal(
            barrier, inc=1, device_id={"section": behind}, device_id_type=MESH
        )
        count += 1
    pl.semaphore_wait(barrier, count)


def rows_of(block, size):
    return pl.ds(pl.multiple_of(block * size, size), size)


class TpGather:
    def __init__(self, team, ref, size, sends, recvs):
        self.team, self.ref, self.size, self.sends, self.recvs = team, ref, size, sends, recvs

    def copy(self, hop, arriving):
        bit, mask = hop
        team = self.team
        block = team.column(mask | ((1 << bit) if arriving else 0))
        part = self.ref.at[rows_of(block, self.size)]
        return pltpu.make_async_remote_copy(
            src_ref=part,
            dst_ref=part,
            send_sem=self.sends(team.place[hop]),
            recv_sem=self.recvs(team.place[hop]),
            device_id={"tp": flipped(team.t, bit)},
            device_id_type=MESH,
        )

    def begin(self):
        for bit in reversed(range(self.team.bits)):
            self.copy((bit, 0), False).start()

    def relay(self):
        for hop in self.team.hops:
            bit, mask = hop
            if bit:
                self.copy(hop, True).wait_recv()
                for lower in reversed(range(bit)):
                    self.copy((lower, mask | (1 << bit)), False).start()

    def arrive(self):
        for hop in self.team.hops:
            if hop[0] == 0:
                self.copy(hop, True).wait_recv()

    def drain(self):
        for hop in self.team.hops:
            self.copy(hop, False).wait_send()


def add_blocks(target, rows, other, width, experts):
    wide = target[rows, :width].astype(jnp.float32) + other[:, :width].astype(jnp.float32)
    target[rows, :width] = wide.astype(target.dtype)
    if target.shape[1] > width:
        both = target[rows, width:].astype(jnp.float32) + other[:, width:].astype(jnp.float32)
        target[rows, width:] = two_parts(both, experts)


def two_parts(both, experts):
    lane = lax.broadcasted_iota(jnp.int32, both.shape, 1)
    first = lane < experts
    full = both + jnp.where(
        first, pltpu.roll(both, LANES - experts, 1), pltpu.roll(both, experts, 1)
    )
    return parted(full, first, lane < 2 * experts)


def parted(full, first, second):
    high = full.astype(jnp.bfloat16)
    low = (full - high.astype(jnp.float32)).astype(jnp.bfloat16)
    zero = jnp.zeros_like(high)
    return jnp.where(first, high, jnp.where(second, low, zero))


class TpScatter:
    def __init__(self, team, ref, size, landing, sends, recvs, width, experts):
        self.team, self.ref, self.size, self.landing = team, ref, size, landing
        self.sends, self.recvs, self.width, self.experts = sends, recvs, width, experts

    def copy(self, hop):
        bit, mask = hop
        team = self.team
        block = team.column(mask | (1 << bit))
        return pltpu.make_async_remote_copy(
            src_ref=self.ref.at[rows_of(block, self.size)],
            dst_ref=self.landing(team.place[hop]),
            send_sem=self.sends(team.place[hop]),
            recv_sem=self.recvs(team.place[hop]),
            device_id={"tp": flipped(team.t, bit)},
            device_id_type=MESH,
        )

    def send(self, bit):
        for hop in self.team.hops:
            if hop[0] == bit:
                self.copy(hop).start()

    def add(self, bit):
        for hop in self.team.hops:
            if hop[0] == bit:
                self.copy(hop).wait_recv()
                add_blocks(
                    self.ref,
                    rows_of(self.team.column(hop[1]), self.size),
                    self.landing(self.team.place[hop]),
                    self.width,
                    self.experts,
                )

    def drain(self):
        for hop in self.team.hops:
            self.copy(hop).wait_send()

    def run(self):
        for bit in range(self.team.bits):
            self.send(bit)
            self.add(bit)


def ring_copy(team, step, source, target, sends, recvs):
    ahead = lax.rem(team.s + team.sections + step, team.sections)
    return pltpu.make_async_remote_copy(
        src_ref=source,
        dst_ref=target,
        send_sem=sends.at[0],
        recv_sem=recvs.at[0],
        device_id={"section": ahead},
        device_id_type=MESH,
    )


def group_exchange(team, gathered, partial, landing, across, sems, size, width, experts, prepare, first, second, spare=None):
    ag_send, ag_recv, agz_send, agz_recv, rs_send, rs_recv, rsz_send, rsz_recv = sems
    count = team.fsdp

    def gather(i):
        return TpGather(
            team,
            gathered.at[team.row(i)],
            size,
            lambda place: ag_send.at[i, place],
            lambda place: ag_recv.at[i, place],
        )

    def scatter(i):
        return TpScatter(
            team,
            partial.at[team.row(i)],
            size,
            lambda place: landing.at[i, place],
            lambda place: rs_send.at[i, place],
            lambda place: rs_recv.at[i, place],
            width,
            experts,
        )

    def own_rows():
        return rows_of(team.t, size)

    def gather_across(i, arriving):
        source = team.row(i) if arriving else team.f
        part = gathered.at[source, own_rows()]
        return pltpu.make_async_remote_copy(
            src_ref=part,
            dst_ref=part,
            send_sem=agz_send.at[i],
            recv_sem=agz_recv.at[source],
            device_id={"fsdp": team.row(i)},
            device_id_type=MESH,
        )

    def scatter_across(i, arriving):
        source = team.row(i) if arriving else team.f
        return pltpu.make_async_remote_copy(
            src_ref=partial.at[team.row(i), own_rows()],
            dst_ref=across.at[source],
            send_sem=rsz_send.at[i],
            recv_sem=rsz_recv.at[source],
            device_id={"fsdp": team.row(i)},
            device_id_type=MESH,
        )

    def relay_across(i):
        gather_across(i, True).wait_recv()
        gather(i).begin()

    gather(0).begin()
    for i in range(1, min(count, 3)):
        gather_across(i, False).start()
    gather(0).relay()
    for i in range(3, count):
        gather_across(i, False).start()
    prepare()
    if count > 1:
        relay_across(1)

    def step(i, carry):
        @pl.when(i < count)
        def _():
            gather(i).arrive()
            first(team.row(i))

        @pl.when(i + 2 < count)
        def _():
            relay_across(i + 2)

        for bit in range(team.bits):
            done = i - 1 - bit

            @pl.when((done >= min(bit, 1)) & (done < count))
            def _():
                scatter(done).add(bit)

                @pl.when(done > 0)
                def _():
                    if bit + 1 < team.bits:
                        scatter(done).send(bit + 1)
                    else:
                        scatter_across(done, False).start()

        @pl.when(i + 1 < count)
        def _():
            gather(i + 1).relay()

        @pl.when(i < count)
        def _():
            second(team.row(i))
            scatter(i).send(0)

        if team.bits > 1:

            @pl.when(i == max(count, 1))
            def _():
                scatter(0).send(1)

        if spare is not None:

            @pl.when(i >= count)
            def _():
                spare(i - count)

        return carry

    lax.fori_loop(0, count + team.bits, step, 0)
    for bit in range(1, team.bits):
        scatter(0).add(bit)
        if bit + 1 < team.bits:
            scatter(0).send(bit + 1)
    if spare is not None:
        spare(team.bits)

    def finish(i, carry):
        gather_across(i, False).wait_send()
        scatter_across(i, False).wait_send()
        return carry

    def settle(i, carry):
        gather(i).drain()
        scatter(i).drain()
        return carry

    total = partial[team.f, own_rows()].astype(jnp.float32)
    for i in range(1, count):
        scatter_across(i, True).wait_recv()
        total = total + across[team.row(i)].astype(jnp.float32)
    lax.fori_loop(1, count, finish, 0)
    lax.fori_loop(0, count, settle, 0)
    return total[:, :width], (total[:, width:] if total.shape[1] > width else None)


def group_sems(team_sizes):
    _, fsdp, tp = team_sizes
    dma = pltpu.SemaphoreType.DMA
    return [
        dma((fsdp, tp)), dma((fsdp, tp)), dma((fsdp,)), dma((fsdp,)),
        dma((fsdp, tp)), dma((fsdp, tp)), dma((fsdp,)), dma((fsdp,)),
    ]


def share_parts(share, experts):
    lane = lax.broadcasted_iota(jnp.int32, share.shape, 1)
    high = share.astype(jnp.bfloat16)
    rest = share - high.astype(jnp.float32)
    middle = rest.astype(jnp.bfloat16)
    low = (rest - middle.astype(jnp.float32)).astype(jnp.bfloat16)
    zero = jnp.zeros_like(high)
    return jnp.where(
        lane < experts,
        high,
        jnp.where(lane < 2 * experts, middle, jnp.where(lane < 3 * experts, low, zero)),
    )


def chunks(length, body, size=1024):
    size = min(size, length)

    def step(c, carry):
        body(pl.multiple_of(c * size, size), size)
        return carry

    lax.fori_loop(0, length // size, step, 0)


def product(left, right):
    return jnp.dot(left, right, preferred_element_type=jnp.float32)


def product_turned(left, right):
    return lax.dot_general(
        left, right, (((1,), (1,)), ((), ())), preferred_element_type=jnp.float32
    )


def comm_params(number):
    return pltpu.CompilerParams(
        collective_id=number, has_side_effects=True, vmem_limit_bytes=VMEM_LIMIT
    )


def begin_layer(sizes, layer_in, gain, number):
    rows, width = layer_in.shape
    tp = sizes[2]

    def kernel(in_ref, gain_ref, out_ref, sends, recvs):
        team = Team(sizes)
        greet(team, False, 0)
        scaled, _, _ = norm_rows(in_ref[...].astype(jnp.float32), gain_ref[...])
        out_ref[rows_of(team.t, rows)] = scaled.astype(jnp.bfloat16)
        gather = TpGather(team, out_ref, rows, lambda p: sends.at[p], lambda p: recvs.at[p])
        gather.begin()
        gather.relay()
        gather.arrive()
        gather.drain()

    return pl.pallas_call(
        kernel,
        out_shape=jax.ShapeDtypeStruct((tp * rows, width), jnp.bfloat16),
        in_specs=[WHOLE_VMEM] * 2,
        out_specs=WHOLE_VMEM,
        scratch_shapes=[pltpu.SemaphoreType.DMA((tp,)), pltpu.SemaphoreType.DMA((tp,))],
        compiler_params=comm_params(number),
    )(layer_in, gain)


def moe_forward(sizes, partial_out, residual, chosen, weights, fresh, experts, number):
    router, gain_one, gain_two, gate_up, down, spread_map = weights
    sections, fsdp, tp = sizes
    rows, width = residual.shape
    band = tp * rows
    hidden = down.shape[0]
    copies = LANES // experts
    tail = fresh is not None
    bf16, f32 = jnp.bfloat16, jnp.float32
    shapes = [
        jax.ShapeDtypeStruct((fsdp, band, width), bf16),
        jax.ShapeDtypeStruct((fsdp, band, 2 * hidden), bf16),
        jax.ShapeDtypeStruct((fsdp, band, LANES), f32),
        jax.ShapeDtypeStruct((rows, width), f32),
        jax.ShapeDtypeStruct((rows, width), bf16),
    ]
    if tail:
        shapes += [
            jax.ShapeDtypeStruct((rows, width), bf16),
            jax.ShapeDtypeStruct((band, width), bf16),
        ]
    dma = pltpu.SemaphoreType.DMA
    scratch = [
        pltpu.VMEM((band, width), bf16),
        pltpu.VMEM((tp, rows, width), bf16),
        pltpu.VMEM((fsdp, band, width), bf16),
        pltpu.VMEM((fsdp, tp - 1, rows, width), bf16),
        pltpu.VMEM((fsdp, rows, width), bf16),
        pltpu.VMEM((band, hidden), bf16),
        pltpu.VMEM((band, LANES), bf16),
        pltpu.VMEM((rows, width), bf16),
        pltpu.VMEM((width, 2 * hidden), bf16),
        pltpu.VMEM((hidden, width), bf16),
        pltpu.VMEM((fsdp, band, width), bf16),
        pltpu.VMEM((fsdp, band, 2 * hidden), bf16),
        dma((tp,)), dma((tp,)), dma((tp,)), dma((tp,)), dma((1,)), dma((1,)),
        dma((2,)), dma((fsdp,)), dma((fsdp,)),
    ] + group_sems(sizes)
    own, out = WHOLE_VMEM, pl.BlockSpec(memory_space=pl.ANY)

    def kernel(*refs):
        part_ref, res_ref, chosen_ref, router_ref, one_ref, two_ref, both_hbm, down_hbm, map_ref = refs[:9]
        refs = refs[9:]
        if tail:
            fresh_ref, refs = refs[0], refs[1:]
        all_hbm, pre_hbm, share_ref, state_ref, result_ref = refs[:5]
        refs = refs[5:]
        if tail:
            next_ref, attn_ref = refs[:2]
            refs = refs[2:]
        sums, sums_in, partial, landing, across, weighted, parts, moved = refs[:8]
        both_ref, down_ref, all_ref, pre_ref = refs[8:12]
        tr_send, tr_recv, tg_send, tg_recv, sec_send, sec_recv, load_sem, all_sem, pre_sem = refs[12:21]
        sems = refs[21:]
        team = Team(sizes)
        loads = [
            pltpu.make_async_copy(both_hbm, both_ref, load_sem.at[0]),
            pltpu.make_async_copy(down_hbm, down_ref, load_sem.at[1]),
        ]
        for load in loads:
            load.start()

        def all_out(row):
            return pltpu.make_async_copy(all_ref.at[row], all_hbm.at[row], all_sem.at[row])

        def pre_out(row):
            return pltpu.make_async_copy(pre_ref.at[row], pre_hbm.at[row], pre_sem.at[row])

        def prepare():
            for load in loads:
                load.wait()

        sums[...] = part_ref[...]
        greet(team, True, 1 if tail else 0)
        reduce = TpScatter(
            team, sums, rows, lambda p: sums_in.at[p], lambda p: tr_send.at[p],
            lambda p: tr_recv.at[p], width, experts,
        )
        reduce.run()
        state = res_ref[...].astype(f32) + branch_scale * sums[rows_of(team.t, rows)].astype(f32)
        state_ref[...] = state
        scaled, _, _ = norm_rows(state, two_ref[...])
        all_ref[team.f, rows_of(team.t, rows)] = scaled.astype(bf16)

        def first(row):
            all_out(row).start()
            logits = product(all_ref[row], router_ref[...])
            logits = jnp.where(chosen_ref[row].astype(f32) > 0.5, logits, masked_score)
            grown = jnp.exp(logits - jnp.max(logits, axis=-1, keepdims=True))
            total = jnp.sum(grown, axis=-1, keepdims=True) * (1.0 / copies)
            share = grown / total
            share_ref[row] = share
            parts[...] = share_parts(share, experts)

            def piece(start, size):
                here, there = pl.ds(start, size), pl.ds(pl.multiple_of(hidden + start, size), size)
                gate = product(all_ref[row], both_ref[:, here])
                up = product(all_ref[row], both_ref[:, there])
                pre_ref[row, :, here] = gate.astype(bf16)
                pre_ref[row, :, there] = up.astype(bf16)
                wide = product(parts[...], map_ref[:, here])
                weighted[:, here] = (wide * (gate * jax.nn.sigmoid(gate) * up)).astype(bf16)

            chunks(hidden, piece)
            pre_out(row).start()

        def second(row):
            def piece(start, size):
                here = pl.ds(start, size)
                partial[row, :, here] = product(weighted[...], down_ref[:, here]).astype(bf16)

            chunks(width, piece)

        total, _ = group_exchange(
            team, all_ref, partial, landing, across, sems, rows, width, experts, prepare, first, second
        )
        result_ref[...] = (state_ref[...] + branch_scale * total).astype(bf16)
        reduce.drain()
        if tail:
            move = ring_copy(team, 1, result_ref, moved, sec_send, sec_recv)
            move.start()
            move.wait_recv()
            layer_in = jnp.where(team.s == 0, fresh_ref[...], moved[...])
            next_ref[...] = layer_in
            scaled, _, _ = norm_rows(layer_in.astype(f32), one_ref[...])
            attn_ref[rows_of(team.t, rows)] = scaled.astype(bf16)
            gather = TpGather(
                team, attn_ref, rows, lambda p: tg_send.at[p], lambda p: tg_recv.at[p]
            )
            gather.begin()
            gather.relay()
            gather.arrive()
            gather.drain()
            move.wait_send()
        for row in range(fsdp):
            all_out(row).wait()
            pre_out(row).wait()

    args = [partial_out, residual, chosen, router, gain_one, gain_two, gate_up, down, spread_map]
    if tail:
        args.append(fresh)
    return pl.pallas_call(
        kernel,
        out_shape=shapes,
        in_specs=[own] * 6 + [out] * 2 + [own] * (len(args) - 8),
        out_specs=[out] * 2 + [own] * (len(shapes) - 2),
        scratch_shapes=scratch,
        compiler_params=comm_params(number),
        name="moe_forward",
    )(*args)


def moe_backward(sizes, upstream, state, share, pre, moe_in, weights, experts, sums, final, number):
    router, gain_two, gate_up, down, spread_map, pick_map = weights
    sections, fsdp, tp = sizes
    rows, width = upstream.shape
    band = tp * rows
    hidden = down.shape[0]
    bf16, f32 = jnp.bfloat16, jnp.float32
    leaving = bf16 if final else f32
    shapes = [
        jax.ShapeDtypeStruct((width, 2 * hidden), leaving),
        jax.ShapeDtypeStruct((hidden, width), f32),
        jax.ShapeDtypeStruct((rows, LANES), bf16),
        jax.ShapeDtypeStruct((1, width), f32),
        jax.ShapeDtypeStruct((rows, width), f32),
        jax.ShapeDtypeStruct((band, width), bf16),
    ]
    dma = pltpu.SemaphoreType.DMA
    wider = width + LANES
    both_units = team_units(tp)
    both_step = 2 * hidden // both_units
    loops = [both_step // chunk_size(both_step), width // chunk_size(width)]
    both_size, down_size = chunk_size(both_step), chunk_size(width)
    scratch = [
        pltpu.VMEM((fsdp, band, wider), bf16),
        pltpu.VMEM((fsdp, tp - 1, rows, wider), bf16),
        pltpu.VMEM((fsdp, rows, wider), bf16),
        pltpu.VMEM((band, LANES), bf16),
        pltpu.VMEM((band, LANES), f32),
        pltpu.VMEM((width, 2 * hidden), bf16),
        pltpu.VMEM((hidden, width), bf16),
        pltpu.VMEM((fsdp, band, 2 * hidden), bf16),
        pltpu.VMEM((fsdp, band, width), bf16),
        pltpu.VMEM((fsdp, band, 2 * hidden), bf16),
        pltpu.VMEM((fsdp, band, hidden), bf16),
        pltpu.VMEM((fsdp, band, width), bf16),
        pltpu.VMEM((width, 2 * hidden), f32),
        pltpu.VMEM((hidden, width), f32),
        pltpu.VMEM((width, 2 * hidden) if final else (16, LANES), bf16),
        dma((tp,)), dma((tp,)), dma((5,)), dma((fsdp,)), dma((2,)),
    ] + group_sems(sizes)
    own, out = WHOLE_VMEM, pl.BlockSpec(memory_space=pl.ANY)
    adding = sums is not None

    def kernel(*refs):
        up_ref, state_ref, share_ref, pre_hbm, router_ref, gain_ref, both_hbm, down_hbm, map_ref, pick_ref, in_hbm = refs[:11]
        refs = refs[11:]
        if adding:
            both_old, down_old = refs[:2]
            refs = refs[2:]
        both_out, down_out, logit_ref, gain_out, state_out, attn_ref = refs[:6]
        partial, landing, across, parts, share_sum, both_ref, down_ref, pre_ref, all_ref, grad_ref, weighted_ref = refs[6:17]
        in_ref, both_sum, down_sum, both_low, tg_send, tg_recv, load_sem, pre_sem, out_sem = refs[17:26]
        sems = refs[26:]
        team = Team(sizes)
        loads = [
            pltpu.make_async_copy(down_hbm, down_ref, load_sem.at[0]),
            pltpu.make_async_copy(both_hbm, both_ref, load_sem.at[1]),
        ]
        later = [pltpu.make_async_copy(in_hbm, in_ref, load_sem.at[2])]
        if adding:
            later += [
                pltpu.make_async_copy(both_old, both_sum, load_sem.at[3]),
                pltpu.make_async_copy(down_old, down_sum, load_sem.at[4]),
            ]
        outs = [
            pltpu.make_async_copy(both_low if final else both_sum, both_out, out_sem.at[0]),
            pltpu.make_async_copy(down_sum, down_out, out_sem.at[1]),
        ]

        def pre_in(row):
            return pltpu.make_async_copy(pre_hbm.at[row], pre_ref.at[row], pre_sem.at[row])

        loads[0].start()
        for i in range(fsdp):
            pre_in(i).start()
        loads[1].start()
        for load in later:
            load.start()

        def prepare():
            for load in loads:
                load.wait()
            for i in range(fsdp):
                pre_in(i).wait()

        def spare(unit):
            @pl.when(unit == 0)
            def _():
                for load in later:
                    load.wait()

            if isinstance(unit, int):
                left, right, total, size = weighted_ref, all_ref, down_sum, down_size
                start, count = 0, loops[1]
            else:
                left, right, total, size = in_ref, grad_ref, both_sum, both_size
                start, count = unit * both_step, loops[0]

            def turn(c, carry):
                here = pl.ds(pl.multiple_of(start + c * size, size), size)
                made = lax.dot_general(
                    left[...].reshape(fsdp * band, left.shape[2]),
                    right[:, :, here].reshape(fsdp * band, size),
                    (((0,), (0,)), ((), ())),
                    preferred_element_type=f32,
                )
                if adding:
                    made = made + total[:, here]
                if final and total is both_sum:
                    both_low[:, here] = made.astype(bf16)
                else:
                    total[:, here] = made
                return carry

            lax.fori_loop(0, count, turn, 0)
            if isinstance(unit, int):
                for done in outs:
                    done.start()

        greet(team, True, 0)
        all_ref[team.f, rows_of(team.t, rows)] = (branch_scale * up_ref[...]).astype(bf16)

        def first(row):
            parts[...] = share_parts(share_ref[row], experts)
            share_sum[...] = jnp.zeros_like(share_sum)

            def piece(start, size):
                here, there = pl.ds(start, size), pl.ds(pl.multiple_of(hidden + start, size), size)
                hidden_grad = product_turned(all_ref[row], down_ref[here])
                gate = pre_ref[row, :, here].astype(f32)
                up = pre_ref[row, :, there].astype(f32)
                wide = product(parts[...], map_ref[:, here])
                sigmoid_gate = jax.nn.sigmoid(gate)
                swish = gate * sigmoid_gate
                value = swish * up
                weighted_ref[row, :, here] = (wide * value).astype(bf16)
                both = hidden_grad * value
                high = both.astype(bf16)
                low = (both - high.astype(f32)).astype(bf16)
                share_sum[...] += product(high, pick_ref[here]) + product(low, pick_ref[here])
                scaled = wide * hidden_grad
                grad_ref[row, :, here] = (
                    scaled * up * sigmoid_gate * (1.0 + gate * (1.0 - sigmoid_gate))
                ).astype(bf16)
                grad_ref[row, :, there] = (scaled * swish).astype(bf16)

            chunks(hidden, piece)

        def second(row):
            def piece(start, size):
                here = pl.ds(start, size)
                partial[row, :, here] = product_turned(grad_ref[row], both_ref[here]).astype(bf16)

            chunks(width, piece)
            lane = lax.broadcasted_iota(jnp.int32, (band, LANES), 1)
            partial[row, :, width:] = parted(share_sum[...], lane < experts, lane < 2 * experts)

        total, extra = group_exchange(
            team, all_ref, partial, landing, across, sems, rows, width, experts, prepare, first, second, spare
        )
        lane = lax.broadcasted_iota(jnp.int32, (rows, LANES), 1)
        valid = lane < experts
        share_grad = extra + pltpu.roll(extra, LANES - experts, 1)
        own_share = jnp.where(valid, share_ref[team.f, rows_of(team.t, rows)], 0.0)
        inner = jnp.sum(own_share * share_grad, axis=-1, keepdims=True)
        logit_grad = (own_share * (share_grad - inner)).astype(bf16)
        logit_ref[...] = logit_grad
        norm_grad = total + product_turned(logit_grad, router_ref[...])
        _, normed, inverse = norm_rows(state_ref[...], gain_ref[...])
        back, gain_grad = norm_back(norm_grad, normed, inverse, gain_ref[...])
        gain_out[...] = gain_grad
        state_grad = up_ref[...] + back
        state_out[...] = state_grad
        attn_ref[rows_of(team.t, rows)] = (branch_scale * state_grad).astype(bf16)
        gather = TpGather(team, attn_ref, rows, lambda p: tg_send.at[p], lambda p: tg_recv.at[p])
        gather.begin()
        gather.relay()
        gather.arrive()
        gather.drain()
        for done in outs:
            done.wait()

    args = [upstream, state, share, pre, router, gain_two, gate_up, down, spread_map, pick_map, moe_in]
    if adding:
        args += list(sums)
    return pl.pallas_call(
        kernel,
        out_shape=shapes,
        in_specs=[own] * 3 + [out] + [own] * 2 + [out] * 2 + [own] * 2 + [out] * (len(args) - 10),
        out_specs=[out] * 2 + [own] * 4,
        scratch_shapes=scratch,
        compiler_params=comm_params(number),
        name="moe_backward",
    )(*args)


def team_units(tp):
    return tp.bit_length() - 1


def chunk_size(length, most=512):
    return min(length, most)


def end_layer(sizes, partial_in, layer_in, state_grad, gain, number):
    tp = sizes[2]
    rows, width = layer_in.shape
    bf16, f32 = jnp.bfloat16, jnp.float32
    dma = pltpu.SemaphoreType.DMA

    def kernel(
        part_ref, in_ref, grad_ref, gain_ref, out_ref, gain_out, arrived_ref,
        sums, sums_in, leaving, tr_send, tr_recv, sec_send, sec_recv,
    ):
        team = Team(sizes)
        sums[...] = part_ref[...]
        greet(team, False, -1)
        reduce = TpScatter(
            team, sums, rows, lambda p: sums_in.at[p], lambda p: tr_send.at[p],
            lambda p: tr_recv.at[p], width, 0,
        )
        reduce.run()
        norm_grad = sums[rows_of(team.t, rows)].astype(f32)
        _, normed, inverse = norm_rows(in_ref[...].astype(f32), gain_ref[...])
        back, gain_grad = norm_back(norm_grad, normed, inverse, gain_ref[...])
        gain_out[...] = gain_grad
        result = grad_ref[...] + back
        out_ref[...] = result
        leaving[...] = result.astype(bf16)
        move = ring_copy(team, -1, leaving, arrived_ref, sec_send, sec_recv)
        move.start()
        reduce.drain()
        move.wait()

    return pl.pallas_call(
        kernel,
        out_shape=[
            jax.ShapeDtypeStruct((rows, width), f32),
            jax.ShapeDtypeStruct((1, width), f32),
            jax.ShapeDtypeStruct((rows, width), bf16),
        ],
        in_specs=[WHOLE_VMEM] * 4,
        out_specs=[WHOLE_VMEM] * 3,
        scratch_shapes=[
            pltpu.VMEM((tp * rows, width), bf16),
            pltpu.VMEM((tp, rows, width), bf16),
            pltpu.VMEM((rows, width), bf16),
            dma((tp,)), dma((tp,)), dma((1,)), dma((1,)),
        ],
        compiler_params=comm_params(number),
        name="end_layer",
    )(partial_in, layer_in, state_grad, gain)


def order_map(inputs, outputs, count, part, turned):
    across = count * part
    source = lax.broadcasted_iota(jnp.int32, (inputs, outputs), 1 if turned else 0)
    target = lax.broadcasted_iota(jnp.int32, (inputs, outputs), 0 if turned else 1)
    e, rest = lax.div(source, across), lax.rem(source, across)
    f, h = lax.div(rest, part), lax.rem(rest, part)
    return (f * LANES + e * part + h == target).astype(jnp.bfloat16)


def block_steps(blocks):
    for steps in (2, 1):
        if blocks % steps == 0:
            return steps


def outgoing_experts(w_gate, w_up, count):
    experts, depth, hidden = w_gate.shape
    part = hidden // count
    bunch = LANES // part
    across = bunch * hidden
    steps = block_steps(experts // bunch)
    each = experts // bunch // steps

    def kernel(gate_ref, up_ref, out_ref, table):
        @pl.when((pl.program_id(0) == 0) & (pl.program_id(1) == 0))
        def _():
            table[...] = order_map(across, count * LANES, count, part, False)

        def move(ref):
            for b in range(each):
                lanes = jnp.concatenate([ref[b * bunch + e] for e in range(bunch)], axis=1)
                moved = product(lanes, table[...]).astype(jnp.bfloat16)
                for f in range(count):
                    out_ref[f, :, b * LANES : (b + 1) * LANES] = moved[:, f * LANES : (f + 1) * LANES]

        @pl.when(pl.program_id(0) == 0)
        def _():
            move(gate_ref)

        @pl.when(pl.program_id(0) == 1)
        def _():
            move(up_ref)

    block = (each * bunch, depth, hidden)
    return pl.pallas_call(
        kernel,
        grid=(2, steps),
        out_shape=jax.ShapeDtypeStruct((count, depth, 2 * steps * each * LANES), jnp.bfloat16),
        in_specs=[
            pl.BlockSpec(block, lambda w, b: (jnp.where(w == 0, b, steps - 1), 0, 0)),
            pl.BlockSpec(block, lambda w, b: (jnp.where(w == 1, b, 0), 0, 0)),
        ],
        out_specs=pl.BlockSpec((count, depth, each * LANES), lambda w, b: (0, 0, w * steps + b)),
        scratch_shapes=[pltpu.VMEM((across, count * LANES), jnp.bfloat16)],
        compiler_params=pltpu.CompilerParams(vmem_limit_bytes=VMEM_LIMIT),
        name="outgoing_experts",
    )(w_gate, w_up)


def incoming_experts(both, experts, hidden):
    count, depth, width = both.shape
    part = hidden // count
    bunch = LANES // part
    across = bunch * hidden
    steps = block_steps(experts // bunch)
    each = experts // bunch // steps

    def kernel(in_ref, gate_ref, up_ref, table):
        @pl.when((pl.program_id(0) == 0) & (pl.program_id(1) == 0))
        def _():
            table[...] = order_map(count * LANES, across, count, part, True)

        def store(ref):
            for b in range(each):
                lanes = jnp.concatenate(
                    [in_ref[f, :, b * LANES : (b + 1) * LANES] for f in range(count)], axis=1
                )
                moved = product(lanes, table[...])
                for e in range(bunch):
                    ref[b * bunch + e] = moved[:, e * hidden : (e + 1) * hidden]

        @pl.when(pl.program_id(0) == 0)
        def _():
            store(gate_ref)

        @pl.when(pl.program_id(0) == 1)
        def _():
            store(up_ref)

    shape = jax.ShapeDtypeStruct((experts, depth, hidden), jnp.float32)
    block = (each * bunch, depth, hidden)
    return pl.pallas_call(
        kernel,
        grid=(2, steps),
        out_shape=[shape, shape],
        in_specs=[pl.BlockSpec((count, depth, each * LANES), lambda w, b: (0, 0, w * steps + b))],
        out_specs=[
            pl.BlockSpec(block, lambda w, b: (jnp.where(w == 0, b, steps - 1), 0, 0)),
            pl.BlockSpec(block, lambda w, b: (jnp.where(w == 1, b, 0), 0, 0)),
        ],
        scratch_shapes=[pltpu.VMEM((count * LANES, across), jnp.bfloat16)],
        compiler_params=pltpu.CompilerParams(vmem_limit_bytes=VMEM_LIMIT),
        name="incoming_experts",
    )(both)


def line_barrier(team, tp):
    barrier = pltpu.get_barrier_semaphore()
    count = 0
    for i in range(1, team.fsdp):
        pl.semaphore_signal(
            barrier,
            inc=1,
            device_id={"fsdp": lax.rem(team.f + i, team.fsdp)},
            device_id_type=MESH,
        )
        count += 1
    if tp:
        for bit in range(team.bits):
            pl.semaphore_signal(
                barrier, inc=1, device_id={"tp": flipped(team.t, bit)}, device_id_type=MESH
            )
            count += 1
    pl.semaphore_wait(barrier, count)


def gather_weights(sizes, matrix, small, number):
    fsdp = sizes[1]
    depth, width = matrix.shape
    dma = pltpu.SemaphoreType.DMA

    def kernel(matrix_ref, small_ref, all_ref, few_ref, held, *sems):
        up_send, up_recv, down_send, down_recv, few_send, few_recv, local, out_sem = sems
        team = Team(sizes)
        f = team.f
        mine = pltpu.make_async_copy(matrix_ref, held.at[f], local.at[0])
        mine.start()
        few_ref[f] = small_ref[...]
        line_barrier(team, False)

        def few(i, arriving):
            other = lax.rem(f + (fsdp - i if arriving else i), fsdp)
            part = few_ref.at[other if arriving else f]
            return pltpu.make_async_remote_copy(
                src_ref=part,
                dst_ref=part,
                send_sem=few_send.at[i],
                recv_sem=few_recv.at[i],
                device_id={"fsdp": other},
                device_id_type=MESH,
            )

        for i in range(1, fsdp):
            few(i, False).start()
        mine.wait()

        def hand(block, step):
            sends, recvs = (up_send, up_recv) if step > 0 else (down_send, down_recv)
            return pltpu.make_async_remote_copy(
                src_ref=held.at[block],
                dst_ref=held.at[block],
                send_sem=sends.at[block],
                recv_sem=recvs.at[block],
                device_id={"fsdp": lax.rem(f + step + fsdp, fsdp)},
                device_id_type=MESH,
            )

        def out(block):
            return pltpu.make_async_copy(held.at[block], all_ref.at[block], out_sem.at[block])

        @pl.when(f < fsdp - 1)
        def _():
            hand(f, 1).start()

        @pl.when(f > 0)
        def _():
            hand(f, -1).start()

        out(f).start()

        def step(i, carry):
            below, above = f - i, f + i

            @pl.when(below >= 0)
            def _():
                hand(below, 1).wait_recv()

                @pl.when(f < fsdp - 1)
                def _():
                    hand(below, 1).start()

                out(below).start()

            @pl.when(above < fsdp)
            def _():
                hand(above, -1).wait_recv()

                @pl.when(f > 0)
                def _():
                    hand(above, -1).start()

                out(above).start()

            return carry

        lax.fori_loop(1, fsdp, step, 0)

        def finish(g, carry):
            @pl.when((g <= f) & (f < fsdp - 1))
            def _():
                hand(g, 1).wait_send()

            @pl.when((g >= f) & (f > 0))
            def _():
                hand(g, -1).wait_send()

            out(g).wait()
            return carry

        lax.fori_loop(0, fsdp, finish, 0)
        for i in range(1, fsdp):
            few(i, True).wait_recv()
            few(i, False).wait_send()

    anywhere = pl.BlockSpec(memory_space=pl.ANY)
    return pl.pallas_call(
        kernel,
        out_shape=[
            jax.ShapeDtypeStruct((fsdp, depth, width), matrix.dtype),
            jax.ShapeDtypeStruct((fsdp,) + small.shape, small.dtype),
        ],
        in_specs=[anywhere, WHOLE_VMEM],
        out_specs=[anywhere, WHOLE_VMEM],
        scratch_shapes=[pltpu.VMEM((fsdp, depth, width), matrix.dtype)]
        + [dma((fsdp,)) for _ in range(6)]
        + [dma((1,)), dma((fsdp,))],
        compiler_params=comm_params(number),
        name="gather_weights",
    )(matrix, small)


def reduce_weights(sizes, matrix, small, number):
    tp, fsdp = sizes[2], sizes[1]
    _, depth, width = matrix.shape
    count_rows = small.shape[0]
    portion = small.shape[1] // fsdp
    bits = tp.bit_length() - 1
    bf16, f32 = jnp.bfloat16, jnp.float32
    dma = pltpu.SemaphoreType.DMA

    def kernel(matrix_ref, small_ref, sum_ref, few_ref, up, down, up_in, down_in, few_sum, few_tp, few_cut, few_in, *sems):
        up_send, up_recv, down_send, down_recv, tp_send, tp_recv, few_send, few_recv = sems
        team = Team(sizes)
        f = team.f
        line_barrier(team, True)

        def pass_on(g, step):
            sends, recvs = (up_send, up_recv) if step > 0 else (down_send, down_recv)
            return pltpu.make_async_remote_copy(
                src_ref=(up if step > 0 else down).at[g],
                dst_ref=(up_in if step > 0 else down_in).at[g],
                send_sem=sends.at[g],
                recv_sem=recvs.at[g],
                device_id={"fsdp": lax.rem(f + step + fsdp, fsdp)},
                device_id_type=MESH,
            )

        def tp_copy(bit):
            return pltpu.make_async_remote_copy(
                src_ref=few_sum.at[bit],
                dst_ref=few_tp.at[bit],
                send_sem=tp_send.at[bit],
                recv_sem=tp_recv.at[bit],
                device_id={"tp": flipped(team.t, bit)},
                device_id_type=MESH,
            )

        few_sum[0] = small_ref[...]

        def step(i, carry):
            high, low = fsdp - 1 - i, i

            @pl.when(high > f)
            def _():
                @pl.when(f == 0)
                def _():
                    up[high] = matrix_ref[high]

                @pl.when(f > 0)
                def _():
                    pass_on(high, 1).wait_recv()
                    up[high] = (matrix_ref[high].astype(f32) + up_in[high].astype(f32)).astype(bf16)

                pass_on(high, 1).start()

            @pl.when(low < f)
            def _():
                @pl.when(f == fsdp - 1)
                def _():
                    down[low] = matrix_ref[low]

                @pl.when(f < fsdp - 1)
                def _():
                    pass_on(low, -1).wait_recv()
                    down[low] = (matrix_ref[low].astype(f32) + down_in[low].astype(f32)).astype(bf16)

                pass_on(low, -1).start()

            return carry

        lax.fori_loop(0, fsdp - 1, step, 0)
        for bit in range(bits):
            tp_copy(bit).start()
            tp_copy(bit).wait_recv()
            few_sum[bit + 1] = few_sum[bit] + few_tp[bit]
        for g in range(fsdp):
            few_cut[g] = few_sum[bits, :, g * portion : (g + 1) * portion]

        def few(i, arriving):
            other = lax.rem(f + (fsdp - i if arriving else i), fsdp)
            return pltpu.make_async_remote_copy(
                src_ref=few_cut.at[other],
                dst_ref=few_in.at[i],
                send_sem=few_send.at[i],
                recv_sem=few_recv.at[i],
                device_id={"fsdp": other},
                device_id_type=MESH,
            )

        for i in range(1, fsdp):
            few(i, False).start()
        sum_ref[...] = matrix_ref[f].astype(f32)

        @pl.when(f > 0)
        def _():
            pass_on(f, 1).wait_recv()
            sum_ref[...] += up_in[f].astype(f32)

        @pl.when(f < fsdp - 1)
        def _():
            pass_on(f, -1).wait_recv()
            sum_ref[...] += down_in[f].astype(f32)

        total = few_cut[f]
        for i in range(1, fsdp):
            few(i, True).wait_recv()
            total = total + few_in[i]
        few_ref[...] = total

        def finish(g, carry):
            @pl.when(g > f)
            def _():
                pass_on(g, 1).wait_send()

            @pl.when(g < f)
            def _():
                pass_on(g, -1).wait_send()

            return carry

        lax.fori_loop(0, fsdp, finish, 0)
        for i in range(1, fsdp):
            few(i, False).wait_send()
        for bit in range(bits):
            tp_copy(bit).wait_send()

    return pl.pallas_call(
        kernel,
        out_shape=[
            jax.ShapeDtypeStruct((depth, width), f32),
            jax.ShapeDtypeStruct((count_rows, portion), f32),
        ],
        in_specs=[WHOLE_VMEM] * 2,
        out_specs=[WHOLE_VMEM] * 2,
        scratch_shapes=[pltpu.VMEM((fsdp, depth, width), bf16) for _ in range(4)]
        + [
            pltpu.VMEM((bits + 1,) + small.shape, f32),
            pltpu.VMEM((bits,) + small.shape, f32),
            pltpu.VMEM((fsdp, count_rows, portion), f32),
            pltpu.VMEM((fsdp, count_rows, portion), f32),
        ]
        + [dma((fsdp,)) for _ in range(4)]
        + [dma((tp,)), dma((tp,)), dma((fsdp,)), dma((fsdp,))],
        compiler_params=comm_params(number),
        name="reduce_weights",
    )(matrix, small)


def exchange(blocks):
    return lax.all_to_all(blocks, "fsdp", split_axis=0, concat_axis=0, tiled=True)


def attention_forward(attn_in, segment, w_qkv, w_output):
    query_width = w_output.shape[0]
    key_width = (w_qkv.shape[1] - query_width) // 2
    key_value_heads = key_width // HEAD_SIZE
    count_of_tokens = attn_in.shape[0]
    permitted_mask = allowed_pairs(segment)
    cosine, sine = rope_tables(permitted_mask)
    qkv = jnp.dot(attn_in, w_qkv, preferred_element_type=jnp.float32)
    turned = rotate(
        qkv[:, : query_width + key_width].reshape(count_of_tokens, -1, HEAD_SIZE), cosine, sine
    ).astype(jnp.bfloat16)
    query_rows = turned[:, : query_width // HEAD_SIZE].reshape(
        count_of_tokens, key_value_heads, QUERY_HEADS // KEY_VALUE_HEADS, HEAD_SIZE
    )
    key_matrix = turned[:, query_width // HEAD_SIZE :]
    value_matrix = (
        qkv[:, query_width + key_width :]
        .astype(jnp.bfloat16)
        .reshape(count_of_tokens, key_value_heads, HEAD_SIZE)
    )
    attended, log_sum_exp = attend(query_rows, key_matrix, value_matrix, permitted_mask)
    mixed_heads = attended.reshape(count_of_tokens, -1)
    partial = jnp.dot(mixed_heads, w_output, preferred_element_type=jnp.float32)
    kept = (
        query_rows, key_matrix, value_matrix, attended, log_sum_exp, cosine, sine, permitted_mask
    )
    return (partial.astype(jnp.bfloat16), kept)


def attention_gradients(attn_grad, kept, w_qkv, w_output):
    (
        query_rows, key_matrix, value_matrix, attended, log_sum_exp, cosine, sine, permitted_mask
    ) = kept
    count_of_tokens = attn_grad.shape[0]
    key_value_heads = key_matrix.shape[1]
    mixed_heads = attended.reshape(count_of_tokens, -1)
    head_gradient = jnp.dot(attn_grad, w_output.T, preferred_element_type=jnp.float32).astype(
        jnp.bfloat16
    )
    query_gradient, key_gradient, value_gradient = attention_backward(
        query_rows,
        key_matrix,
        value_matrix,
        permitted_mask,
        log_sum_exp,
        head_gradient.reshape(
            count_of_tokens, key_value_heads, QUERY_HEADS // KEY_VALUE_HEADS, HEAD_SIZE
        ),
    )
    turned = jnp.concatenate(
        [query_gradient.reshape(count_of_tokens, -1, HEAD_SIZE), key_gradient], axis=1
    )
    turned = rotate_back(turned, cosine, sine).reshape(count_of_tokens, -1)
    qkv_grad = jnp.concatenate(
        [turned, value_gradient.reshape(count_of_tokens, -1)], axis=1
    ).astype(jnp.bfloat16)
    input_part = lax.dot_general(
        qkv_grad, w_qkv, (((1,), (1,)), ((), ())), preferred_element_type=jnp.float32
    )
    return (input_part.astype(jnp.bfloat16), qkv_grad, mixed_heads)


def summed_product(pairs):
    left = jnp.concatenate([pair[0] for pair in pairs], axis=0)
    right = jnp.concatenate([pair[1] for pair in pairs], axis=0)
    return lax.dot_general(
        left, right, (((0,), (0,)), ((), ())), preferred_element_type=jnp.float32
    )


def per_device(
    sizes,
    inputs,
    segment_ids,
    routes,
    w_query,
    key_weight,
    value_weight,
    w_output,
    w_router,
    gain_attn,
    gain_moe,
    w_gate,
    w_up,
    w_down,
    out_grad,
):
    section_count, fsdp_count, tp_count = sizes
    section_index = lax.axis_index("section")
    micro_count, local_rows, model_width = inputs.shape
    depth = w_query.shape[1]
    expert_count = w_router.shape[2]
    hidden_units = w_gate.shape[3]
    own_units = hidden_units // fsdp_count
    hidden = expert_count * own_units
    copies = LANES // expert_count
    query_width = w_query.shape[2]
    key_width = key_weight.shape[2]
    qkv_width = query_width + 2 * key_width
    flat_output = w_output[0].reshape(depth, -1)
    matrix = jnp.concatenate(
        [w_query[0], key_weight[0], value_weight[0], flat_output], axis=1
    )
    few = jnp.concatenate(
        [w_router[0].T, gain_attn.astype(jnp.bfloat16), gain_moe.astype(jnp.bfloat16)], axis=0
    )
    few_rows = -(-few.shape[0] // 16) * 16
    few = jnp.pad(few, ((0, few_rows - few.shape[0]), (0, 0)))
    expert_ids = jnp.arange(expert_count, dtype=jnp.int32)
    chosen_rows = jnp.any(routes[0][..., None] == expert_ids, axis=2).astype(jnp.bfloat16)
    chosen_shape = chosen_rows.shape
    few = jnp.concatenate([few, chosen_rows.reshape(-1, few.shape[1])], axis=0)
    both_out = outgoing_experts(w_gate[0], w_up[0], fsdp_count)
    matrix, few = gather_weights(sizes, matrix, few, 5)
    matrix, few, both_out = lax.optimization_barrier((matrix, few, both_out))
    gate_up = exchange(both_out).reshape(model_width, 2 * hidden)
    matrix = matrix.reshape(model_width, -1)
    chosen_rows = few[:, few_rows:].reshape((fsdp_count,) + chosen_shape)
    few = few[:, :few_rows].transpose(1, 0, 2).reshape(few_rows, model_width)
    w_qkv = matrix[:, :qkv_width]
    out_full = matrix[:, qkv_width:].reshape(-1, model_width)
    router = jnp.tile(few[:expert_count].T, (1, copies))
    gain_one = few[expert_count].astype(jnp.float32)[None]
    gain_two = few[expert_count + 1].astype(jnp.float32)[None]
    down = w_down[0].reshape(hidden, model_width)
    lane = jnp.arange(LANES, dtype=jnp.int32)
    owner = jnp.arange(hidden, dtype=jnp.int32) // own_units
    match = (lane % expert_count)[:, None] == owner[None, :]
    spread_map = (match & (lane < 3 * expert_count)[:, None]).astype(jnp.bfloat16)
    pick_map = (match & (lane < 2 * expert_count)[:, None]).astype(jnp.bfloat16).T
    chosen_rows = jnp.tile(chosen_rows, (1, 1, 1, copies))
    segment_rows = segment_ids[:, 0, :]
    tick_count = micro_count + section_count - 1
    outputs = jnp.zeros((micro_count, local_rows, model_width), jnp.bfloat16)
    history = []
    layer_in = jnp.where(section_index == 0, inputs[0], jnp.zeros_like(inputs[0]))
    attn_in = begin_layer(sizes, layer_in, gain_one, 0)
    for tick_step in range(tick_count):
        mb_index = tick_step - section_index
        active = (mb_index >= 0) & (mb_index < micro_count)
        mb_pick = jnp.clip(mb_index, 0, micro_count - 1)
        segment = lax.dynamic_index_in_dim(segment_rows, mb_pick, 0, keepdims=False)
        chosen = lax.dynamic_index_in_dim(chosen_rows, mb_pick, 1, keepdims=False)
        partial, kept = attention_forward(attn_in, segment, w_qkv, out_full)
        last = tick_step == tick_count - 1
        fresh = None if last else inputs[min(tick_step + 1, micro_count - 1)]
        weights = (router, gain_one, gain_two, gate_up, down, spread_map)
        made = moe_forward(
            sizes, partial, layer_in, chosen, weights, fresh, expert_count, 2 if last else 1
        )
        moe_in, pre, share, state, result = made[:5]
        history.append((attn_in, layer_in, kept, moe_in, pre, share, state))
        outputs = jnp.where(
            active, lax.dynamic_update_index_in_dim(outputs, result, mb_pick, 0), outputs
        )
        if not last:
            layer_in, attn_in = made[5:]
    input_grads = jnp.zeros((micro_count, local_rows, model_width), jnp.float32)
    gain_sums = None
    all_terms = []
    arrived = None
    place = (lax.axis_index("fsdp"), lax.axis_index("tp") * local_rows, 0)
    for tick_step in range(tick_count):
        mb_index = micro_count + section_count - 2 - tick_step - section_index
        active = (mb_index >= 0) & (mb_index < micro_count)
        mb_pick = jnp.clip(mb_index, 0, micro_count - 1)
        upstream = out_grad[max(micro_count - 1 - tick_step, 0)].astype(jnp.float32)
        if arrived is None:
            arrived = jnp.zeros_like(upstream)
        upstream = jnp.where(
            section_index == section_count - 1, upstream, arrived.astype(jnp.float32)
        )
        upstream = jnp.where(active, upstream, jnp.zeros_like(upstream))
        attn_in, layer_in, kept, moe_in, pre, share, state = history[tick_count - 1 - tick_step]
        last = tick_step == tick_count - 1
        both_sum, down_sum, logit_grad, gain_two_part, state_grad, attn_grad = moe_backward(
            sizes,
            upstream,
            state,
            share,
            pre,
            moe_in,
            (router, gain_two, gate_up, down, spread_map, pick_map),
            expert_count,
            None if tick_step == 0 else (both_sum, down_sum),
            last,
            7 if tick_step == 0 else 8 if last else 3,
        )
        if last:
            both_sum = exchange(both_sum.reshape(fsdp_count, depth, 2 * hidden))
        input_part, qkv_grad, mixed_heads = attention_gradients(attn_grad, kept, w_qkv, out_full)
        grad_out, gain_one_part, arrived = end_layer(
            sizes, input_part, layer_in, state_grad, gain_one, 4
        )
        input_grads = jnp.where(
            active, lax.dynamic_update_index_in_dim(input_grads, grad_out, mb_pick, 0), input_grads
        )
        gains = (gain_one_part, gain_two_part)
        gain_sums = gains if gain_sums is None else tuple(a + b for a, b in zip(gain_sums, gains))
        own_rows = lax.dynamic_slice(moe_in, place, (1, local_rows, model_width))[0]
        all_terms.append(
            (
                active,
                (
                    (attn_in, qkv_grad),
                    (mixed_heads, attn_grad),
                    (logit_grad[:, :expert_count], own_rows),
                ),
            )
        )
    chosen_terms = []
    for first in range(micro_count):
        picked = all_terms[first][1]
        for active, terms in all_terms[first + micro_count :: micro_count]:
            picked = jax.tree.map(lambda a, b: jnp.where(active, b, a), picked, terms)
        chosen_terms.append(picked)
    qkv_pairs, output_pairs, router_pairs = zip(*chosen_terms)
    gate_shard, up_shard = incoming_experts(both_sum, expert_count, hidden_units)
    down_shard = down_sum.reshape(expert_count, own_units, model_width)
    small = jnp.concatenate([summed_product(router_pairs)] + list(gain_sums), axis=0)
    small = jnp.pad(small, ((0, few_rows - small.shape[0]), (0, 0)))
    matrix_grad = jnp.concatenate(
        [summed_product(qkv_pairs), summed_product(output_pairs).reshape(model_width, -1)], axis=1
    ).astype(jnp.bfloat16)
    matrix_grad, few_grad = reduce_weights(
        sizes, matrix_grad.reshape(fsdp_count, depth, -1), small, 6
    )
    shard_sums = (
        matrix_grad[:, :query_width],
        matrix_grad[:, query_width : query_width + key_width],
        matrix_grad[:, query_width + key_width : qkv_width],
        matrix_grad[:, qkv_width:].reshape(-1, model_width),
        few_grad[:expert_count].T,
        few_grad[expert_count],
        few_grad[expert_count + 1],
        gate_shard,
        up_shard,
        down_shard,
    )
    return (outputs[None], input_grads[None]) + tuple((part[None] for part in shard_sums))


def solution(mesh):
    in_specs = (
        P(None, ("fsdp", "tp"), None),
        P(None, "fsdp", None),
        P("section", None, "fsdp", None),
        P("section", "fsdp", "tp"),
        P("section", "fsdp", "tp"),
        P("section", "fsdp", "tp"),
        P("section", ("tp", "fsdp"), None),
        P("section", "fsdp", None),
        P("section", "fsdp"),
        P("section", "fsdp"),
        P("section", None, "fsdp", "tp"),
        P("section", None, "fsdp", "tp"),
        P("section", None, ("tp", "fsdp"), None),
        P(None, ("fsdp", "tp"), None),
    )
    out_specs = (
        P("section", None, ("fsdp", "tp"), None),
        P("section", None, ("fsdp", "tp"), None),
        P("section", "fsdp", "tp"),
        P("section", "fsdp", "tp"),
        P("section", "fsdp", "tp"),
        P("section", ("tp", "fsdp"), None),
        P("section", "fsdp", None),
        P("section", "fsdp"),
        P("section", "fsdp"),
        P("section", None, "fsdp", "tp"),
        P("section", None, "fsdp", "tp"),
        P("section", None, ("tp", "fsdp"), None),
    )
    sizes = tuple(mesh.shape[axis] for axis in ("section", "fsdp", "tp"))
    return jax.shard_map(
        functools.partial(per_device, sizes), mesh=mesh, in_specs=in_specs, out_specs=out_specs, check_vma=False
    )
```

```python
import functools

import jax
import jax.numpy as jnp
from jax import lax
from jax.experimental import pallas as pl
from jax.experimental.pallas import tpu as pltpu
from jax.sharding import PartitionSpec as P

QUERY_HEADS = 16
KEY_VALUE_HEADS = 8
HEAD_SIZE = 64


norm_eps = 1e-06
branch_scale = 0.22
score_scale = 0.015625
rope_base = 10000.0
masked_score = -1e30


def norm_rows(vectors, gain_vec):
    inverse = lax.rsqrt(jnp.mean(vectors * vectors, axis=-1, keepdims=True) + norm_eps)
    normed = vectors * inverse
    return (normed * gain_vec, normed, inverse)


def norm_back(upstream, normed, inverse, gain_vec):
    scaled_grad = upstream * gain_vec
    gain_grad = jnp.sum(upstream * normed, axis=0, keepdims=True)
    inner_mean = jnp.mean(scaled_grad * normed, axis=-1, keepdims=True)
    return (inverse * (scaled_grad - normed * inner_mean), gain_grad)


def rope_tables(permitted_mask):
    offsets = (jnp.sum(permitted_mask.astype(jnp.int32), axis=1) - 1).astype(jnp.float32)
    half_dim = HEAD_SIZE // 2
    frequency = rope_base ** (-(jnp.arange(half_dim, dtype=jnp.float32) * 2.0 / HEAD_SIZE))
    angles = offsets[:, None] * frequency[None, :]
    return (jnp.cos(angles)[:, None, :], jnp.sin(angles)[:, None, :])


def rotate(vectors, cosine, sine):
    half_dim = vectors.shape[-1] // 2
    front_half = vectors[..., :half_dim]
    back_half = vectors[..., half_dim:]
    return jnp.concatenate(
        [front_half * cosine - back_half * sine, back_half * cosine + front_half * sine], axis=-1
    )


def rotate_back(vectors, cosine, sine):
    half_dim = vectors.shape[-1] // 2
    front_half = vectors[..., :half_dim]
    back_half = vectors[..., half_dim:]
    return jnp.concatenate(
        [front_half * cosine + back_half * sine, back_half * cosine - front_half * sine], axis=-1
    )


def allowed_pairs(segment):
    position = jnp.arange(segment.shape[0], dtype=jnp.int32)
    return (segment[:, None] == segment[None, :]) & (position[None, :] <= position[:, None])


def attend(query_rows, key_matrix, value_matrix, permitted_mask):
    scores = (
        jnp.einsum("qhgd,khd->hgqk", query_rows, key_matrix, preferred_element_type=jnp.float32)
        * score_scale
    )
    scores = jnp.where(permitted_mask[None, None], scores, masked_score)
    row_max = jnp.max(scores, axis=-1, keepdims=True)
    log_sum_exp = row_max + jnp.log(jnp.sum(jnp.exp(scores - row_max), axis=-1, keepdims=True))
    weights_low = jnp.exp(scores - log_sum_exp).astype(jnp.bfloat16)
    attended = jnp.einsum(
        "hgqk,khd->qhgd", weights_low, value_matrix, preferred_element_type=jnp.float32
    )
    return (attended.astype(jnp.bfloat16), log_sum_exp)


def attention_backward(
    query_rows, key_matrix, value_matrix, permitted_mask, log_sum_exp, head_gradient
):
    scores = (
        jnp.einsum("qhgd,khd->hgqk", query_rows, key_matrix, preferred_element_type=jnp.float32)
        * score_scale
    )
    scores = jnp.where(permitted_mask[None, None], scores, masked_score)
    weights_full = jnp.exp(scores - log_sum_exp)
    weights_low = weights_full.astype(jnp.bfloat16)
    value_gradient = jnp.einsum(
        "hgqk,qhgd->khd", weights_low, head_gradient, preferred_element_type=jnp.float32
    )
    weight_grad = jnp.einsum(
        "qhgd,khd->hgqk", head_gradient, value_matrix, preferred_element_type=jnp.float32
    )
    inner_sum = jnp.sum(weights_full * weight_grad, axis=-1, keepdims=True)
    score_grad = (weights_full * (weight_grad - inner_sum) * score_scale).astype(jnp.bfloat16)
    query_gradient = jnp.einsum(
        "hgqk,khd->qhgd", score_grad, key_matrix, preferred_element_type=jnp.float32
    )
    key_gradient = jnp.einsum(
        "hgqk,qhgd->khd", score_grad, query_rows, preferred_element_type=jnp.float32
    )
    return (query_gradient, key_gradient, value_gradient)


MESH = pl.DeviceIdType.MESH
LANES = 128
VMEM_LIMIT = 60 * 1024 * 1024
WHOLE_VMEM = pl.BlockSpec(memory_space=pltpu.VMEM)


def flipped(index, bit):
    step = 1 << bit
    return index + step - 2 * step * lax.rem(lax.div(index, step), 2)


def crossed(index, mask, bits):
    for bit in range(bits):
        if (mask >> bit) & 1:
            index = flipped(index, bit)
    return index


class Team:
    def __init__(self, sizes):
        self.sections, self.fsdp, self.tp = sizes
        self.bits = self.tp.bit_length() - 1
        assert 1 << self.bits == self.tp
        self.s = lax.axis_index("section")
        self.f = lax.axis_index("fsdp")
        self.t = lax.axis_index("tp")
        self.hops = [
            (bit, mask)
            for bit in reversed(range(self.bits))
            for mask in range(0, self.tp, 2 << bit)
        ]
        self.place = {hop: number for number, hop in enumerate(self.hops)}

    def row(self, i):
        above = self.fsdp - 1 - self.f
        short = jnp.minimum(self.f, above)
        paired = i <= 2 * short
        distance = jnp.where(paired, lax.div(i + 1, 2), i - short)
        upward = jnp.where(paired, lax.rem(i, 2) == 1, self.f < above)
        return jnp.where(upward, self.f + distance, self.f - distance)

    def column(self, mask):
        return crossed(self.t, mask, self.bits)


def greet(team, fsdp, section_step):
    barrier = pltpu.get_barrier_semaphore()
    count = 0
    if fsdp:
        for i in range(1, team.fsdp):
            pl.semaphore_signal(
                barrier,
                inc=1,
                device_id={"fsdp": lax.rem(team.f + i, team.fsdp)},
                device_id_type=MESH,
            )
            count += 1
    for bit in range(team.bits):
        pl.semaphore_signal(
            barrier, inc=1, device_id={"tp": flipped(team.t, bit)}, device_id_type=MESH
        )
        count += 1
    if section_step:
        behind = lax.rem(team.s + team.sections - section_step, team.sections)
        pl.semaphore_signal(
            barrier, inc=1, device_id={"section": behind}, device_id_type=MESH
        )
        count += 1
    pl.semaphore_wait(barrier, count)


def rows_of(block, size):
    return pl.ds(pl.multiple_of(block * size, size), size)


SLICES = 2


def slice_of(block, size, part):
    share = size // SLICES
    return pl.ds(pl.multiple_of(block * size + part * share, share), share)


class TpGather:
    def __init__(self, team, ref, size, sends, recvs, part):
        self.team, self.ref, self.size, self.part = team, ref, size, part
        self.sends = lambda place: sends(place * SLICES + part)
        self.recvs = lambda place: recvs(place * SLICES + part)

    def copy(self, hop, arriving):
        bit, mask = hop
        team = self.team
        block = team.column(mask | ((1 << bit) if arriving else 0))
        part = self.ref.at[slice_of(block, self.size, self.part)]
        return pltpu.make_async_remote_copy(
            src_ref=part,
            dst_ref=part,
            send_sem=self.sends(team.place[hop]),
            recv_sem=self.recvs(team.place[hop]),
            device_id={"tp": flipped(team.t, bit)},
            device_id_type=MESH,
        )

    def begin(self):
        for bit in reversed(range(self.team.bits)):
            self.copy((bit, 0), False).start()

    def relay(self):
        for hop in self.team.hops:
            bit, mask = hop
            if bit:
                self.copy(hop, True).wait_recv()
                for lower in reversed(range(bit)):
                    self.copy((lower, mask | (1 << bit)), False).start()

    def arrive(self):
        for hop in self.team.hops:
            if hop[0] == 0:
                self.copy(hop, True).wait_recv()

    def drain(self):
        for hop in self.team.hops:
            self.copy(hop, False).wait_send()


def add_blocks(target, rows, other, width, experts):
    wide = target[rows, :width].astype(jnp.float32) + other[:, :width].astype(jnp.float32)
    target[rows, :width] = wide.astype(target.dtype)
    if target.shape[1] > width:
        both = target[rows, width:].astype(jnp.float32) + other[:, width:].astype(jnp.float32)
        target[rows, width:] = two_parts(both, experts)


def two_parts(both, experts):
    lane = lax.broadcasted_iota(jnp.int32, both.shape, 1)
    first = lane < experts
    full = both + jnp.where(
        first, pltpu.roll(both, LANES - experts, 1), pltpu.roll(both, experts, 1)
    )
    return parted(full, first, lane < 2 * experts)


def parted(full, first, second):
    high = full.astype(jnp.bfloat16)
    low = (full - high.astype(jnp.float32)).astype(jnp.bfloat16)
    zero = jnp.zeros_like(high)
    return jnp.where(first, high, jnp.where(second, low, zero))


class TpScatter:
    def __init__(self, team, ref, size, landing, sends, recvs, width, experts, part):
        share = size // SLICES
        self.team, self.ref, self.size, self.part = team, ref, size, part
        self.landing = lambda place: landing(place).at[pl.ds(part * share, share)]
        self.sends = lambda place: sends(place * SLICES + part)
        self.recvs = lambda place: recvs(place * SLICES + part)
        self.width, self.experts = width, experts

    def copy(self, hop):
        bit, mask = hop
        team = self.team
        block = team.column(mask | (1 << bit))
        return pltpu.make_async_remote_copy(
            src_ref=self.ref.at[slice_of(block, self.size, self.part)],
            dst_ref=self.landing(team.place[hop]),
            send_sem=self.sends(team.place[hop]),
            recv_sem=self.recvs(team.place[hop]),
            device_id={"tp": flipped(team.t, bit)},
            device_id_type=MESH,
        )

    def send(self, bit):
        for hop in self.team.hops:
            if hop[0] == bit:
                self.copy(hop).start()

    def add(self, bit):
        for hop in self.team.hops:
            if hop[0] == bit:
                self.copy(hop).wait_recv()
                add_blocks(
                    self.ref,
                    slice_of(self.team.column(hop[1]), self.size, self.part),
                    self.landing(self.team.place[hop]),
                    self.width,
                    self.experts,
                )

    def drain(self):
        for hop in self.team.hops:
            self.copy(hop).wait_send()


def gather_all(team, ref, size, sends, recvs):
    slices = [
        TpGather(team, ref, size, lambda p: sends.at[p], lambda p: recvs.at[p], part)
        for part in range(SLICES)
    ]
    for phase in ("begin", "relay", "arrive", "drain"):
        for one in slices:
            getattr(one, phase)()


def scatter_all(team, ref, size, landing, sends, recvs, width):
    slices = [
        TpScatter(
            team, ref, size, lambda p: landing.at[p], lambda p: sends.at[p], lambda p: recvs.at[p], width, 0, part
        )
        for part in range(SLICES)
    ]
    for one in slices:
        one.send(0)
    for bit in range(team.bits):
        for one in slices:
            one.add(bit)
            if bit + 1 < team.bits:
                one.send(bit + 1)
    return slices


def ring_copy(team, step, source, target, sends, recvs):
    ahead = lax.rem(team.s + team.sections + step, team.sections)
    return pltpu.make_async_remote_copy(
        src_ref=source,
        dst_ref=target,
        send_sem=sends.at[0],
        recv_sem=recvs.at[0],
        device_id={"section": ahead},
        device_id_type=MESH,
    )


def group_exchange(team, gathered, partial, landing, across, sems, size, width, experts, prepare, first, second, spare=None):
    ag_send, ag_recv, agz_send, agz_recv, rs_send, rs_recv, rsz_send, rsz_recv = sems
    count = team.fsdp

    def gather(i, part):
        return TpGather(
            team,
            gathered.at[team.row(i)],
            size,
            lambda place: ag_send.at[i, place],
            lambda place: ag_recv.at[i, place],
            part,
        )

    def scatter(i, part):
        return TpScatter(
            team,
            partial.at[team.row(i)],
            size,
            lambda place: landing.at[i, place],
            lambda place: rs_send.at[i, place],
            lambda place: rs_recv.at[i, place],
            width,
            experts,
            part,
        )

    parts = range(SLICES)
    share = size // SLICES

    def gather_across(i, part, arriving):
        source = team.row(i) if arriving else team.f
        block = gathered.at[source, slice_of(team.t, size, part)]
        return pltpu.make_async_remote_copy(
            src_ref=block,
            dst_ref=block,
            send_sem=agz_send.at[i, part],
            recv_sem=agz_recv.at[source, part],
            device_id={"fsdp": team.row(i)},
            device_id_type=MESH,
        )

    def scatter_across(i, part, arriving):
        source = team.row(i) if arriving else team.f
        return pltpu.make_async_remote_copy(
            src_ref=partial.at[team.row(i), slice_of(team.t, size, part)],
            dst_ref=across.at[source, pl.ds(part * share, share)],
            send_sem=rsz_send.at[i, part],
            recv_sem=rsz_recv.at[source, part],
            device_id={"fsdp": team.row(i)},
            device_id_type=MESH,
        )

    def relay_across(i):
        for part in parts:
            gather_across(i, part, True).wait_recv()
            gather(i, part).begin()

    for part in parts:
        gather(0, part).begin()
    for i in range(1, min(count, 3)):
        for part in parts:
            gather_across(i, part, False).start()
    for part in parts:
        gather(0, part).relay()
    for i in range(3, count):
        for part in parts:
            gather_across(i, part, False).start()
    prepare()
    if count > 1:
        relay_across(1)

    def step(i, carry):
        @pl.when(i < count)
        def _():
            for part in parts:
                gather(i, part).arrive()
            first(team.row(i))

        @pl.when(i + 2 < count)
        def _():
            relay_across(i + 2)

        for bit in range(team.bits):
            done = i - 1 - bit

            @pl.when((done >= min(bit, 1)) & (done < count))
            def _():
                for part in parts:
                    scatter(done, part).add(bit)

                    @pl.when(done > 0)
                    def _():
                        if bit + 1 < team.bits:
                            scatter(done, part).send(bit + 1)
                        else:
                            scatter_across(done, part, False).start()

        @pl.when(i + 1 < count)
        def _():
            for part in parts:
                gather(i + 1, part).relay()

        @pl.when(i < count)
        def _():
            second(team.row(i))
            for part in parts:
                scatter(i, part).send(0)

        if team.bits > 1:

            @pl.when(i == count)
            def _():
                for part in parts:
                    scatter(0, part).send(1)

        if spare is not None:

            @pl.when(i >= count)
            def _():
                spare(i - count)

        return carry

    lax.fori_loop(0, count + team.bits, step, 0)
    for bit in range(1, team.bits):
        for part in parts:
            scatter(0, part).add(bit)
            if bit + 1 < team.bits:
                scatter(0, part).send(bit + 1)
    if spare is not None:
        spare(team.bits)

    def finish(i, carry):
        for part in parts:
            gather_across(i, part, False).wait_send()
            scatter_across(i, part, False).wait_send()
        return carry

    def settle(i, carry):
        for part in parts:
            gather(i, part).drain()
            scatter(i, part).drain()
        return carry

    total = partial[team.f, rows_of(team.t, size)].astype(jnp.float32)
    for i in range(1, count):
        for part in parts:
            scatter_across(i, part, True).wait_recv()
        total = total + across[team.row(i)].astype(jnp.float32)
    lax.fori_loop(1, count, finish, 0)
    lax.fori_loop(0, count, settle, 0)
    return total[:, :width], (total[:, width:] if total.shape[1] > width else None)


def group_sems(team_sizes):
    _, fsdp, tp = team_sizes
    dma = pltpu.SemaphoreType.DMA
    return [
        dma((fsdp, SLICES * tp)), dma((fsdp, SLICES * tp)), dma((fsdp, SLICES)), dma((fsdp, SLICES)),
        dma((fsdp, SLICES * tp)), dma((fsdp, SLICES * tp)), dma((fsdp, SLICES)), dma((fsdp, SLICES)),
    ]


def share_parts(share, experts):
    lane = lax.broadcasted_iota(jnp.int32, share.shape, 1)
    high = share.astype(jnp.bfloat16)
    rest = share - high.astype(jnp.float32)
    middle = rest.astype(jnp.bfloat16)
    low = (rest - middle.astype(jnp.float32)).astype(jnp.bfloat16)
    zero = jnp.zeros_like(high)
    return jnp.where(
        lane < experts,
        high,
        jnp.where(lane < 2 * experts, middle, jnp.where(lane < 3 * experts, low, zero)),
    )


def chunks(length, body, size=1024):
    size = min(size, length)

    def step(c, carry):
        body(pl.multiple_of(c * size, size), size)
        return carry

    lax.fori_loop(0, length // size, step, 0)


def product(left, right):
    return jnp.dot(left, right, preferred_element_type=jnp.float32)


def product_turned(left, right):
    return lax.dot_general(
        left, right, (((1,), (1,)), ((), ())), preferred_element_type=jnp.float32
    )


def comm_params(number):
    return pltpu.CompilerParams(
        collective_id=number, has_side_effects=True, vmem_limit_bytes=VMEM_LIMIT
    )


def begin_layer(sizes, layer_in, gain, number):
    rows, width = layer_in.shape
    tp = sizes[2]

    def kernel(in_ref, gain_ref, out_ref, sends, recvs):
        team = Team(sizes)
        greet(team, False, 0)
        scaled, _, _ = norm_rows(in_ref[...].astype(jnp.float32), gain_ref[...])
        out_ref[rows_of(team.t, rows)] = scaled.astype(jnp.bfloat16)
        gather_all(team, out_ref, rows, sends, recvs)

    return pl.pallas_call(
        kernel,
        out_shape=jax.ShapeDtypeStruct((tp * rows, width), jnp.bfloat16),
        in_specs=[WHOLE_VMEM] * 2,
        out_specs=WHOLE_VMEM,
        scratch_shapes=[pltpu.SemaphoreType.DMA((SLICES * tp,)), pltpu.SemaphoreType.DMA((SLICES * tp,))],
        compiler_params=comm_params(number),
    )(layer_in, gain)


def moe_forward(sizes, partial_out, residual, chosen, weights, fresh, experts, number):
    router, gain_one, gain_two, gate_up, down, spread_map = weights
    sections, fsdp, tp = sizes
    rows, width = residual.shape
    band = tp * rows
    hidden = down.shape[0]
    copies = LANES // experts
    tail = fresh is not None
    bf16, f32 = jnp.bfloat16, jnp.float32
    shapes = [
        jax.ShapeDtypeStruct((fsdp, band, width), bf16),
        jax.ShapeDtypeStruct((fsdp, band, 2 * hidden), bf16),
        jax.ShapeDtypeStruct((fsdp, band, LANES), f32),
        jax.ShapeDtypeStruct((rows, width), f32),
        jax.ShapeDtypeStruct((rows, width), bf16),
    ]
    if tail:
        shapes += [
            jax.ShapeDtypeStruct((rows, width), bf16),
            jax.ShapeDtypeStruct((band, width), bf16),
        ]
    dma = pltpu.SemaphoreType.DMA
    scratch = [
        pltpu.VMEM((band, width), bf16),
        pltpu.VMEM((tp, rows, width), bf16),
        pltpu.VMEM((fsdp, band, width), bf16),
        pltpu.VMEM((fsdp, tp - 1, rows, width), bf16),
        pltpu.VMEM((fsdp, rows, width), bf16),
        pltpu.VMEM((band, hidden), bf16),
        pltpu.VMEM((band, LANES), bf16),
        pltpu.VMEM((rows, width), bf16),
        pltpu.VMEM((width, 2 * hidden), bf16),
        pltpu.VMEM((hidden, width), bf16),
        pltpu.VMEM((fsdp, band, width), bf16),
        pltpu.VMEM((fsdp, band, 2 * hidden), bf16),
        dma((SLICES * tp,)), dma((SLICES * tp,)), dma((SLICES * tp,)), dma((SLICES * tp,)), dma((1,)), dma((1,)),
        dma((2,)), dma((fsdp,)), dma((fsdp,)),
    ] + group_sems(sizes)
    own, out = WHOLE_VMEM, pl.BlockSpec(memory_space=pl.ANY)

    def kernel(*refs):
        part_ref, res_ref, chosen_ref, router_ref, one_ref, two_ref, both_hbm, down_hbm, map_ref = refs[:9]
        refs = refs[9:]
        if tail:
            fresh_ref, refs = refs[0], refs[1:]
        all_hbm, pre_hbm, share_ref, state_ref, result_ref = refs[:5]
        refs = refs[5:]
        if tail:
            next_ref, attn_ref = refs[:2]
            refs = refs[2:]
        sums, sums_in, partial, landing, across, weighted, parts, moved = refs[:8]
        both_ref, down_ref, all_ref, pre_ref = refs[8:12]
        tr_send, tr_recv, tg_send, tg_recv, sec_send, sec_recv, load_sem, all_sem, pre_sem = refs[12:21]
        sems = refs[21:]
        team = Team(sizes)
        loads = [
            pltpu.make_async_copy(both_hbm, both_ref, load_sem.at[0]),
            pltpu.make_async_copy(down_hbm, down_ref, load_sem.at[1]),
        ]
        for load in loads:
            load.start()

        def all_out(row):
            return pltpu.make_async_copy(all_ref.at[row], all_hbm.at[row], all_sem.at[row])

        def pre_out(row):
            return pltpu.make_async_copy(pre_ref.at[row], pre_hbm.at[row], pre_sem.at[row])

        def prepare():
            for load in loads:
                load.wait()

        sums[...] = part_ref[...]
        greet(team, True, 1 if tail else 0)
        reduce = scatter_all(team, sums, rows, sums_in, tr_send, tr_recv, width)
        state = res_ref[...].astype(f32) + branch_scale * sums[rows_of(team.t, rows)].astype(f32)
        state_ref[...] = state
        scaled, _, _ = norm_rows(state, two_ref[...])
        all_ref[team.f, rows_of(team.t, rows)] = scaled.astype(bf16)

        def first(row):
            all_out(row).start()
            logits = product(all_ref[row], router_ref[...])
            logits = jnp.where(chosen_ref[row].astype(f32) > 0.5, logits, masked_score)
            grown = jnp.exp(logits - jnp.max(logits, axis=-1, keepdims=True))
            total = jnp.sum(grown, axis=-1, keepdims=True) * (1.0 / copies)
            share = grown / total
            share_ref[row] = share
            parts[...] = share_parts(share, experts)

            def piece(start, size):
                here, there = pl.ds(start, size), pl.ds(pl.multiple_of(hidden + start, size), size)
                gate = product(all_ref[row], both_ref[:, here])
                up = product(all_ref[row], both_ref[:, there])
                pre_ref[row, :, here] = gate.astype(bf16)
                pre_ref[row, :, there] = up.astype(bf16)
                wide = product(parts[...], map_ref[:, here])
                weighted[:, here] = (wide * (gate * jax.nn.sigmoid(gate) * up)).astype(bf16)

            chunks(hidden, piece)
            pre_out(row).start()

        def second(row):
            def piece(start, size):
                here = pl.ds(start, size)
                partial[row, :, here] = product(weighted[...], down_ref[:, here]).astype(bf16)

            chunks(width, piece)

        total, _ = group_exchange(
            team, all_ref, partial, landing, across, sems, rows, width, experts, prepare, first, second
        )
        result_ref[...] = (state_ref[...] + branch_scale * total).astype(bf16)
        for one in reduce:
            one.drain()
        if tail:
            move = ring_copy(team, 1, result_ref, moved, sec_send, sec_recv)
            move.start()
            move.wait_recv()
            layer_in = jnp.where(team.s == 0, fresh_ref[...], moved[...])
            next_ref[...] = layer_in
            scaled, _, _ = norm_rows(layer_in.astype(f32), one_ref[...])
            attn_ref[rows_of(team.t, rows)] = scaled.astype(bf16)
            gather_all(team, attn_ref, rows, tg_send, tg_recv)
            move.wait_send()
        for row in range(fsdp):
            all_out(row).wait()
            pre_out(row).wait()

    args = [partial_out, residual, chosen, router, gain_one, gain_two, gate_up, down, spread_map]
    if tail:
        args.append(fresh)
    return pl.pallas_call(
        kernel,
        out_shape=shapes,
        in_specs=[own] * 6 + [out] * 2 + [own] * (len(args) - 8),
        out_specs=[out] * 2 + [own] * (len(shapes) - 2),
        scratch_shapes=scratch,
        compiler_params=comm_params(number),
        name="moe_forward",
    )(*args)


def moe_backward(sizes, upstream, state, share, pre, moe_in, weights, experts, sums, final, number):
    router, gain_two, gate_up, down, spread_map, pick_map = weights
    sections, fsdp, tp = sizes
    rows, width = upstream.shape
    band = tp * rows
    hidden = down.shape[0]
    bf16, f32 = jnp.bfloat16, jnp.float32
    leaving = bf16 if final else f32
    shapes = [
        jax.ShapeDtypeStruct((width, 2 * hidden), leaving),
        jax.ShapeDtypeStruct((hidden, width), f32),
        jax.ShapeDtypeStruct((rows, LANES), bf16),
        jax.ShapeDtypeStruct((1, width), f32),
        jax.ShapeDtypeStruct((rows, width), f32),
        jax.ShapeDtypeStruct((band, width), bf16),
    ]
    dma = pltpu.SemaphoreType.DMA
    wider = width + LANES
    both_units = team_units(tp)
    both_step = 2 * hidden // both_units
    loops = [both_step // chunk_size(both_step), width // chunk_size(width)]
    both_size, down_size = chunk_size(both_step), chunk_size(width)
    scratch = [
        pltpu.VMEM((fsdp, band, wider), bf16),
        pltpu.VMEM((fsdp, tp - 1, rows, wider), bf16),
        pltpu.VMEM((fsdp, rows, wider), bf16),
        pltpu.VMEM((band, LANES), bf16),
        pltpu.VMEM((band, LANES), f32),
        pltpu.VMEM((width, 2 * hidden), bf16),
        pltpu.VMEM((hidden, width), bf16),
        pltpu.VMEM((fsdp, band, 2 * hidden), bf16),
        pltpu.VMEM((fsdp, band, width), bf16),
        pltpu.VMEM((fsdp, band, 2 * hidden), bf16),
        pltpu.VMEM((fsdp, band, hidden), bf16),
        pltpu.VMEM((fsdp, band, width), bf16),
        pltpu.VMEM((width, 2 * hidden), f32),
        pltpu.VMEM((hidden, width), f32),
        pltpu.VMEM((width, 2 * hidden) if final else (16, LANES), bf16),
        dma((SLICES * tp,)), dma((SLICES * tp,)), dma((5,)), dma((fsdp,)), dma((2,)),
    ] + group_sems(sizes)
    own, out = WHOLE_VMEM, pl.BlockSpec(memory_space=pl.ANY)
    adding = sums is not None

    def kernel(*refs):
        up_ref, state_ref, share_ref, pre_hbm, router_ref, gain_ref, both_hbm, down_hbm, map_ref, pick_ref, in_hbm = refs[:11]
        refs = refs[11:]
        if adding:
            both_old, down_old = refs[:2]
            refs = refs[2:]
        both_out, down_out, logit_ref, gain_out, state_out, attn_ref = refs[:6]
        partial, landing, across, parts, share_sum, both_ref, down_ref, pre_ref, all_ref, grad_ref, weighted_ref = refs[6:17]
        in_ref, both_sum, down_sum, both_low, tg_send, tg_recv, load_sem, pre_sem, out_sem = refs[17:26]
        sems = refs[26:]
        team = Team(sizes)
        loads = [
            pltpu.make_async_copy(down_hbm, down_ref, load_sem.at[0]),
            pltpu.make_async_copy(both_hbm, both_ref, load_sem.at[1]),
        ]
        later = [pltpu.make_async_copy(in_hbm, in_ref, load_sem.at[2])]
        if adding:
            later += [
                pltpu.make_async_copy(both_old, both_sum, load_sem.at[3]),
                pltpu.make_async_copy(down_old, down_sum, load_sem.at[4]),
            ]
        outs = [
            pltpu.make_async_copy(both_low if final else both_sum, both_out, out_sem.at[0]),
            pltpu.make_async_copy(down_sum, down_out, out_sem.at[1]),
        ]

        def pre_in(row):
            return pltpu.make_async_copy(pre_hbm.at[row], pre_ref.at[row], pre_sem.at[row])

        loads[0].start()
        for i in range(fsdp):
            pre_in(i).start()
        loads[1].start()
        for load in later:
            load.start()

        def prepare():
            for load in loads:
                load.wait()
            for i in range(fsdp):
                pre_in(i).wait()

        def spare(unit):
            @pl.when(unit == 0)
            def _():
                for load in later:
                    load.wait()

            if isinstance(unit, int):
                left, right, total, size = weighted_ref, all_ref, down_sum, down_size
                start, count = 0, loops[1]
            else:
                left, right, total, size = in_ref, grad_ref, both_sum, both_size
                start, count = unit * both_step, loops[0]

            def turn(c, carry):
                here = pl.ds(pl.multiple_of(start + c * size, size), size)
                made = lax.dot_general(
                    left[...].reshape(fsdp * band, left.shape[2]),
                    right[:, :, here].reshape(fsdp * band, size),
                    (((0,), (0,)), ((), ())),
                    preferred_element_type=f32,
                )
                if adding:
                    made = made + total[:, here]
                if final and total is both_sum:
                    both_low[:, here] = made.astype(bf16)
                else:
                    total[:, here] = made
                return carry

            lax.fori_loop(0, count, turn, 0)
            if isinstance(unit, int):
                for done in outs:
                    done.start()

        greet(team, True, 0)
        all_ref[team.f, rows_of(team.t, rows)] = (branch_scale * up_ref[...]).astype(bf16)

        def first(row):
            parts[...] = share_parts(share_ref[row], experts)
            share_sum[...] = jnp.zeros_like(share_sum)

            def piece(start, size):
                here, there = pl.ds(start, size), pl.ds(pl.multiple_of(hidden + start, size), size)
                hidden_grad = product_turned(all_ref[row], down_ref[here])
                gate = pre_ref[row, :, here].astype(f32)
                up = pre_ref[row, :, there].astype(f32)
                wide = product(parts[...], map_ref[:, here])
                sigmoid_gate = jax.nn.sigmoid(gate)
                swish = gate * sigmoid_gate
                value = swish * up
                weighted_ref[row, :, here] = (wide * value).astype(bf16)
                both = hidden_grad * value
                high = both.astype(bf16)
                low = (both - high.astype(f32)).astype(bf16)
                share_sum[...] += product(high, pick_ref[here]) + product(low, pick_ref[here])
                scaled = wide * hidden_grad
                grad_ref[row, :, here] = (
                    scaled * up * sigmoid_gate * (1.0 + gate * (1.0 - sigmoid_gate))
                ).astype(bf16)
                grad_ref[row, :, there] = (scaled * swish).astype(bf16)

            chunks(hidden, piece)

        def second(row):
            def piece(start, size):
                here = pl.ds(start, size)
                partial[row, :, here] = product_turned(grad_ref[row], both_ref[here]).astype(bf16)

            chunks(width, piece)
            lane = lax.broadcasted_iota(jnp.int32, (band, LANES), 1)
            partial[row, :, width:] = parted(share_sum[...], lane < experts, lane < 2 * experts)

        total, extra = group_exchange(
            team, all_ref, partial, landing, across, sems, rows, width, experts, prepare, first, second, spare
        )
        lane = lax.broadcasted_iota(jnp.int32, (rows, LANES), 1)
        valid = lane < experts
        share_grad = extra + pltpu.roll(extra, LANES - experts, 1)
        own_share = jnp.where(valid, share_ref[team.f, rows_of(team.t, rows)], 0.0)
        inner = jnp.sum(own_share * share_grad, axis=-1, keepdims=True)
        logit_grad = (own_share * (share_grad - inner)).astype(bf16)
        logit_ref[...] = logit_grad
        norm_grad = total + product_turned(logit_grad, router_ref[...])
        _, normed, inverse = norm_rows(state_ref[...], gain_ref[...])
        back, gain_grad = norm_back(norm_grad, normed, inverse, gain_ref[...])
        gain_out[...] = gain_grad
        state_grad = up_ref[...] + back
        state_out[...] = state_grad
        attn_ref[rows_of(team.t, rows)] = (branch_scale * state_grad).astype(bf16)
        gather_all(team, attn_ref, rows, tg_send, tg_recv)
        for done in outs:
            done.wait()

    args = [upstream, state, share, pre, router, gain_two, gate_up, down, spread_map, pick_map, moe_in]
    if adding:
        args += list(sums)
    return pl.pallas_call(
        kernel,
        out_shape=shapes,
        in_specs=[own] * 3 + [out] + [own] * 2 + [out] * 2 + [own] * 2 + [out] * (len(args) - 10),
        out_specs=[out] * 2 + [own] * 4,
        scratch_shapes=scratch,
        compiler_params=comm_params(number),
        name="moe_backward",
    )(*args)


def team_units(tp):
    return tp.bit_length() - 1


def chunk_size(length, most=512):
    return min(length, most)


def end_layer(sizes, partial_in, layer_in, state_grad, gain, number):
    tp = sizes[2]
    rows, width = layer_in.shape
    bf16, f32 = jnp.bfloat16, jnp.float32
    dma = pltpu.SemaphoreType.DMA

    def kernel(
        part_ref, in_ref, grad_ref, gain_ref, out_ref, gain_out, arrived_ref,
        sums, sums_in, leaving, tr_send, tr_recv, sec_send, sec_recv,
    ):
        team = Team(sizes)
        sums[...] = part_ref[...]
        greet(team, False, -1)
        reduce = scatter_all(team, sums, rows, sums_in, tr_send, tr_recv, width)
        norm_grad = sums[rows_of(team.t, rows)].astype(f32)
        _, normed, inverse = norm_rows(in_ref[...].astype(f32), gain_ref[...])
        back, gain_grad = norm_back(norm_grad, normed, inverse, gain_ref[...])
        gain_out[...] = gain_grad
        result = grad_ref[...] + back
        out_ref[...] = result
        leaving[...] = result.astype(bf16)
        move = ring_copy(team, -1, leaving, arrived_ref, sec_send, sec_recv)
        move.start()
        for one in reduce:
            one.drain()
        move.wait()

    return pl.pallas_call(
        kernel,
        out_shape=[
            jax.ShapeDtypeStruct((rows, width), f32),
            jax.ShapeDtypeStruct((1, width), f32),
            jax.ShapeDtypeStruct((rows, width), bf16),
        ],
        in_specs=[WHOLE_VMEM] * 4,
        out_specs=[WHOLE_VMEM] * 3,
        scratch_shapes=[
            pltpu.VMEM((tp * rows, width), bf16),
            pltpu.VMEM((tp, rows, width), bf16),
            pltpu.VMEM((rows, width), bf16),
            dma((SLICES * tp,)), dma((SLICES * tp,)), dma((1,)), dma((1,)),
        ],
        compiler_params=comm_params(number),
        name="end_layer",
    )(partial_in, layer_in, state_grad, gain)


def plain_copy(array, steps):
    rows, width = array.shape

    def kernel(in_ref, out_ref):
        out_ref[...] = in_ref[...]

    block = pl.BlockSpec((rows // steps, width), lambda i: (i, 0))
    return pl.pallas_call(
        kernel,
        grid=(steps,),
        out_shape=jax.ShapeDtypeStruct(array.shape, array.dtype),
        in_specs=[block],
        out_specs=block,
        name="plain_copy",
    )(array)


def order_map(inputs, outputs, count, part, turned):
    across = count * part
    source = lax.broadcasted_iota(jnp.int32, (inputs, outputs), 1 if turned else 0)
    target = lax.broadcasted_iota(jnp.int32, (inputs, outputs), 0 if turned else 1)
    e, rest = lax.div(source, across), lax.rem(source, across)
    f, h = lax.div(rest, part), lax.rem(rest, part)
    return (f * LANES + e * part + h == target).astype(jnp.bfloat16)


def block_steps(blocks):
    for steps in (2, 1):
        if blocks % steps == 0:
            return steps


def outgoing_experts(w_gate, w_up, count):
    experts, depth, hidden = w_gate.shape
    part = hidden // count
    bunch = LANES // part
    across = bunch * hidden
    steps = block_steps(experts // bunch)
    each = experts // bunch // steps

    def kernel(gate_ref, up_ref, out_ref, table):
        @pl.when((pl.program_id(0) == 0) & (pl.program_id(1) == 0))
        def _():
            table[...] = order_map(across, count * LANES, count, part, False)

        def move(ref):
            for b in range(each):
                lanes = jnp.concatenate([ref[b * bunch + e] for e in range(bunch)], axis=1)
                moved = product(lanes, table[...]).astype(jnp.bfloat16)
                for f in range(count):
                    out_ref[f, :, b * LANES : (b + 1) * LANES] = moved[:, f * LANES : (f + 1) * LANES]

        @pl.when(pl.program_id(0) == 0)
        def _():
            move(gate_ref)

        @pl.when(pl.program_id(0) == 1)
        def _():
            move(up_ref)

    block = (each * bunch, depth, hidden)
    return pl.pallas_call(
        kernel,
        grid=(2, steps),
        out_shape=jax.ShapeDtypeStruct((count, depth, 2 * steps * each * LANES), jnp.bfloat16),
        in_specs=[
            pl.BlockSpec(block, lambda w, b: (jnp.where(w == 0, b, steps - 1), 0, 0)),
            pl.BlockSpec(block, lambda w, b: (jnp.where(w == 1, b, 0), 0, 0)),
        ],
        out_specs=pl.BlockSpec((count, depth, each * LANES), lambda w, b: (0, 0, w * steps + b)),
        scratch_shapes=[pltpu.VMEM((across, count * LANES), jnp.bfloat16)],
        compiler_params=pltpu.CompilerParams(vmem_limit_bytes=VMEM_LIMIT),
        name="outgoing_experts",
    )(w_gate, w_up)


def incoming_experts(both, experts, hidden):
    count, depth, width = both.shape
    part = hidden // count
    bunch = LANES // part
    across = bunch * hidden
    steps = block_steps(experts // bunch)
    each = experts // bunch // steps

    def kernel(in_ref, gate_ref, up_ref, table):
        @pl.when((pl.program_id(0) == 0) & (pl.program_id(1) == 0))
        def _():
            table[...] = order_map(count * LANES, across, count, part, True)

        def store(ref):
            for b in range(each):
                lanes = jnp.concatenate(
                    [in_ref[f, :, b * LANES : (b + 1) * LANES] for f in range(count)], axis=1
                )
                moved = product(lanes, table[...])
                for e in range(bunch):
                    ref[b * bunch + e] = moved[:, e * hidden : (e + 1) * hidden]

        @pl.when(pl.program_id(0) == 0)
        def _():
            store(gate_ref)

        @pl.when(pl.program_id(0) == 1)
        def _():
            store(up_ref)

    shape = jax.ShapeDtypeStruct((experts, depth, hidden), jnp.float32)
    block = (each * bunch, depth, hidden)
    return pl.pallas_call(
        kernel,
        grid=(2, steps),
        out_shape=[shape, shape],
        in_specs=[pl.BlockSpec((count, depth, each * LANES), lambda w, b: (0, 0, w * steps + b))],
        out_specs=[
            pl.BlockSpec(block, lambda w, b: (jnp.where(w == 0, b, steps - 1), 0, 0)),
            pl.BlockSpec(block, lambda w, b: (jnp.where(w == 1, b, 0), 0, 0)),
        ],
        scratch_shapes=[pltpu.VMEM((count * LANES, across), jnp.bfloat16)],
        compiler_params=pltpu.CompilerParams(vmem_limit_bytes=VMEM_LIMIT),
        name="incoming_experts",
    )(both)


def line_barrier(team, tp):
    barrier = pltpu.get_barrier_semaphore()
    count = 0
    for i in range(1, team.fsdp):
        pl.semaphore_signal(
            barrier,
            inc=1,
            device_id={"fsdp": lax.rem(team.f + i, team.fsdp)},
            device_id_type=MESH,
        )
        count += 1
    if tp:
        for bit in range(team.bits):
            pl.semaphore_signal(
                barrier, inc=1, device_id={"tp": flipped(team.t, bit)}, device_id_type=MESH
            )
            count += 1
    pl.semaphore_wait(barrier, count)


def gather_weights(sizes, matrix, small, number):
    fsdp = sizes[1]
    depth, width = matrix.shape
    dma = pltpu.SemaphoreType.DMA

    def kernel(matrix_ref, small_ref, all_ref, few_ref, held, *sems):
        up_send, up_recv, down_send, down_recv, few_send, few_recv, local, out_sem = sems
        team = Team(sizes)
        f = team.f
        mine = pltpu.make_async_copy(matrix_ref, held.at[f], local.at[0])
        mine.start()
        few_ref[f] = small_ref[...]
        line_barrier(team, False)

        def few(i, arriving):
            other = lax.rem(f + (fsdp - i if arriving else i), fsdp)
            part = few_ref.at[other if arriving else f]
            return pltpu.make_async_remote_copy(
                src_ref=part,
                dst_ref=part,
                send_sem=few_send.at[i],
                recv_sem=few_recv.at[i],
                device_id={"fsdp": other},
                device_id_type=MESH,
            )

        for i in range(1, fsdp):
            few(i, False).start()
        mine.wait()

        def hand(block, step):
            sends, recvs = (up_send, up_recv) if step > 0 else (down_send, down_recv)
            return pltpu.make_async_remote_copy(
                src_ref=held.at[block],
                dst_ref=held.at[block],
                send_sem=sends.at[block],
                recv_sem=recvs.at[block],
                device_id={"fsdp": lax.rem(f + step + fsdp, fsdp)},
                device_id_type=MESH,
            )

        def out(block):
            return pltpu.make_async_copy(held.at[block], all_ref.at[block], out_sem.at[block])

        @pl.when(f < fsdp - 1)
        def _():
            hand(f, 1).start()

        @pl.when(f > 0)
        def _():
            hand(f, -1).start()

        out(f).start()

        def step(i, carry):
            below, above = f - i, f + i

            @pl.when(below >= 0)
            def _():
                hand(below, 1).wait_recv()

                @pl.when(f < fsdp - 1)
                def _():
                    hand(below, 1).start()

                out(below).start()

            @pl.when(above < fsdp)
            def _():
                hand(above, -1).wait_recv()

                @pl.when(f > 0)
                def _():
                    hand(above, -1).start()

                out(above).start()

            return carry

        lax.fori_loop(1, fsdp, step, 0)

        def finish(g, carry):
            @pl.when((g <= f) & (f < fsdp - 1))
            def _():
                hand(g, 1).wait_send()

            @pl.when((g >= f) & (f > 0))
            def _():
                hand(g, -1).wait_send()

            out(g).wait()
            return carry

        lax.fori_loop(0, fsdp, finish, 0)
        for i in range(1, fsdp):
            few(i, True).wait_recv()
            few(i, False).wait_send()

    anywhere = pl.BlockSpec(memory_space=pl.ANY)
    return pl.pallas_call(
        kernel,
        out_shape=[
            jax.ShapeDtypeStruct((fsdp, depth, width), matrix.dtype),
            jax.ShapeDtypeStruct((fsdp,) + small.shape, small.dtype),
        ],
        in_specs=[anywhere, WHOLE_VMEM],
        out_specs=[anywhere, WHOLE_VMEM],
        scratch_shapes=[pltpu.VMEM((fsdp, depth, width), matrix.dtype)]
        + [dma((fsdp,)) for _ in range(6)]
        + [dma((1,)), dma((fsdp,))],
        compiler_params=comm_params(number),
        name="gather_weights",
    )(matrix, small)


def reduce_weights(sizes, matrix, small, number):
    tp, fsdp = sizes[2], sizes[1]
    _, depth, width = matrix.shape
    count_rows = small.shape[0]
    portion = small.shape[1] // fsdp
    bits = tp.bit_length() - 1
    bf16, f32 = jnp.bfloat16, jnp.float32
    dma = pltpu.SemaphoreType.DMA

    def kernel(matrix_ref, small_ref, sum_ref, few_ref, up, down, up_in, down_in, few_sum, few_tp, few_cut, few_in, *sems):
        up_send, up_recv, down_send, down_recv, tp_send, tp_recv, few_send, few_recv = sems
        team = Team(sizes)
        f = team.f
        line_barrier(team, True)

        def pass_on(g, step):
            sends, recvs = (up_send, up_recv) if step > 0 else (down_send, down_recv)
            return pltpu.make_async_remote_copy(
                src_ref=(up if step > 0 else down).at[g],
                dst_ref=(up_in if step > 0 else down_in).at[g],
                send_sem=sends.at[g],
                recv_sem=recvs.at[g],
                device_id={"fsdp": lax.rem(f + step + fsdp, fsdp)},
                device_id_type=MESH,
            )

        def tp_copy(bit):
            return pltpu.make_async_remote_copy(
                src_ref=few_sum.at[bit],
                dst_ref=few_tp.at[bit],
                send_sem=tp_send.at[bit],
                recv_sem=tp_recv.at[bit],
                device_id={"tp": flipped(team.t, bit)},
                device_id_type=MESH,
            )

        few_sum[0] = small_ref[...]

        def step(i, carry):
            high, low = fsdp - 1 - i, i

            @pl.when(high > f)
            def _():
                @pl.when(f == 0)
                def _():
                    up[high] = matrix_ref[high]

                @pl.when(f > 0)
                def _():
                    pass_on(high, 1).wait_recv()
                    up[high] = (matrix_ref[high].astype(f32) + up_in[high].astype(f32)).astype(bf16)

                pass_on(high, 1).start()

            @pl.when(low < f)
            def _():
                @pl.when(f == fsdp - 1)
                def _():
                    down[low] = matrix_ref[low]

                @pl.when(f < fsdp - 1)
                def _():
                    pass_on(low, -1).wait_recv()
                    down[low] = (matrix_ref[low].astype(f32) + down_in[low].astype(f32)).astype(bf16)

                pass_on(low, -1).start()

            return carry

        lax.fori_loop(0, fsdp - 1, step, 0)
        for bit in range(bits):
            tp_copy(bit).start()
            tp_copy(bit).wait_recv()
            few_sum[bit + 1] = few_sum[bit] + few_tp[bit]
        for g in range(fsdp):
            few_cut[g] = few_sum[bits, :, g * portion : (g + 1) * portion]

        def few(i, arriving):
            other = lax.rem(f + (fsdp - i if arriving else i), fsdp)
            return pltpu.make_async_remote_copy(
                src_ref=few_cut.at[other],
                dst_ref=few_in.at[i],
                send_sem=few_send.at[i],
                recv_sem=few_recv.at[i],
                device_id={"fsdp": other},
                device_id_type=MESH,
            )

        for i in range(1, fsdp):
            few(i, False).start()
        sum_ref[...] = matrix_ref[f].astype(f32)

        @pl.when(f > 0)
        def _():
            pass_on(f, 1).wait_recv()
            sum_ref[...] += up_in[f].astype(f32)

        @pl.when(f < fsdp - 1)
        def _():
            pass_on(f, -1).wait_recv()
            sum_ref[...] += down_in[f].astype(f32)

        total = few_cut[f]
        for i in range(1, fsdp):
            few(i, True).wait_recv()
            total = total + few_in[i]
        few_ref[...] = total

        def finish(g, carry):
            @pl.when(g > f)
            def _():
                pass_on(g, 1).wait_send()

            @pl.when(g < f)
            def _():
                pass_on(g, -1).wait_send()

            return carry

        lax.fori_loop(0, fsdp, finish, 0)
        for i in range(1, fsdp):
            few(i, False).wait_send()
        for bit in range(bits):
            tp_copy(bit).wait_send()

    return pl.pallas_call(
        kernel,
        out_shape=[
            jax.ShapeDtypeStruct((depth, width), f32),
            jax.ShapeDtypeStruct((count_rows, portion), f32),
        ],
        in_specs=[WHOLE_VMEM] * 2,
        out_specs=[WHOLE_VMEM] * 2,
        scratch_shapes=[pltpu.VMEM((fsdp, depth, width), bf16) for _ in range(4)]
        + [
            pltpu.VMEM((bits + 1,) + small.shape, f32),
            pltpu.VMEM((bits,) + small.shape, f32),
            pltpu.VMEM((fsdp, count_rows, portion), f32),
            pltpu.VMEM((fsdp, count_rows, portion), f32),
        ]
        + [dma((fsdp,)) for _ in range(4)]
        + [dma((tp,)), dma((tp,)), dma((fsdp,)), dma((fsdp,))],
        compiler_params=comm_params(number),
        name="reduce_weights",
    )(matrix, small)


def exchange(blocks):
    return lax.all_to_all(blocks, "fsdp", split_axis=0, concat_axis=0, tiled=True)


def attention_forward(attn_in, segment, w_qkv, w_output):
    query_width = w_output.shape[0]
    key_width = (w_qkv.shape[1] - query_width) // 2
    key_value_heads = key_width // HEAD_SIZE
    count_of_tokens = attn_in.shape[0]
    permitted_mask = allowed_pairs(segment)
    cosine, sine = rope_tables(permitted_mask)
    qkv = jnp.dot(attn_in, w_qkv, preferred_element_type=jnp.float32)
    turned = rotate(
        qkv[:, : query_width + key_width].reshape(count_of_tokens, -1, HEAD_SIZE), cosine, sine
    ).astype(jnp.bfloat16)
    query_rows = turned[:, : query_width // HEAD_SIZE].reshape(
        count_of_tokens, key_value_heads, QUERY_HEADS // KEY_VALUE_HEADS, HEAD_SIZE
    )
    key_matrix = turned[:, query_width // HEAD_SIZE :]
    value_matrix = (
        qkv[:, query_width + key_width :]
        .astype(jnp.bfloat16)
        .reshape(count_of_tokens, key_value_heads, HEAD_SIZE)
    )
    attended, log_sum_exp = attend(query_rows, key_matrix, value_matrix, permitted_mask)
    mixed_heads = attended.reshape(count_of_tokens, -1)
    partial = jnp.dot(mixed_heads, w_output, preferred_element_type=jnp.float32)
    kept = (
        query_rows, key_matrix, value_matrix, attended, log_sum_exp, cosine, sine, permitted_mask
    )
    return (partial.astype(jnp.bfloat16), kept)


def attention_gradients(attn_grad, kept, w_qkv, w_output):
    (
        query_rows, key_matrix, value_matrix, attended, log_sum_exp, cosine, sine, permitted_mask
    ) = kept
    count_of_tokens = attn_grad.shape[0]
    key_value_heads = key_matrix.shape[1]
    mixed_heads = attended.reshape(count_of_tokens, -1)
    head_gradient = jnp.dot(attn_grad, w_output.T, preferred_element_type=jnp.float32).astype(
        jnp.bfloat16
    )
    query_gradient, key_gradient, value_gradient = attention_backward(
        query_rows,
        key_matrix,
        value_matrix,
        permitted_mask,
        log_sum_exp,
        head_gradient.reshape(
            count_of_tokens, key_value_heads, QUERY_HEADS // KEY_VALUE_HEADS, HEAD_SIZE
        ),
    )
    turned = jnp.concatenate(
        [query_gradient.reshape(count_of_tokens, -1, HEAD_SIZE), key_gradient], axis=1
    )
    turned = rotate_back(turned, cosine, sine).reshape(count_of_tokens, -1)
    qkv_grad = jnp.concatenate(
        [turned, value_gradient.reshape(count_of_tokens, -1)], axis=1
    ).astype(jnp.bfloat16)
    input_part = lax.dot_general(
        qkv_grad, w_qkv, (((1,), (1,)), ((), ())), preferred_element_type=jnp.float32
    )
    return (input_part.astype(jnp.bfloat16), qkv_grad, mixed_heads)


def summed_product(pairs):
    left = jnp.concatenate([pair[0] for pair in pairs], axis=0)
    right = jnp.concatenate([pair[1] for pair in pairs], axis=0)
    return lax.dot_general(
        left, right, (((0,), (0,)), ((), ())), preferred_element_type=jnp.float32
    )


def per_device(
    sizes,
    inputs,
    segment_ids,
    routes,
    w_query,
    key_weight,
    value_weight,
    w_output,
    w_router,
    gain_attn,
    gain_moe,
    w_gate,
    w_up,
    w_down,
    out_grad,
):
    section_count, fsdp_count, tp_count = sizes
    section_index = lax.axis_index("section")
    micro_count, local_rows, model_width = inputs.shape
    depth = w_query.shape[1]
    expert_count = w_router.shape[2]
    hidden_units = w_gate.shape[3]
    own_units = hidden_units // fsdp_count
    hidden = expert_count * own_units
    copies = LANES // expert_count
    query_width = w_query.shape[2]
    key_width = key_weight.shape[2]
    qkv_width = query_width + 2 * key_width
    flat_output = w_output[0].reshape(depth, -1)
    matrix = jnp.concatenate(
        [w_query[0], key_weight[0], value_weight[0], flat_output], axis=1
    )
    few = jnp.concatenate(
        [w_router[0].T, gain_attn.astype(jnp.bfloat16), gain_moe.astype(jnp.bfloat16)], axis=0
    )
    few_rows = -(-few.shape[0] // 16) * 16
    few = jnp.pad(few, ((0, few_rows - few.shape[0]), (0, 0)))
    expert_ids = jnp.arange(expert_count, dtype=jnp.int32)
    chosen_rows = jnp.any(routes[0][..., None] == expert_ids, axis=2).astype(jnp.bfloat16)
    chosen_shape = chosen_rows.shape
    few = jnp.concatenate([few, chosen_rows.reshape(-1, few.shape[1])], axis=0)
    both_out = outgoing_experts(w_gate[0], w_up[0], fsdp_count)
    matrix, few = gather_weights(sizes, matrix, few, 5)
    matrix, few, both_out = lax.optimization_barrier((matrix, few, both_out))
    gate_up = exchange(both_out).reshape(model_width, 2 * hidden)
    matrix = matrix.reshape(model_width, -1)
    chosen_rows = few[:, few_rows:].reshape((fsdp_count,) + chosen_shape)
    few = few[:, :few_rows].transpose(1, 0, 2).reshape(few_rows, model_width)
    w_qkv = matrix[:, :qkv_width]
    out_full = matrix[:, qkv_width:].reshape(-1, model_width)
    router = jnp.tile(few[:expert_count].T, (1, copies))
    gain_one = few[expert_count].astype(jnp.float32)[None]
    gain_two = few[expert_count + 1].astype(jnp.float32)[None]
    down = w_down[0].reshape(hidden, model_width)
    lane = jnp.arange(LANES, dtype=jnp.int32)
    owner = jnp.arange(hidden, dtype=jnp.int32) // own_units
    match = (lane % expert_count)[:, None] == owner[None, :]
    spread_map = (match & (lane < 3 * expert_count)[:, None]).astype(jnp.bfloat16)
    pick_map = (match & (lane < 2 * expert_count)[:, None]).astype(jnp.bfloat16).T
    chosen_rows = jnp.tile(chosen_rows, (1, 1, 1, copies))
    segment_rows = segment_ids[:, 0, :]
    tick_count = micro_count + section_count - 1
    outputs = jnp.zeros((micro_count, local_rows, model_width), jnp.bfloat16)
    history = []
    layer_in = jnp.where(section_index == 0, inputs[0], jnp.zeros_like(inputs[0]))
    attn_in = begin_layer(sizes, layer_in, gain_one, 0)
    for tick_step in range(tick_count):
        mb_index = tick_step - section_index
        active = (mb_index >= 0) & (mb_index < micro_count)
        mb_pick = jnp.clip(mb_index, 0, micro_count - 1)
        segment = lax.dynamic_index_in_dim(segment_rows, mb_pick, 0, keepdims=False)
        chosen = lax.dynamic_index_in_dim(chosen_rows, mb_pick, 1, keepdims=False)
        partial, kept = attention_forward(attn_in, segment, w_qkv, out_full)
        last = tick_step == tick_count - 1
        fresh = None if last else inputs[min(tick_step + 1, micro_count - 1)]
        weights = (router, gain_one, gain_two, gate_up, down, spread_map)
        made = moe_forward(
            sizes, partial, layer_in, chosen, weights, fresh, expert_count, 2 if last else 1
        )
        moe_in, pre, share, state, result = made[:5]
        history.append((attn_in, layer_in, kept, moe_in, pre, share, state))
        outputs = jnp.where(
            active, lax.dynamic_update_index_in_dim(outputs, result, mb_pick, 0), outputs
        )
        if not last:
            layer_in, attn_in = made[5:]
    input_grads = jnp.zeros((micro_count, local_rows, model_width), jnp.float32)
    gain_sums = None
    all_terms = []
    arrived = None
    place = (lax.axis_index("fsdp"), lax.axis_index("tp") * local_rows, 0)
    for tick_step in range(tick_count):
        mb_index = micro_count + section_count - 2 - tick_step - section_index
        active = (mb_index >= 0) & (mb_index < micro_count)
        mb_pick = jnp.clip(mb_index, 0, micro_count - 1)
        upstream = out_grad[max(micro_count - 1 - tick_step, 0)].astype(jnp.float32)
        if arrived is None:
            arrived = jnp.zeros_like(upstream)
        upstream = jnp.where(
            section_index == section_count - 1, upstream, arrived.astype(jnp.float32)
        )
        upstream = jnp.where(active, upstream, jnp.zeros_like(upstream))
        attn_in, layer_in, kept, moe_in, pre, share, state = history[tick_count - 1 - tick_step]
        last = tick_step == tick_count - 1
        both_sum, down_sum, logit_grad, gain_two_part, state_grad, attn_grad = moe_backward(
            sizes,
            upstream,
            state,
            share,
            pre,
            moe_in,
            (router, gain_two, gate_up, down, spread_map, pick_map),
            expert_count,
            None if tick_step == 0 else (both_sum, down_sum),
            last,
            7 if tick_step == 0 else 8 if last else 3,
        )
        if last:
            both_sum = exchange(both_sum.reshape(fsdp_count, depth, 2 * hidden))
        input_part, qkv_grad, mixed_heads = attention_gradients(attn_grad, kept, w_qkv, out_full)
        grad_out, gain_one_part, arrived = end_layer(
            sizes, input_part, layer_in, state_grad, gain_one, 4
        )
        input_grads = jnp.where(
            active, lax.dynamic_update_index_in_dim(input_grads, grad_out, mb_pick, 0), input_grads
        )
        gains = (gain_one_part, gain_two_part)
        gain_sums = gains if gain_sums is None else tuple(a + b for a, b in zip(gain_sums, gains))
        own_rows = lax.dynamic_slice(moe_in, place, (1, local_rows, model_width))[0]
        all_terms.append(
            (
                active,
                (
                    (attn_in, qkv_grad),
                    (mixed_heads, attn_grad),
                    (logit_grad[:, :expert_count], own_rows),
                ),
            )
        )
    chosen_terms = []
    for first in range(micro_count):
        picked = all_terms[first][1]
        for active, terms in all_terms[first + micro_count :: micro_count]:
            picked = jax.tree.map(lambda a, b: jnp.where(active, b, a), picked, terms)
        chosen_terms.append(picked)
    qkv_pairs, output_pairs, router_pairs = zip(*chosen_terms)
    gate_shard, up_shard = incoming_experts(both_sum, expert_count, hidden_units)
    down_shard = down_sum.reshape(expert_count, own_units, model_width)
    small = jnp.concatenate([summed_product(router_pairs)] + list(gain_sums), axis=0)
    small = jnp.pad(small, ((0, few_rows - small.shape[0]), (0, 0)))
    matrix_grad = jnp.concatenate(
        [summed_product(qkv_pairs), summed_product(output_pairs).reshape(model_width, -1)], axis=1
    ).astype(jnp.bfloat16)
    down_sum, matrix_grad = lax.optimization_barrier((plain_copy(down_sum, 4), matrix_grad))
    matrix_grad, few_grad = reduce_weights(
        sizes, matrix_grad.reshape(fsdp_count, depth, -1), small, 6
    )
    shard_sums = (
        matrix_grad[:, :query_width],
        matrix_grad[:, query_width : query_width + key_width],
        matrix_grad[:, query_width + key_width : qkv_width],
        matrix_grad[:, qkv_width:].reshape(-1, model_width),
        few_grad[:expert_count].T,
        few_grad[expert_count],
        few_grad[expert_count + 1],
        gate_shard,
        up_shard,
        down_shard,
    )
    return (outputs[None], input_grads[None]) + tuple((part[None] for part in shard_sums))


def solution(mesh):
    in_specs = (
        P(None, ("fsdp", "tp"), None),
        P(None, "fsdp", None),
        P("section", None, "fsdp", None),
        P("section", "fsdp", "tp"),
        P("section", "fsdp", "tp"),
        P("section", "fsdp", "tp"),
        P("section", ("tp", "fsdp"), None),
        P("section", "fsdp", None),
        P("section", "fsdp"),
        P("section", "fsdp"),
        P("section", None, "fsdp", "tp"),
        P("section", None, "fsdp", "tp"),
        P("section", None, ("tp", "fsdp"), None),
        P(None, ("fsdp", "tp"), None),
    )
    out_specs = (
        P("section", None, ("fsdp", "tp"), None),
        P("section", None, ("fsdp", "tp"), None),
        P("section", "fsdp", "tp"),
        P("section", "fsdp", "tp"),
        P("section", "fsdp", "tp"),
        P("section", ("tp", "fsdp"), None),
        P("section", "fsdp", None),
        P("section", "fsdp"),
        P("section", "fsdp"),
        P("section", None, "fsdp", "tp"),
        P("section", None, "fsdp", "tp"),
        P("section", None, ("tp", "fsdp"), None),
    )
    sizes = tuple(mesh.shape[axis] for axis in ("section", "fsdp", "tp"))
    return jax.shard_map(
        functools.partial(per_device, sizes), mesh=mesh, in_specs=in_specs, out_specs=out_specs, check_vma=False
    )
```

```python
import functools

import jax
import jax.numpy as jnp
from jax import lax
from jax.experimental import pallas as pl
from jax.experimental.pallas import tpu as pltpu
from jax.sharding import PartitionSpec as P

QUERY_HEADS = 16
KEY_VALUE_HEADS = 8
HEAD_SIZE = 64


norm_eps = 1e-06
branch_scale = 0.22
score_scale = 0.015625
rope_base = 10000.0
masked_score = -1e30


def norm_rows(vectors, gain_vec):
    inverse = lax.rsqrt(jnp.mean(vectors * vectors, axis=-1, keepdims=True) + norm_eps)
    normed = vectors * inverse
    return (normed * gain_vec, normed, inverse)


def norm_back(upstream, normed, inverse, gain_vec):
    scaled_grad = upstream * gain_vec
    gain_grad = jnp.sum(upstream * normed, axis=0, keepdims=True)
    inner_mean = jnp.mean(scaled_grad * normed, axis=-1, keepdims=True)
    return (inverse * (scaled_grad - normed * inner_mean), gain_grad)


def rope_tables(permitted_mask):
    offsets = (jnp.sum(permitted_mask.astype(jnp.int32), axis=1) - 1).astype(jnp.float32)
    half_dim = HEAD_SIZE // 2
    frequency = rope_base ** (-(jnp.arange(half_dim, dtype=jnp.float32) * 2.0 / HEAD_SIZE))
    angles = offsets[:, None] * frequency[None, :]
    return (jnp.cos(angles)[:, None, :], jnp.sin(angles)[:, None, :])


def rotate(vectors, cosine, sine):
    half_dim = vectors.shape[-1] // 2
    front_half = vectors[..., :half_dim]
    back_half = vectors[..., half_dim:]
    return jnp.concatenate(
        [front_half * cosine - back_half * sine, back_half * cosine + front_half * sine], axis=-1
    )


def allowed_pairs(segment):
    position = jnp.arange(segment.shape[0], dtype=jnp.int32)
    return (segment[:, None] == segment[None, :]) & (position[None, :] <= position[:, None])


def attend(query_rows, key_matrix, value_matrix, permitted_mask):
    scores = (
        jnp.einsum("qhgd,khd->hgqk", query_rows, key_matrix, preferred_element_type=jnp.float32)
        * score_scale
    )
    scores = jnp.where(permitted_mask[None, None], scores, masked_score)
    row_max = jnp.max(scores, axis=-1, keepdims=True)
    log_sum_exp = row_max + jnp.log(jnp.sum(jnp.exp(scores - row_max), axis=-1, keepdims=True))
    weights_low = jnp.exp(scores - log_sum_exp).astype(jnp.bfloat16)
    attended = jnp.einsum(
        "hgqk,khd->qhgd", weights_low, value_matrix, preferred_element_type=jnp.float32
    )
    return attended.astype(jnp.bfloat16)


MESH = pl.DeviceIdType.MESH
LANES = 128
VMEM_LIMIT = 60 * 1024 * 1024
WHOLE_VMEM = pl.BlockSpec(memory_space=pltpu.VMEM)


def flipped(index, bit):
    step = 1 << bit
    return index + step - 2 * step * lax.rem(lax.div(index, step), 2)


def crossed(index, mask, bits):
    for bit in range(bits):
        if (mask >> bit) & 1:
            index = flipped(index, bit)
    return index


class Team:
    def __init__(self, sizes):
        self.sections, self.fsdp, self.tp = sizes
        self.bits = self.tp.bit_length() - 1
        assert 1 << self.bits == self.tp
        self.s = lax.axis_index("section")
        self.f = lax.axis_index("fsdp")
        self.t = lax.axis_index("tp")
        self.hops = [
            (bit, mask)
            for bit in reversed(range(self.bits))
            for mask in range(0, self.tp, 2 << bit)
        ]
        self.place = {hop: number for number, hop in enumerate(self.hops)}

    def row(self, i):
        above = self.fsdp - 1 - self.f
        short = jnp.minimum(self.f, above)
        paired = i <= 2 * short
        distance = jnp.where(paired, lax.div(i + 1, 2), i - short)
        upward = jnp.where(paired, lax.rem(i, 2) == 1, self.f < above)
        return jnp.where(upward, self.f + distance, self.f - distance)

    def column(self, mask):
        return crossed(self.t, mask, self.bits)


def greet(team, fsdp, section_step):
    barrier = pltpu.get_barrier_semaphore()
    count = 0
    if fsdp:
        for i in range(1, team.fsdp):
            pl.semaphore_signal(
                barrier,
                inc=1,
                device_id={"fsdp": lax.rem(team.f + i, team.fsdp)},
                device_id_type=MESH,
            )
            count += 1
    for bit in range(team.bits):
        pl.semaphore_signal(
            barrier, inc=1, device_id={"tp": flipped(team.t, bit)}, device_id_type=MESH
        )
        count += 1
    if section_step:
        behind = lax.rem(team.s + team.sections - section_step, team.sections)
        pl.semaphore_signal(
            barrier, inc=1, device_id={"section": behind}, device_id_type=MESH
        )
        count += 1
    pl.semaphore_wait(barrier, count)


def rows_of(block, size):
    return pl.ds(pl.multiple_of(block * size, size), size)


SLICES = 2


def slice_of(block, size, part):
    share = size // SLICES
    return pl.ds(pl.multiple_of(block * size + part * share, share), share)


class TpGather:
    def __init__(self, team, ref, size, sends, recvs, part):
        self.team, self.ref, self.size, self.part = team, ref, size, part
        self.sends = lambda place: sends(place * SLICES + part)
        self.recvs = lambda place: recvs(place * SLICES + part)

    def copy(self, hop, arriving):
        bit, mask = hop
        team = self.team
        block = team.column(mask | ((1 << bit) if arriving else 0))
        part = self.ref.at[slice_of(block, self.size, self.part)]
        return pltpu.make_async_remote_copy(
            src_ref=part,
            dst_ref=part,
            send_sem=self.sends(team.place[hop]),
            recv_sem=self.recvs(team.place[hop]),
            device_id={"tp": flipped(team.t, bit)},
            device_id_type=MESH,
        )

    def begin(self):
        for bit in reversed(range(self.team.bits)):
            self.copy((bit, 0), False).start()

    def relay(self):
        for hop in self.team.hops:
            bit, mask = hop
            if bit:
                self.copy(hop, True).wait_recv()
                for lower in reversed(range(bit)):
                    self.copy((lower, mask | (1 << bit)), False).start()

    def arrive(self):
        for hop in self.team.hops:
            if hop[0] == 0:
                self.copy(hop, True).wait_recv()

    def drain(self):
        for hop in self.team.hops:
            self.copy(hop, False).wait_send()


def add_blocks(target, rows, other, width, experts):
    wide = target[rows, :width].astype(jnp.float32) + other[:, :width].astype(jnp.float32)
    target[rows, :width] = wide.astype(target.dtype)
    if target.shape[1] > width:
        both = target[rows, width:].astype(jnp.float32) + other[:, width:].astype(jnp.float32)
        target[rows, width:] = two_parts(both, experts)


def two_parts(both, experts):
    lane = lax.broadcasted_iota(jnp.int32, both.shape, 1)
    first = lane < experts
    full = both + jnp.where(
        first, pltpu.roll(both, LANES - experts, 1), pltpu.roll(both, experts, 1)
    )
    return parted(full, first, lane < 2 * experts)


def parted(full, first, second):
    high = full.astype(jnp.bfloat16)
    low = (full - high.astype(jnp.float32)).astype(jnp.bfloat16)
    zero = jnp.zeros_like(high)
    return jnp.where(first, high, jnp.where(second, low, zero))


class TpScatter:
    def __init__(self, team, ref, size, landing, sends, recvs, width, experts, part):
        share = size // SLICES
        self.team, self.ref, self.size, self.part = team, ref, size, part
        self.landing = lambda place: landing(place).at[pl.ds(part * share, share)]
        self.sends = lambda place: sends(place * SLICES + part)
        self.recvs = lambda place: recvs(place * SLICES + part)
        self.width, self.experts = width, experts

    def copy(self, hop):
        bit, mask = hop
        team = self.team
        block = team.column(mask | (1 << bit))
        return pltpu.make_async_remote_copy(
            src_ref=self.ref.at[slice_of(block, self.size, self.part)],
            dst_ref=self.landing(team.place[hop]),
            send_sem=self.sends(team.place[hop]),
            recv_sem=self.recvs(team.place[hop]),
            device_id={"tp": flipped(team.t, bit)},
            device_id_type=MESH,
        )

    def send(self, bit):
        for hop in self.team.hops:
            if hop[0] == bit:
                self.copy(hop).start()

    def add(self, bit):
        for hop in self.team.hops:
            if hop[0] == bit:
                self.copy(hop).wait_recv()
                add_blocks(
                    self.ref,
                    slice_of(self.team.column(hop[1]), self.size, self.part),
                    self.landing(self.team.place[hop]),
                    self.width,
                    self.experts,
                )

    def drain(self):
        for hop in self.team.hops:
            self.copy(hop).wait_send()


def gather_all(team, ref, size, sends, recvs):
    slices = [
        TpGather(team, ref, size, lambda p: sends.at[p], lambda p: recvs.at[p], part)
        for part in range(SLICES)
    ]
    for phase in ("begin", "relay", "arrive", "drain"):
        for one in slices:
            getattr(one, phase)()


def scatter_all(team, ref, size, landing, sends, recvs, width):
    slices = [
        TpScatter(
            team, ref, size, lambda p: landing.at[p], lambda p: sends.at[p], lambda p: recvs.at[p], width, 0, part
        )
        for part in range(SLICES)
    ]
    for one in slices:
        one.send(0)
    for bit in range(team.bits):
        for one in slices:
            one.add(bit)
            if bit + 1 < team.bits:
                one.send(bit + 1)
    return slices


def ring_copy(team, step, source, target, sends, recvs):
    ahead = lax.rem(team.s + team.sections + step, team.sections)
    return pltpu.make_async_remote_copy(
        src_ref=source,
        dst_ref=target,
        send_sem=sends.at[0],
        recv_sem=recvs.at[0],
        device_id={"section": ahead},
        device_id_type=MESH,
    )


def group_exchange(team, gathered, partial, landing, across, sems, size, width, experts, prepare, first, second, spare=None):
    ag_send, ag_recv, agz_send, agz_recv, rs_send, rs_recv, rsz_send, rsz_recv = sems
    count = team.fsdp

    def gather(i, part):
        return TpGather(
            team,
            gathered.at[team.row(i)],
            size,
            lambda place: ag_send.at[i, place],
            lambda place: ag_recv.at[i, place],
            part,
        )

    def scatter(i, part):
        return TpScatter(
            team,
            partial.at[team.row(i)],
            size,
            lambda place: landing.at[i, place],
            lambda place: rs_send.at[i, place],
            lambda place: rs_recv.at[i, place],
            width,
            experts,
            part,
        )

    parts = range(SLICES)
    share = size // SLICES

    def gather_across(i, part, arriving):
        source = team.row(i) if arriving else team.f
        block = gathered.at[source, slice_of(team.t, size, part)]
        return pltpu.make_async_remote_copy(
            src_ref=block,
            dst_ref=block,
            send_sem=agz_send.at[i, part],
            recv_sem=agz_recv.at[source, part],
            device_id={"fsdp": team.row(i)},
            device_id_type=MESH,
        )

    def scatter_across(i, part, arriving):
        source = team.row(i) if arriving else team.f
        return pltpu.make_async_remote_copy(
            src_ref=partial.at[team.row(i), slice_of(team.t, size, part)],
            dst_ref=across.at[source, pl.ds(part * share, share)],
            send_sem=rsz_send.at[i, part],
            recv_sem=rsz_recv.at[source, part],
            device_id={"fsdp": team.row(i)},
            device_id_type=MESH,
        )

    def relay_across(i):
        for part in parts:
            gather_across(i, part, True).wait_recv()
            gather(i, part).begin()

    for part in parts:
        gather(0, part).begin()
    for i in range(1, min(count, 3)):
        for part in parts:
            gather_across(i, part, False).start()
    for part in parts:
        gather(0, part).relay()
    for i in range(3, count):
        for part in parts:
            gather_across(i, part, False).start()
    prepare()
    if count > 1:
        relay_across(1)

    def step(i, carry):
        @pl.when(i < count)
        def _():
            for part in parts:
                gather(i, part).arrive()
            first(team.row(i))

        @pl.when(i + 2 < count)
        def _():
            relay_across(i + 2)

        for bit in range(team.bits):
            done = i - 1 - bit

            @pl.when((done >= min(bit, 1)) & (done < count))
            def _():
                for part in parts:
                    scatter(done, part).add(bit)

                    @pl.when(done > 0)
                    def _():
                        if bit + 1 < team.bits:
                            scatter(done, part).send(bit + 1)
                        else:
                            scatter_across(done, part, False).start()

        @pl.when(i + 1 < count)
        def _():
            for part in parts:
                gather(i + 1, part).relay()

        @pl.when(i < count)
        def _():
            second(team.row(i))
            for part in parts:
                scatter(i, part).send(0)

        if team.bits > 1:

            @pl.when(i == count)
            def _():
                for part in parts:
                    scatter(0, part).send(1)

        if spare is not None:

            @pl.when(i >= count)
            def _():
                spare(i - count)

        return carry

    lax.fori_loop(0, count + team.bits, step, 0)
    for bit in range(1, team.bits):
        for part in parts:
            scatter(0, part).add(bit)
            if bit + 1 < team.bits:
                scatter(0, part).send(bit + 1)
    if spare is not None:
        spare(team.bits)

    def finish(i, carry):
        for part in parts:
            gather_across(i, part, False).wait_send()
            scatter_across(i, part, False).wait_send()
        return carry

    def settle(i, carry):
        for part in parts:
            gather(i, part).drain()
            scatter(i, part).drain()
        return carry

    total = partial[team.f, rows_of(team.t, size)].astype(jnp.float32)
    for i in range(1, count):
        for part in parts:
            scatter_across(i, part, True).wait_recv()
        total = total + across[team.row(i)].astype(jnp.float32)
    lax.fori_loop(1, count, finish, 0)
    lax.fori_loop(0, count, settle, 0)
    return total[:, :width], (total[:, width:] if total.shape[1] > width else None)


def group_sems(team_sizes):
    _, fsdp, tp = team_sizes
    dma = pltpu.SemaphoreType.DMA
    return [
        dma((fsdp, SLICES * tp)), dma((fsdp, SLICES * tp)), dma((fsdp, SLICES)), dma((fsdp, SLICES)),
        dma((fsdp, SLICES * tp)), dma((fsdp, SLICES * tp)), dma((fsdp, SLICES)), dma((fsdp, SLICES)),
    ]


def share_parts(share, experts):
    lane = lax.broadcasted_iota(jnp.int32, share.shape, 1)
    high = share.astype(jnp.bfloat16)
    rest = share - high.astype(jnp.float32)
    middle = rest.astype(jnp.bfloat16)
    low = (rest - middle.astype(jnp.float32)).astype(jnp.bfloat16)
    zero = jnp.zeros_like(high)
    return jnp.where(
        lane < experts,
        high,
        jnp.where(lane < 2 * experts, middle, jnp.where(lane < 3 * experts, low, zero)),
    )


def chunks(length, body, size=1024):
    size = min(size, length)

    def step(c, carry):
        body(pl.multiple_of(c * size, size), size)
        return carry

    lax.fori_loop(0, length // size, step, 0)


def product(left, right):
    return jnp.dot(left, right, preferred_element_type=jnp.float32)


def product_turned(left, right):
    return lax.dot_general(
        left, right, (((1,), (1,)), ((), ())), preferred_element_type=jnp.float32
    )


def product_over_rows(left, right):
    return lax.dot_general(
        left, right, (((0,), (0,)), ((), ())), preferred_element_type=jnp.float32
    )


def comm_params(number):
    return pltpu.CompilerParams(
        collective_id=number, has_side_effects=True, vmem_limit_bytes=VMEM_LIMIT
    )


def begin_layer(sizes, layer_in, gain, number):
    rows, width = layer_in.shape
    tp = sizes[2]

    def kernel(in_ref, gain_ref, out_ref, sends, recvs):
        team = Team(sizes)
        greet(team, False, 0)
        scaled, _, _ = norm_rows(in_ref[...].astype(jnp.float32), gain_ref[...])
        out_ref[rows_of(team.t, rows)] = scaled.astype(jnp.bfloat16)
        gather_all(team, out_ref, rows, sends, recvs)

    return pl.pallas_call(
        kernel,
        out_shape=jax.ShapeDtypeStruct((tp * rows, width), jnp.bfloat16),
        in_specs=[WHOLE_VMEM] * 2,
        out_specs=WHOLE_VMEM,
        scratch_shapes=[pltpu.SemaphoreType.DMA((SLICES * tp,)), pltpu.SemaphoreType.DMA((SLICES * tp,))],
        compiler_params=comm_params(number),
    )(layer_in, gain)


def moe_forward(sizes, partial_out, residual, chosen, weights, fresh, experts, number):
    router, gain_one, gain_two, gate_up, down, spread_map = weights
    sections, fsdp, tp = sizes
    rows, width = residual.shape
    band = tp * rows
    hidden = down.shape[0]
    copies = LANES // experts
    tail = fresh is not None
    bf16, f32 = jnp.bfloat16, jnp.float32
    shapes = [
        jax.ShapeDtypeStruct((fsdp, band, width), bf16),
        jax.ShapeDtypeStruct((fsdp, band, 2 * hidden), bf16),
        jax.ShapeDtypeStruct((fsdp, band, LANES), f32),
        jax.ShapeDtypeStruct((rows, width), f32),
        jax.ShapeDtypeStruct((rows, width), bf16),
    ]
    if tail:
        shapes += [
            jax.ShapeDtypeStruct((rows, width), bf16),
            jax.ShapeDtypeStruct((band, width), bf16),
        ]
    dma = pltpu.SemaphoreType.DMA
    scratch = [
        pltpu.VMEM((band, width), bf16),
        pltpu.VMEM((tp, rows, width), bf16),
        pltpu.VMEM((fsdp, band, width), bf16),
        pltpu.VMEM((fsdp, tp - 1, rows, width), bf16),
        pltpu.VMEM((fsdp, rows, width), bf16),
        pltpu.VMEM((band, hidden), bf16),
        pltpu.VMEM((band, LANES), bf16),
        pltpu.VMEM((rows, width), bf16),
        pltpu.VMEM((width, 2 * hidden), bf16),
        pltpu.VMEM((hidden, width), bf16),
        pltpu.VMEM((fsdp, band, width), bf16),
        pltpu.VMEM((fsdp, band, 2 * hidden), bf16),
        dma((SLICES * tp,)), dma((SLICES * tp,)), dma((SLICES * tp,)), dma((SLICES * tp,)), dma((1,)), dma((1,)),
        dma((2,)), dma((fsdp,)), dma((fsdp,)),
    ] + group_sems(sizes)
    own, out = WHOLE_VMEM, pl.BlockSpec(memory_space=pl.ANY)

    def kernel(*refs):
        part_ref, res_ref, chosen_ref, router_ref, one_ref, two_ref, both_hbm, down_hbm, map_ref = refs[:9]
        refs = refs[9:]
        if tail:
            fresh_ref, refs = refs[0], refs[1:]
        all_hbm, pre_hbm, share_ref, state_ref, result_ref = refs[:5]
        refs = refs[5:]
        if tail:
            next_ref, attn_ref = refs[:2]
            refs = refs[2:]
        sums, sums_in, partial, landing, across, weighted, parts, moved = refs[:8]
        both_ref, down_ref, all_ref, pre_ref = refs[8:12]
        tr_send, tr_recv, tg_send, tg_recv, sec_send, sec_recv, load_sem, all_sem, pre_sem = refs[12:21]
        sems = refs[21:]
        team = Team(sizes)
        loads = [
            pltpu.make_async_copy(both_hbm, both_ref, load_sem.at[0]),
            pltpu.make_async_copy(down_hbm, down_ref, load_sem.at[1]),
        ]
        for load in loads:
            load.start()

        def all_out(row):
            return pltpu.make_async_copy(all_ref.at[row], all_hbm.at[row], all_sem.at[row])

        def pre_out(row):
            return pltpu.make_async_copy(pre_ref.at[row], pre_hbm.at[row], pre_sem.at[row])

        def prepare():
            for load in loads:
                load.wait()

        sums[...] = part_ref[...]
        greet(team, True, 1 if tail else 0)
        reduce = scatter_all(team, sums, rows, sums_in, tr_send, tr_recv, width)
        state = res_ref[...].astype(f32) + branch_scale * sums[rows_of(team.t, rows)].astype(f32)
        state_ref[...] = state
        scaled, _, _ = norm_rows(state, two_ref[...])
        all_ref[team.f, rows_of(team.t, rows)] = scaled.astype(bf16)

        def first(row):
            all_out(row).start()
            logits = product(all_ref[row], router_ref[...])
            logits = jnp.where(chosen_ref[row].astype(f32) > 0.5, logits, masked_score)
            grown = jnp.exp(logits - jnp.max(logits, axis=-1, keepdims=True))
            total = jnp.sum(grown, axis=-1, keepdims=True) * (1.0 / copies)
            share = grown / total
            share_ref[row] = share
            parts[...] = share_parts(share, experts)

            def piece(start, size):
                here, there = pl.ds(start, size), pl.ds(pl.multiple_of(hidden + start, size), size)
                gate = product(all_ref[row], both_ref[:, here])
                up = product(all_ref[row], both_ref[:, there])
                pre_ref[row, :, here] = gate.astype(bf16)
                pre_ref[row, :, there] = up.astype(bf16)
                wide = product(parts[...], map_ref[:, here])
                weighted[:, here] = (wide * (gate * jax.nn.sigmoid(gate) * up)).astype(bf16)

            chunks(hidden, piece)
            pre_out(row).start()

        def second(row):
            def piece(start, size):
                here = pl.ds(start, size)
                partial[row, :, here] = product(weighted[...], down_ref[:, here]).astype(bf16)

            chunks(width, piece)

        total, _ = group_exchange(
            team, all_ref, partial, landing, across, sems, rows, width, experts, prepare, first, second
        )
        result_ref[...] = (state_ref[...] + branch_scale * total).astype(bf16)
        for one in reduce:
            one.drain()
        if tail:
            move = ring_copy(team, 1, result_ref, moved, sec_send, sec_recv)
            move.start()
            move.wait_recv()
            layer_in = jnp.where(team.s == 0, fresh_ref[...], moved[...])
            next_ref[...] = layer_in
            scaled, _, _ = norm_rows(layer_in.astype(f32), one_ref[...])
            attn_ref[rows_of(team.t, rows)] = scaled.astype(bf16)
            gather_all(team, attn_ref, rows, tg_send, tg_recv)
            move.wait_send()
        for row in range(fsdp):
            all_out(row).wait()
            pre_out(row).wait()

    args = [partial_out, residual, chosen, router, gain_one, gain_two, gate_up, down, spread_map]
    if tail:
        args.append(fresh)
    return pl.pallas_call(
        kernel,
        out_shape=shapes,
        in_specs=[own] * 6 + [out] * 2 + [own] * (len(args) - 8),
        out_specs=[out] * 2 + [own] * (len(shapes) - 2),
        scratch_shapes=scratch,
        compiler_params=comm_params(number),
        name="moe_forward",
    )(*args)


def moe_backward(sizes, upstream, state, share, pre, moe_in, weights, experts, sums, final, number):
    router, gain_two, gate_up, down, spread_map, pick_map = weights
    sections, fsdp, tp = sizes
    rows, width = upstream.shape
    band = tp * rows
    hidden = down.shape[0]
    bf16, f32 = jnp.bfloat16, jnp.float32
    leaving = bf16 if final else f32
    shapes = [
        jax.ShapeDtypeStruct((width, 2 * hidden), leaving),
        jax.ShapeDtypeStruct((hidden, width), f32),
        jax.ShapeDtypeStruct((rows, LANES), bf16),
        jax.ShapeDtypeStruct((1, width), f32),
        jax.ShapeDtypeStruct((rows, width), f32),
        jax.ShapeDtypeStruct((band, width), bf16),
    ]
    dma = pltpu.SemaphoreType.DMA
    wider = width + LANES
    both_units = team_units(tp)
    both_step = 2 * hidden // both_units
    loops = [both_step // chunk_size(both_step), width // chunk_size(width)]
    both_size, down_size = chunk_size(both_step), chunk_size(width)
    scratch = [
        pltpu.VMEM((fsdp, band, wider), bf16),
        pltpu.VMEM((fsdp, tp - 1, rows, wider), bf16),
        pltpu.VMEM((fsdp, rows, wider), bf16),
        pltpu.VMEM((band, LANES), bf16),
        pltpu.VMEM((band, LANES), f32),
        pltpu.VMEM((width, 2 * hidden), bf16),
        pltpu.VMEM((hidden, width), bf16),
        pltpu.VMEM((fsdp, band, 2 * hidden), bf16),
        pltpu.VMEM((fsdp, band, width), bf16),
        pltpu.VMEM((fsdp, band, 2 * hidden), bf16),
        pltpu.VMEM((fsdp, band, hidden), bf16),
        pltpu.VMEM((fsdp, band, width), bf16),
        pltpu.VMEM((width, 2 * hidden), f32),
        pltpu.VMEM((hidden, width), f32),
        pltpu.VMEM((width, 2 * hidden) if final else (16, LANES), bf16),
        dma((SLICES * tp,)), dma((SLICES * tp,)), dma((5,)), dma((fsdp,)), dma((2,)),
    ] + group_sems(sizes)
    own, out = WHOLE_VMEM, pl.BlockSpec(memory_space=pl.ANY)
    adding = sums is not None

    def kernel(*refs):
        up_ref, state_ref, share_ref, pre_hbm, router_ref, gain_ref, both_hbm, down_hbm, map_ref, pick_ref, in_hbm = refs[:11]
        refs = refs[11:]
        if adding:
            both_old, down_old = refs[:2]
            refs = refs[2:]
        both_out, down_out, logit_ref, gain_out, state_out, attn_ref = refs[:6]
        partial, landing, across, parts, share_sum, both_ref, down_ref, pre_ref, all_ref, grad_ref, weighted_ref = refs[6:17]
        in_ref, both_sum, down_sum, both_low, tg_send, tg_recv, load_sem, pre_sem, out_sem = refs[17:26]
        sems = refs[26:]
        team = Team(sizes)
        loads = [
            pltpu.make_async_copy(down_hbm, down_ref, load_sem.at[0]),
            pltpu.make_async_copy(both_hbm, both_ref, load_sem.at[1]),
        ]
        later = [pltpu.make_async_copy(in_hbm, in_ref, load_sem.at[2])]
        if adding:
            later += [
                pltpu.make_async_copy(both_old, both_sum, load_sem.at[3]),
                pltpu.make_async_copy(down_old, down_sum, load_sem.at[4]),
            ]
        outs = [
            pltpu.make_async_copy(both_low if final else both_sum, both_out, out_sem.at[0]),
            pltpu.make_async_copy(down_sum, down_out, out_sem.at[1]),
        ]

        def pre_in(row):
            return pltpu.make_async_copy(pre_hbm.at[row], pre_ref.at[row], pre_sem.at[row])

        loads[0].start()
        for i in range(fsdp):
            pre_in(i).start()
        loads[1].start()
        for load in later:
            load.start()

        def prepare():
            for load in loads:
                load.wait()
            for i in range(fsdp):
                pre_in(i).wait()

        def spare(unit):
            @pl.when(unit == 0)
            def _():
                for load in later:
                    load.wait()

            if isinstance(unit, int):
                left, right, total, size = weighted_ref, all_ref, down_sum, down_size
                start, count = 0, loops[1]
            else:
                left, right, total, size = in_ref, grad_ref, both_sum, both_size
                start, count = unit * both_step, loops[0]

            def turn(c, carry):
                here = pl.ds(pl.multiple_of(start + c * size, size), size)
                made = lax.dot_general(
                    left[...].reshape(fsdp * band, left.shape[2]),
                    right[:, :, here].reshape(fsdp * band, size),
                    (((0,), (0,)), ((), ())),
                    preferred_element_type=f32,
                )
                if adding:
                    made = made + total[:, here]
                if final and total is both_sum:
                    both_low[:, here] = made.astype(bf16)
                else:
                    total[:, here] = made
                return carry

            lax.fori_loop(0, count, turn, 0)
            if isinstance(unit, int):
                for done in outs:
                    done.start()

        greet(team, True, 0)
        all_ref[team.f, rows_of(team.t, rows)] = (branch_scale * up_ref[...]).astype(bf16)

        def first(row):
            parts[...] = share_parts(share_ref[row], experts)
            share_sum[...] = jnp.zeros_like(share_sum)

            def piece(start, size):
                here, there = pl.ds(start, size), pl.ds(pl.multiple_of(hidden + start, size), size)
                hidden_grad = product_turned(all_ref[row], down_ref[here])
                gate = pre_ref[row, :, here].astype(f32)
                up = pre_ref[row, :, there].astype(f32)
                wide = product(parts[...], map_ref[:, here])
                sigmoid_gate = jax.nn.sigmoid(gate)
                swish = gate * sigmoid_gate
                value = swish * up
                weighted_ref[row, :, here] = (wide * value).astype(bf16)
                both = hidden_grad * value
                high = both.astype(bf16)
                low = (both - high.astype(f32)).astype(bf16)
                share_sum[...] += product(high, pick_ref[here]) + product(low, pick_ref[here])
                scaled = wide * hidden_grad
                grad_ref[row, :, here] = (
                    scaled * up * sigmoid_gate * (1.0 + gate * (1.0 - sigmoid_gate))
                ).astype(bf16)
                grad_ref[row, :, there] = (scaled * swish).astype(bf16)

            chunks(hidden, piece)

        def second(row):
            def piece(start, size):
                here = pl.ds(start, size)
                partial[row, :, here] = product_turned(grad_ref[row], both_ref[here]).astype(bf16)

            chunks(width, piece)
            lane = lax.broadcasted_iota(jnp.int32, (band, LANES), 1)
            partial[row, :, width:] = parted(share_sum[...], lane < experts, lane < 2 * experts)

        total, extra = group_exchange(
            team, all_ref, partial, landing, across, sems, rows, width, experts, prepare, first, second, spare
        )
        lane = lax.broadcasted_iota(jnp.int32, (rows, LANES), 1)
        valid = lane < experts
        share_grad = extra + pltpu.roll(extra, LANES - experts, 1)
        own_share = jnp.where(valid, share_ref[team.f, rows_of(team.t, rows)], 0.0)
        inner = jnp.sum(own_share * share_grad, axis=-1, keepdims=True)
        logit_grad = (own_share * (share_grad - inner)).astype(bf16)
        logit_ref[...] = logit_grad
        norm_grad = total + product_turned(logit_grad, router_ref[...])
        _, normed, inverse = norm_rows(state_ref[...], gain_ref[...])
        back, gain_grad = norm_back(norm_grad, normed, inverse, gain_ref[...])
        gain_out[...] = gain_grad
        state_grad = up_ref[...] + back
        state_out[...] = state_grad
        attn_ref[rows_of(team.t, rows)] = (branch_scale * state_grad).astype(bf16)
        gather_all(team, attn_ref, rows, tg_send, tg_recv)
        for done in outs:
            done.wait()

    args = [upstream, state, share, pre, router, gain_two, gate_up, down, spread_map, pick_map, moe_in]
    if adding:
        args += list(sums)
    return pl.pallas_call(
        kernel,
        out_shape=shapes,
        in_specs=[own] * 3 + [out] + [own] * 2 + [out] * 2 + [own] * 2 + [out] * (len(args) - 10),
        out_specs=[out] * 2 + [own] * 4,
        scratch_shapes=scratch,
        compiler_params=comm_params(number),
        name="moe_backward",
    )(*args)


def team_units(tp):
    return tp.bit_length() - 1


def chunk_size(length, most=512):
    return min(length, most)


def end_layer(sizes, attn_grad, kept, out_twice, w_qkv, layer_in, state_grad, gain, number):
    queries, keys, values, bias, turn = kept
    tp = sizes[2]
    rows, width = layer_in.shape
    band = tp * rows
    kv_heads = keys.shape[1] // LANES
    each = queries.shape[1] // keys.shape[1]
    qkv_width = w_qkv.shape[1]
    query_width = queries.shape[1] * HEAD_SIZE // LANES
    key_width = keys.shape[1] * HEAD_SIZE // LANES
    held = LANES // HEAD_SIZE
    bf16, f32 = jnp.bfloat16, jnp.float32
    dma = pltpu.SemaphoreType.DMA

    def kernel(
        attn_ref, q_ref, k_ref, v_ref, bias_ref, turn_ref, twice_ref, qkv_ref, in_ref, grad_ref, gain_ref,
        out_ref, gain_out, arrived_ref, made_ref,
        heads, sums, sums_in, leaving, tr_send, tr_recv, sec_send, sec_recv,
    ):
        team = Team(sizes)
        barrier = pltpu.get_barrier_semaphore()
        for bit in range(team.bits):
            pl.semaphore_signal(
                barrier, inc=1, device_id={"tp": flipped(team.t, bit)}, device_id_type=MESH
            )
        pl.semaphore_signal(
            barrier,
            inc=1,
            device_id={"section": lax.rem(team.s + 1, team.sections)},
            device_id_type=MESH,
        )
        heads[...] = product_turned(attn_ref[...], twice_ref[...]).astype(bf16)
        lane = lax.broadcasted_iota(jnp.int32, (band, LANES), 1)
        turning = turn_ref[...]

        def turned_back(array):
            array = array * turning
            return array + pltpu.roll(array, HEAD_SIZE, 1)

        def place(start, parts):
            for number in range(0, len(parts), held):
                block = parts[number]
                for other in range(1, held):
                    block = jnp.where(lane < other * HEAD_SIZE, block, parts[number + other])
                where = start + number * HEAD_SIZE
                made_ref[:, where : where + LANES] = block.astype(bf16)

        def lanes_of(number):
            return slice(number * LANES, (number + 1) * LANES)

        query_parts, key_parts, value_parts = [], [], []
        for g in range(kv_heads):
            key, value = k_ref[:, lanes_of(g)], v_ref[:, lanes_of(g)]
            key_sum = jnp.zeros((band, LANES), f32)
            value_sum = jnp.zeros((band, LANES), f32)
            for h in range(g * each, (g + 1) * each):
                query, head = q_ref[:, lanes_of(h)], heads[:, lanes_of(h)]
                scores = product_turned(query, key) * (0.5 * score_scale) + bias_ref[...]
                grown = jnp.exp(scores - jnp.max(scores, axis=-1, keepdims=True))
                weight = grown / jnp.sum(grown, axis=-1, keepdims=True)
                value_sum += product_over_rows(weight.astype(bf16), head)
                weight_grad = product_turned(head, value)
                inner = jnp.sum(weight * weight_grad, axis=-1, keepdims=True)
                score_grad = (weight * (weight_grad - inner) * score_scale).astype(bf16)
                query_parts.append(turned_back(product(score_grad, key)))
                key_sum += product_over_rows(score_grad, query)
            key_parts.append(turned_back(key_sum))
            value_parts.append(value_sum)
        place(0, query_parts)
        place(query_width, key_parts)
        place(query_width + key_width, value_parts)
        sums[...] = product_turned(made_ref[...], qkv_ref[...]).astype(bf16)
        pl.semaphore_wait(barrier, team.bits + 1)
        reduce = scatter_all(team, sums, rows, sums_in, tr_send, tr_recv, width)
        norm_grad = sums[rows_of(team.t, rows)].astype(f32)
        _, normed, inverse = norm_rows(in_ref[...].astype(f32), gain_ref[...])
        back, gain_grad = norm_back(norm_grad, normed, inverse, gain_ref[...])
        result = grad_ref[...] + back
        leaving[...] = result.astype(bf16)
        move = ring_copy(team, -1, leaving, arrived_ref, sec_send, sec_recv)
        move.start()
        gain_out[...] = gain_grad
        out_ref[...] = result
        for one in reduce:
            one.drain()
        move.wait()

    return pl.pallas_call(
        kernel,
        out_shape=[
            jax.ShapeDtypeStruct((rows, width), f32),
            jax.ShapeDtypeStruct((1, width), f32),
            jax.ShapeDtypeStruct((rows, width), bf16),
            jax.ShapeDtypeStruct((band, qkv_width), bf16),
        ],
        in_specs=[WHOLE_VMEM] * 11,
        out_specs=[WHOLE_VMEM] * 4,
        scratch_shapes=[
            pltpu.VMEM((band, queries.shape[1]), bf16),
            pltpu.VMEM((band, width), bf16),
            pltpu.VMEM((tp, rows, width), bf16),
            pltpu.VMEM((rows, width), bf16),
            dma((SLICES * tp,)), dma((SLICES * tp,)), dma((1,)), dma((1,)),
        ],
        compiler_params=comm_params(number),
        name="end_layer",
    )(attn_grad, queries, keys, values, bias, turn, out_twice, w_qkv, layer_in, state_grad, gain)


def plain_copy(array, steps):
    rows, width = array.shape

    def kernel(in_ref, out_ref):
        out_ref[...] = in_ref[...]

    block = pl.BlockSpec((rows // steps, width), lambda i: (i, 0))
    return pl.pallas_call(
        kernel,
        grid=(steps,),
        out_shape=jax.ShapeDtypeStruct(array.shape, array.dtype),
        in_specs=[block],
        out_specs=block,
        name="plain_copy",
    )(array)


def order_map(inputs, outputs, count, part, turned):
    across = count * part
    source = lax.broadcasted_iota(jnp.int32, (inputs, outputs), 1 if turned else 0)
    target = lax.broadcasted_iota(jnp.int32, (inputs, outputs), 0 if turned else 1)
    e, rest = lax.div(source, across), lax.rem(source, across)
    f, h = lax.div(rest, part), lax.rem(rest, part)
    return (f * LANES + e * part + h == target).astype(jnp.bfloat16)


def block_steps(blocks):
    for steps in (2, 1):
        if blocks % steps == 0:
            return steps


def outgoing_experts(w_gate, w_up, count):
    experts, depth, hidden = w_gate.shape
    part = hidden // count
    bunch = LANES // part
    across = bunch * hidden
    steps = block_steps(experts // bunch)
    each = experts // bunch // steps

    def kernel(gate_ref, up_ref, out_ref, table):
        @pl.when((pl.program_id(0) == 0) & (pl.program_id(1) == 0))
        def _():
            table[...] = order_map(across, count * LANES, count, part, False)

        def move(ref):
            for b in range(each):
                lanes = jnp.concatenate([ref[b * bunch + e] for e in range(bunch)], axis=1)
                moved = product(lanes, table[...]).astype(jnp.bfloat16)
                for f in range(count):
                    out_ref[f, :, b * LANES : (b + 1) * LANES] = moved[:, f * LANES : (f + 1) * LANES]

        @pl.when(pl.program_id(0) == 0)
        def _():
            move(gate_ref)

        @pl.when(pl.program_id(0) == 1)
        def _():
            move(up_ref)

    block = (each * bunch, depth, hidden)
    return pl.pallas_call(
        kernel,
        grid=(2, steps),
        out_shape=jax.ShapeDtypeStruct((count, depth, 2 * steps * each * LANES), jnp.bfloat16),
        in_specs=[
            pl.BlockSpec(block, lambda w, b: (jnp.where(w == 0, b, steps - 1), 0, 0)),
            pl.BlockSpec(block, lambda w, b: (jnp.where(w == 1, b, 0), 0, 0)),
        ],
        out_specs=pl.BlockSpec((count, depth, each * LANES), lambda w, b: (0, 0, w * steps + b)),
        scratch_shapes=[pltpu.VMEM((across, count * LANES), jnp.bfloat16)],
        compiler_params=pltpu.CompilerParams(vmem_limit_bytes=VMEM_LIMIT),
        name="outgoing_experts",
    )(w_gate, w_up)


def incoming_experts(both, experts, hidden):
    count, depth, width = both.shape
    part = hidden // count
    bunch = LANES // part
    across = bunch * hidden
    steps = block_steps(experts // bunch)
    each = experts // bunch // steps

    def kernel(in_ref, gate_ref, up_ref, table):
        @pl.when((pl.program_id(0) == 0) & (pl.program_id(1) == 0))
        def _():
            table[...] = order_map(count * LANES, across, count, part, True)

        def store(ref):
            for b in range(each):
                lanes = jnp.concatenate(
                    [in_ref[f, :, b * LANES : (b + 1) * LANES] for f in range(count)], axis=1
                )
                moved = product(lanes, table[...])
                for e in range(bunch):
                    ref[b * bunch + e] = moved[:, e * hidden : (e + 1) * hidden]

        @pl.when(pl.program_id(0) == 0)
        def _():
            store(gate_ref)

        @pl.when(pl.program_id(0) == 1)
        def _():
            store(up_ref)

    shape = jax.ShapeDtypeStruct((experts, depth, hidden), jnp.float32)
    block = (each * bunch, depth, hidden)
    return pl.pallas_call(
        kernel,
        grid=(2, steps),
        out_shape=[shape, shape],
        in_specs=[pl.BlockSpec((count, depth, each * LANES), lambda w, b: (0, 0, w * steps + b))],
        out_specs=[
            pl.BlockSpec(block, lambda w, b: (jnp.where(w == 0, b, steps - 1), 0, 0)),
            pl.BlockSpec(block, lambda w, b: (jnp.where(w == 1, b, 0), 0, 0)),
        ],
        scratch_shapes=[pltpu.VMEM((count * LANES, across), jnp.bfloat16)],
        compiler_params=pltpu.CompilerParams(vmem_limit_bytes=VMEM_LIMIT),
        name="incoming_experts",
    )(both)


def line_barrier(team, tp):
    barrier = pltpu.get_barrier_semaphore()
    count = 0
    for i in range(1, team.fsdp):
        pl.semaphore_signal(
            barrier,
            inc=1,
            device_id={"fsdp": lax.rem(team.f + i, team.fsdp)},
            device_id_type=MESH,
        )
        count += 1
    if tp:
        for bit in range(team.bits):
            pl.semaphore_signal(
                barrier, inc=1, device_id={"tp": flipped(team.t, bit)}, device_id_type=MESH
            )
            count += 1
    pl.semaphore_wait(barrier, count)


def gather_weights(sizes, matrix, small, number):
    fsdp = sizes[1]
    depth, width = matrix.shape
    dma = pltpu.SemaphoreType.DMA

    def kernel(matrix_ref, small_ref, all_ref, few_ref, held, *sems):
        up_send, up_recv, down_send, down_recv, few_send, few_recv, local, out_sem = sems
        team = Team(sizes)
        f = team.f
        mine = pltpu.make_async_copy(matrix_ref, held.at[f], local.at[0])
        mine.start()
        few_ref[f] = small_ref[...]
        line_barrier(team, False)

        def few(i, arriving):
            other = lax.rem(f + (fsdp - i if arriving else i), fsdp)
            part = few_ref.at[other if arriving else f]
            return pltpu.make_async_remote_copy(
                src_ref=part,
                dst_ref=part,
                send_sem=few_send.at[i],
                recv_sem=few_recv.at[i],
                device_id={"fsdp": other},
                device_id_type=MESH,
            )

        for i in range(1, fsdp):
            few(i, False).start()
        mine.wait()

        def hand(block, step):
            sends, recvs = (up_send, up_recv) if step > 0 else (down_send, down_recv)
            return pltpu.make_async_remote_copy(
                src_ref=held.at[block],
                dst_ref=held.at[block],
                send_sem=sends.at[block],
                recv_sem=recvs.at[block],
                device_id={"fsdp": lax.rem(f + step + fsdp, fsdp)},
                device_id_type=MESH,
            )

        def out(block):
            return pltpu.make_async_copy(held.at[block], all_ref.at[block], out_sem.at[block])

        @pl.when(f < fsdp - 1)
        def _():
            hand(f, 1).start()

        @pl.when(f > 0)
        def _():
            hand(f, -1).start()

        out(f).start()

        def step(i, carry):
            below, above = f - i, f + i

            @pl.when(below >= 0)
            def _():
                hand(below, 1).wait_recv()

                @pl.when(f < fsdp - 1)
                def _():
                    hand(below, 1).start()

                out(below).start()

            @pl.when(above < fsdp)
            def _():
                hand(above, -1).wait_recv()

                @pl.when(f > 0)
                def _():
                    hand(above, -1).start()

                out(above).start()

            return carry

        lax.fori_loop(1, fsdp, step, 0)

        def finish(g, carry):
            @pl.when((g <= f) & (f < fsdp - 1))
            def _():
                hand(g, 1).wait_send()

            @pl.when((g >= f) & (f > 0))
            def _():
                hand(g, -1).wait_send()

            out(g).wait()
            return carry

        lax.fori_loop(0, fsdp, finish, 0)
        for i in range(1, fsdp):
            few(i, True).wait_recv()
            few(i, False).wait_send()

    anywhere = pl.BlockSpec(memory_space=pl.ANY)
    return pl.pallas_call(
        kernel,
        out_shape=[
            jax.ShapeDtypeStruct((fsdp, depth, width), matrix.dtype),
            jax.ShapeDtypeStruct((fsdp,) + small.shape, small.dtype),
        ],
        in_specs=[anywhere, WHOLE_VMEM],
        out_specs=[anywhere, WHOLE_VMEM],
        scratch_shapes=[pltpu.VMEM((fsdp, depth, width), matrix.dtype)]
        + [dma((fsdp,)) for _ in range(6)]
        + [dma((1,)), dma((fsdp,))],
        compiler_params=comm_params(number),
        name="gather_weights",
    )(matrix, small)


def reduce_weights(sizes, matrix, small, number):
    tp, fsdp = sizes[2], sizes[1]
    _, depth, width = matrix.shape
    count_rows = small.shape[0]
    portion = small.shape[1] // fsdp
    bits = tp.bit_length() - 1
    bf16, f32 = jnp.bfloat16, jnp.float32
    dma = pltpu.SemaphoreType.DMA

    def kernel(matrix_ref, small_ref, sum_ref, few_ref, up, down, up_in, down_in, few_sum, few_tp, few_cut, few_in, *sems):
        up_send, up_recv, down_send, down_recv, tp_send, tp_recv, few_send, few_recv = sems
        team = Team(sizes)
        f = team.f
        line_barrier(team, True)

        def pass_on(g, step):
            sends, recvs = (up_send, up_recv) if step > 0 else (down_send, down_recv)
            return pltpu.make_async_remote_copy(
                src_ref=(up if step > 0 else down).at[g],
                dst_ref=(up_in if step > 0 else down_in).at[g],
                send_sem=sends.at[g],
                recv_sem=recvs.at[g],
                device_id={"fsdp": lax.rem(f + step + fsdp, fsdp)},
                device_id_type=MESH,
            )

        def tp_copy(bit):
            return pltpu.make_async_remote_copy(
                src_ref=few_sum.at[bit],
                dst_ref=few_tp.at[bit],
                send_sem=tp_send.at[bit],
                recv_sem=tp_recv.at[bit],
                device_id={"tp": flipped(team.t, bit)},
                device_id_type=MESH,
            )

        few_sum[0] = small_ref[...]

        def step(i, carry):
            high, low = fsdp - 1 - i, i

            @pl.when(high > f)
            def _():
                @pl.when(f == 0)
                def _():
                    up[high] = matrix_ref[high]

                @pl.when(f > 0)
                def _():
                    pass_on(high, 1).wait_recv()
                    up[high] = (matrix_ref[high].astype(f32) + up_in[high].astype(f32)).astype(bf16)

                pass_on(high, 1).start()

            @pl.when(low < f)
            def _():
                @pl.when(f == fsdp - 1)
                def _():
                    down[low] = matrix_ref[low]

                @pl.when(f < fsdp - 1)
                def _():
                    pass_on(low, -1).wait_recv()
                    down[low] = (matrix_ref[low].astype(f32) + down_in[low].astype(f32)).astype(bf16)

                pass_on(low, -1).start()

            return carry

        lax.fori_loop(0, fsdp - 1, step, 0)
        for bit in range(bits):
            tp_copy(bit).start()
            tp_copy(bit).wait_recv()
            few_sum[bit + 1] = few_sum[bit] + few_tp[bit]
        for g in range(fsdp):
            few_cut[g] = few_sum[bits, :, g * portion : (g + 1) * portion]

        def few(i, arriving):
            other = lax.rem(f + (fsdp - i if arriving else i), fsdp)
            return pltpu.make_async_remote_copy(
                src_ref=few_cut.at[other],
                dst_ref=few_in.at[i],
                send_sem=few_send.at[i],
                recv_sem=few_recv.at[i],
                device_id={"fsdp": other},
                device_id_type=MESH,
            )

        for i in range(1, fsdp):
            few(i, False).start()
        sum_ref[...] = matrix_ref[f].astype(f32)

        @pl.when(f > 0)
        def _():
            pass_on(f, 1).wait_recv()
            sum_ref[...] += up_in[f].astype(f32)

        @pl.when(f < fsdp - 1)
        def _():
            pass_on(f, -1).wait_recv()
            sum_ref[...] += down_in[f].astype(f32)

        total = few_cut[f]
        for i in range(1, fsdp):
            few(i, True).wait_recv()
            total = total + few_in[i]
        few_ref[...] = total

        def finish(g, carry):
            @pl.when(g > f)
            def _():
                pass_on(g, 1).wait_send()

            @pl.when(g < f)
            def _():
                pass_on(g, -1).wait_send()

            return carry

        lax.fori_loop(0, fsdp, finish, 0)
        for i in range(1, fsdp):
            few(i, False).wait_send()
        for bit in range(bits):
            tp_copy(bit).wait_send()

    return pl.pallas_call(
        kernel,
        out_shape=[
            jax.ShapeDtypeStruct((depth, width), f32),
            jax.ShapeDtypeStruct((count_rows, portion), f32),
        ],
        in_specs=[WHOLE_VMEM] * 2,
        out_specs=[WHOLE_VMEM] * 2,
        scratch_shapes=[pltpu.VMEM((fsdp, depth, width), bf16) for _ in range(4)]
        + [
            pltpu.VMEM((bits + 1,) + small.shape, f32),
            pltpu.VMEM((bits,) + small.shape, f32),
            pltpu.VMEM((fsdp, count_rows, portion), f32),
            pltpu.VMEM((fsdp, count_rows, portion), f32),
        ]
        + [dma((fsdp,)) for _ in range(4)]
        + [dma((tp,)), dma((tp,)), dma((fsdp,)), dma((fsdp,))],
        compiler_params=comm_params(number),
        name="reduce_weights",
    )(matrix, small)


def exchange(blocks):
    return lax.all_to_all(blocks, "fsdp", split_axis=0, concat_axis=0, tiled=True)


def attention_forward(attn_in, segment, w_qkv, w_output):
    query_width = w_output.shape[0]
    key_width = (w_qkv.shape[1] - query_width) // 2
    key_value_heads = key_width // HEAD_SIZE
    count_of_tokens = attn_in.shape[0]
    permitted_mask = allowed_pairs(segment)
    cosine, sine = rope_tables(permitted_mask)
    qkv = jnp.dot(attn_in, w_qkv, preferred_element_type=jnp.float32)
    turned = rotate(
        qkv[:, : query_width + key_width].reshape(count_of_tokens, -1, HEAD_SIZE), cosine, sine
    ).astype(jnp.bfloat16)
    query_rows = turned[:, : query_width // HEAD_SIZE].reshape(
        count_of_tokens, key_value_heads, QUERY_HEADS // KEY_VALUE_HEADS, HEAD_SIZE
    )
    key_matrix = turned[:, query_width // HEAD_SIZE :]
    value_matrix = (
        qkv[:, query_width + key_width :]
        .astype(jnp.bfloat16)
        .reshape(count_of_tokens, key_value_heads, HEAD_SIZE)
    )
    attended = attend(query_rows, key_matrix, value_matrix, permitted_mask)
    mixed_heads = attended.reshape(count_of_tokens, -1)
    partial = jnp.dot(mixed_heads, w_output, preferred_element_type=jnp.float32)
    half = HEAD_SIZE // 2
    beside = jnp.concatenate([turned, turned[..., half:], turned[..., :half]], axis=-1)
    heads = query_width // HEAD_SIZE
    queries = beside[:, :heads].reshape(count_of_tokens, -1)
    keys = beside[:, heads:].reshape(count_of_tokens, -1)
    values = jnp.concatenate([value_matrix, jnp.zeros_like(value_matrix)], axis=-1)
    bias = jnp.where(permitted_mask, 0.0, masked_score).astype(jnp.float32)
    turn = jnp.concatenate([cosine, cosine, sine, -sine], axis=-1)[:, 0]
    kept = (queries, keys, values.reshape(count_of_tokens, -1), bias, turn)
    return (partial.astype(jnp.bfloat16), kept, mixed_heads)


def summed_product(pairs):
    left = jnp.concatenate([pair[0] for pair in pairs], axis=0)
    right = jnp.concatenate([pair[1] for pair in pairs], axis=0)
    return lax.dot_general(
        left, right, (((0,), (0,)), ((), ())), preferred_element_type=jnp.float32
    )


def per_device(
    sizes,
    inputs,
    segment_ids,
    routes,
    w_query,
    key_weight,
    value_weight,
    w_output,
    w_router,
    gain_attn,
    gain_moe,
    w_gate,
    w_up,
    w_down,
    out_grad,
):
    section_count, fsdp_count, tp_count = sizes
    section_index = lax.axis_index("section")
    micro_count, local_rows, model_width = inputs.shape
    depth = w_query.shape[1]
    expert_count = w_router.shape[2]
    hidden_units = w_gate.shape[3]
    own_units = hidden_units // fsdp_count
    hidden = expert_count * own_units
    copies = LANES // expert_count
    query_width = w_query.shape[2]
    key_width = key_weight.shape[2]
    qkv_width = query_width + 2 * key_width
    flat_output = w_output[0].reshape(depth, -1)
    matrix = jnp.concatenate(
        [w_query[0], key_weight[0], value_weight[0], flat_output], axis=1
    )
    few = jnp.concatenate(
        [w_router[0].T, gain_attn.astype(jnp.bfloat16), gain_moe.astype(jnp.bfloat16)], axis=0
    )
    few_rows = -(-few.shape[0] // 16) * 16
    few = jnp.pad(few, ((0, few_rows - few.shape[0]), (0, 0)))
    expert_ids = jnp.arange(expert_count, dtype=jnp.int32)
    chosen_rows = jnp.any(routes[0][..., None] == expert_ids, axis=2).astype(jnp.bfloat16)
    chosen_shape = chosen_rows.shape
    few = jnp.concatenate([few, chosen_rows.reshape(-1, few.shape[1])], axis=0)
    both_out = outgoing_experts(w_gate[0], w_up[0], fsdp_count)
    matrix, few = gather_weights(sizes, matrix, few, 5)
    matrix, few, both_out = lax.optimization_barrier((matrix, few, both_out))
    gate_up = exchange(both_out).reshape(model_width, 2 * hidden)
    matrix = matrix.reshape(model_width, -1)
    chosen_rows = few[:, few_rows:].reshape((fsdp_count,) + chosen_shape)
    few = few[:, :few_rows].transpose(1, 0, 2).reshape(few_rows, model_width)
    w_qkv = matrix[:, :qkv_width]
    out_full = matrix[:, qkv_width:].reshape(-1, model_width)
    out_heads = out_full.reshape(-1, 1, HEAD_SIZE, model_width)
    out_twice = jnp.tile(out_heads, (1, LANES // HEAD_SIZE, 1, 1)).reshape(-1, model_width)
    router = jnp.tile(few[:expert_count].T, (1, copies))
    gain_one = few[expert_count].astype(jnp.float32)[None]
    gain_two = few[expert_count + 1].astype(jnp.float32)[None]
    down = w_down[0].reshape(hidden, model_width)
    lane = jnp.arange(LANES, dtype=jnp.int32)
    owner = jnp.arange(hidden, dtype=jnp.int32) // own_units
    match = (lane % expert_count)[:, None] == owner[None, :]
    spread_map = (match & (lane < 3 * expert_count)[:, None]).astype(jnp.bfloat16)
    pick_map = (match & (lane < 2 * expert_count)[:, None]).astype(jnp.bfloat16).T
    chosen_rows = jnp.tile(chosen_rows, (1, 1, 1, copies))
    segment_rows = segment_ids[:, 0, :]
    tick_count = micro_count + section_count - 1
    outputs = jnp.zeros((micro_count, local_rows, model_width), jnp.bfloat16)
    history = []
    layer_in = jnp.where(section_index == 0, inputs[0], jnp.zeros_like(inputs[0]))
    attn_in = begin_layer(sizes, layer_in, gain_one, 0)
    for tick_step in range(tick_count):
        mb_index = tick_step - section_index
        active = (mb_index >= 0) & (mb_index < micro_count)
        mb_pick = jnp.clip(mb_index, 0, micro_count - 1)
        segment = lax.dynamic_index_in_dim(segment_rows, mb_pick, 0, keepdims=False)
        chosen = lax.dynamic_index_in_dim(chosen_rows, mb_pick, 1, keepdims=False)
        partial, kept, mixed_heads = attention_forward(attn_in, segment, w_qkv, out_full)
        last = tick_step == tick_count - 1
        fresh = None if last else inputs[min(tick_step + 1, micro_count - 1)]
        weights = (router, gain_one, gain_two, gate_up, down, spread_map)
        made = moe_forward(
            sizes, partial, layer_in, chosen, weights, fresh, expert_count, 2 if last else 1
        )
        moe_in, pre, share, state, result = made[:5]
        history.append((attn_in, layer_in, kept, mixed_heads, moe_in, pre, share, state))
        outputs = jnp.where(
            active, lax.dynamic_update_index_in_dim(outputs, result, mb_pick, 0), outputs
        )
        if not last:
            layer_in, attn_in = made[5:]
    input_grads = jnp.zeros((micro_count, local_rows, model_width), jnp.float32)
    gain_sums = None
    all_terms = []
    arrived = None
    place = (lax.axis_index("fsdp"), lax.axis_index("tp") * local_rows, 0)
    for tick_step in range(tick_count):
        mb_index = micro_count + section_count - 2 - tick_step - section_index
        active = (mb_index >= 0) & (mb_index < micro_count)
        mb_pick = jnp.clip(mb_index, 0, micro_count - 1)
        upstream = out_grad[max(micro_count - 1 - tick_step, 0)].astype(jnp.float32)
        if arrived is None:
            arrived = jnp.zeros_like(upstream)
        upstream = jnp.where(
            section_index == section_count - 1, upstream, arrived.astype(jnp.float32)
        )
        upstream = jnp.where(active, upstream, jnp.zeros_like(upstream))
        attn_in, layer_in, kept, mixed_heads, moe_in, pre, share, state = history[tick_count - 1 - tick_step]
        last = tick_step == tick_count - 1
        both_sum, down_sum, logit_grad, gain_two_part, state_grad, attn_grad = moe_backward(
            sizes,
            upstream,
            state,
            share,
            pre,
            moe_in,
            (router, gain_two, gate_up, down, spread_map, pick_map),
            expert_count,
            None if tick_step == 0 else (both_sum, down_sum),
            last,
            7 if tick_step == 0 else 8 if last else 3,
        )
        if last:
            both_sum = exchange(both_sum.reshape(fsdp_count, depth, 2 * hidden))
        grad_out, gain_one_part, arrived, qkv_grad = end_layer(
            sizes, attn_grad, kept, out_twice, w_qkv, layer_in, state_grad, gain_one, 4
        )
        input_grads = jnp.where(
            active, lax.dynamic_update_index_in_dim(input_grads, grad_out, mb_pick, 0), input_grads
        )
        gains = (gain_one_part, gain_two_part)
        gain_sums = gains if gain_sums is None else tuple(a + b for a, b in zip(gain_sums, gains))
        own_rows = lax.dynamic_slice(moe_in, place, (1, local_rows, model_width))[0]
        all_terms.append(
            (
                active,
                (
                    (attn_in, qkv_grad),
                    (mixed_heads, attn_grad),
                    (logit_grad[:, :expert_count], own_rows),
                ),
            )
        )
    chosen_terms = []
    for first in range(micro_count):
        picked = all_terms[first][1]
        for active, terms in all_terms[first + micro_count :: micro_count]:
            picked = jax.tree.map(lambda a, b: jnp.where(active, b, a), picked, terms)
        chosen_terms.append(picked)
    qkv_pairs, output_pairs, router_pairs = zip(*chosen_terms)
    gate_shard, up_shard = incoming_experts(both_sum, expert_count, hidden_units)
    down_shard = down_sum.reshape(expert_count, own_units, model_width)
    small = jnp.concatenate([summed_product(router_pairs)] + list(gain_sums), axis=0)
    small = jnp.pad(small, ((0, few_rows - small.shape[0]), (0, 0)))
    matrix_grad = jnp.concatenate(
        [summed_product(qkv_pairs), summed_product(output_pairs).reshape(model_width, -1)], axis=1
    ).astype(jnp.bfloat16)
    down_sum, matrix_grad = lax.optimization_barrier((plain_copy(down_sum, 4), matrix_grad))
    matrix_grad, few_grad = reduce_weights(
        sizes, matrix_grad.reshape(fsdp_count, depth, -1), small, 6
    )
    shard_sums = (
        matrix_grad[:, :query_width],
        matrix_grad[:, query_width : query_width + key_width],
        matrix_grad[:, query_width + key_width : qkv_width],
        matrix_grad[:, qkv_width:].reshape(-1, model_width),
        few_grad[:expert_count].T,
        few_grad[expert_count],
        few_grad[expert_count + 1],
        gate_shard,
        up_shard,
        down_shard,
    )
    return (outputs[None], input_grads[None]) + tuple((part[None] for part in shard_sums))


def solution(mesh):
    in_specs = (
        P(None, ("fsdp", "tp"), None),
        P(None, "fsdp", None),
        P("section", None, "fsdp", None),
        P("section", "fsdp", "tp"),
        P("section", "fsdp", "tp"),
        P("section", "fsdp", "tp"),
        P("section", ("tp", "fsdp"), None),
        P("section", "fsdp", None),
        P("section", "fsdp"),
        P("section", "fsdp"),
        P("section", None, "fsdp", "tp"),
        P("section", None, "fsdp", "tp"),
        P("section", None, ("tp", "fsdp"), None),
        P(None, ("fsdp", "tp"), None),
    )
    out_specs = (
        P("section", None, ("fsdp", "tp"), None),
        P("section", None, ("fsdp", "tp"), None),
        P("section", "fsdp", "tp"),
        P("section", "fsdp", "tp"),
        P("section", "fsdp", "tp"),
        P("section", ("tp", "fsdp"), None),
        P("section", "fsdp", None),
        P("section", "fsdp"),
        P("section", "fsdp"),
        P("section", None, "fsdp", "tp"),
        P("section", None, "fsdp", "tp"),
        P("section", None, ("tp", "fsdp"), None),
    )
    sizes = tuple(mesh.shape[axis] for axis in ("section", "fsdp", "tp"))
    return jax.shard_map(
        functools.partial(per_device, sizes), mesh=mesh, in_specs=in_specs, out_specs=out_specs, check_vma=False
    )
```

```python
import functools

import jax
import jax.numpy as jnp
from jax import lax
from jax.experimental import pallas as pl
from jax.experimental.pallas import tpu as pltpu
from jax.sharding import PartitionSpec as P

QUERY_HEADS = 16
KEY_VALUE_HEADS = 8
HEAD_SIZE = 64


norm_eps = 1e-06
branch_scale = 0.22
score_scale = 0.015625
rope_base = 10000.0
masked_score = -1e30


def norm_rows(vectors, gain_vec):
    inverse = lax.rsqrt(jnp.mean(vectors * vectors, axis=-1, keepdims=True) + norm_eps)
    normed = vectors * inverse
    return (normed * gain_vec, normed, inverse)


def norm_back(upstream, normed, inverse, gain_vec):
    scaled_grad = upstream * gain_vec
    gain_grad = jnp.sum(upstream * normed, axis=0, keepdims=True)
    inner_mean = jnp.mean(scaled_grad * normed, axis=-1, keepdims=True)
    return (inverse * (scaled_grad - normed * inner_mean), gain_grad)


def rope_tables(permitted_mask):
    offsets = (jnp.sum(permitted_mask.astype(jnp.int32), axis=1) - 1).astype(jnp.float32)
    half_dim = HEAD_SIZE // 2
    frequency = rope_base ** (-(jnp.arange(half_dim, dtype=jnp.float32) * 2.0 / HEAD_SIZE))
    angles = offsets[:, None] * frequency[None, :]
    return (jnp.cos(angles)[:, None, :], jnp.sin(angles)[:, None, :])


def rotate(vectors, cosine, sine):
    half_dim = vectors.shape[-1] // 2
    front_half = vectors[..., :half_dim]
    back_half = vectors[..., half_dim:]
    return jnp.concatenate(
        [front_half * cosine - back_half * sine, back_half * cosine + front_half * sine], axis=-1
    )


def allowed_pairs(segment):
    position = jnp.arange(segment.shape[0], dtype=jnp.int32)
    return (segment[:, None] == segment[None, :]) & (position[None, :] <= position[:, None])


def attend(query_rows, key_matrix, value_matrix, permitted_mask):
    scores = (
        jnp.einsum("qhgd,khd->hgqk", query_rows, key_matrix, preferred_element_type=jnp.float32)
        * score_scale
    )
    scores = jnp.where(permitted_mask[None, None], scores, masked_score)
    row_max = jnp.max(scores, axis=-1, keepdims=True)
    log_sum_exp = row_max + jnp.log(jnp.sum(jnp.exp(scores - row_max), axis=-1, keepdims=True))
    weights_low = jnp.exp(scores - log_sum_exp).astype(jnp.bfloat16)
    attended = jnp.einsum(
        "hgqk,khd->qhgd", weights_low, value_matrix, preferred_element_type=jnp.float32
    )
    return attended.astype(jnp.bfloat16)


MESH = pl.DeviceIdType.MESH
LANES = 128
VMEM_LIMIT = 60 * 1024 * 1024
WHOLE_VMEM = pl.BlockSpec(memory_space=pltpu.VMEM)


def flipped(index, bit):
    step = 1 << bit
    return index + step - 2 * step * lax.rem(lax.div(index, step), 2)


def crossed(index, mask, bits):
    for bit in range(bits):
        if (mask >> bit) & 1:
            index = flipped(index, bit)
    return index


class Team:
    def __init__(self, sizes):
        self.sections, self.fsdp, self.tp = sizes
        self.bits = self.tp.bit_length() - 1
        assert 1 << self.bits == self.tp
        self.s = lax.axis_index("section")
        self.f = lax.axis_index("fsdp")
        self.t = lax.axis_index("tp")
        self.hops = [
            (bit, mask)
            for bit in reversed(range(self.bits))
            for mask in range(0, self.tp, 2 << bit)
        ]
        self.place = {hop: number for number, hop in enumerate(self.hops)}

    def row(self, i):
        above = self.fsdp - 1 - self.f
        short = jnp.minimum(self.f, above)
        paired = i <= 2 * short
        distance = jnp.where(paired, lax.div(i + 1, 2), i - short)
        upward = jnp.where(paired, lax.rem(i, 2) == 1, self.f < above)
        return jnp.where(upward, self.f + distance, self.f - distance)

    def column(self, mask):
        return crossed(self.t, mask, self.bits)


def greet(team, fsdp, section_step):
    barrier = pltpu.get_barrier_semaphore()
    count = 0
    if fsdp:
        for i in range(1, team.fsdp):
            pl.semaphore_signal(
                barrier,
                inc=1,
                device_id={"fsdp": lax.rem(team.f + i, team.fsdp)},
                device_id_type=MESH,
            )
            count += 1
    for bit in range(team.bits):
        pl.semaphore_signal(
            barrier, inc=1, device_id={"tp": flipped(team.t, bit)}, device_id_type=MESH
        )
        count += 1
    if section_step:
        behind = lax.rem(team.s + team.sections - section_step, team.sections)
        pl.semaphore_signal(
            barrier, inc=1, device_id={"section": behind}, device_id_type=MESH
        )
        count += 1
    pl.semaphore_wait(barrier, count)


def rows_of(block, size):
    return pl.ds(pl.multiple_of(block * size, size), size)


SLICES = 2


def slice_of(block, size, part):
    share = size // SLICES
    return pl.ds(pl.multiple_of(block * size + part * share, share), share)


class TpGather:
    def __init__(self, team, ref, size, sends, recvs, part):
        self.team, self.ref, self.size, self.part = team, ref, size, part
        self.sends = lambda place: sends(place * SLICES + part)
        self.recvs = lambda place: recvs(place * SLICES + part)

    def copy(self, hop, arriving):
        bit, mask = hop
        team = self.team
        block = team.column(mask | ((1 << bit) if arriving else 0))
        part = self.ref.at[slice_of(block, self.size, self.part)]
        return pltpu.make_async_remote_copy(
            src_ref=part,
            dst_ref=part,
            send_sem=self.sends(team.place[hop]),
            recv_sem=self.recvs(team.place[hop]),
            device_id={"tp": flipped(team.t, bit)},
            device_id_type=MESH,
        )

    def begin(self):
        for bit in reversed(range(self.team.bits)):
            self.copy((bit, 0), False).start()

    def relay(self):
        for hop in self.team.hops:
            bit, mask = hop
            if bit:
                self.copy(hop, True).wait_recv()
                for lower in reversed(range(bit)):
                    self.copy((lower, mask | (1 << bit)), False).start()

    def arrive(self):
        for hop in self.team.hops:
            if hop[0] == 0:
                self.copy(hop, True).wait_recv()

    def drain(self):
        for hop in self.team.hops:
            self.copy(hop, False).wait_send()


def add_blocks(target, rows, other, width, experts):
    wide = target[rows, :width].astype(jnp.float32) + other[:, :width].astype(jnp.float32)
    target[rows, :width] = wide.astype(target.dtype)
    if target.shape[1] > width:
        both = target[rows, width:].astype(jnp.float32) + other[:, width:].astype(jnp.float32)
        target[rows, width:] = two_parts(both, experts)


def two_parts(both, experts):
    lane = lax.broadcasted_iota(jnp.int32, both.shape, 1)
    first = lane < experts
    full = both + jnp.where(
        first, pltpu.roll(both, LANES - experts, 1), pltpu.roll(both, experts, 1)
    )
    return parted(full, first, lane < 2 * experts)


def parted(full, first, second):
    high = full.astype(jnp.bfloat16)
    low = (full - high.astype(jnp.float32)).astype(jnp.bfloat16)
    zero = jnp.zeros_like(high)
    return jnp.where(first, high, jnp.where(second, low, zero))


class TpScatter:
    def __init__(self, team, ref, size, landing, sends, recvs, width, experts, part):
        share = size // SLICES
        self.team, self.ref, self.size, self.part = team, ref, size, part
        self.landing = lambda place: landing(place).at[pl.ds(part * share, share)]
        self.sends = lambda place: sends(place * SLICES + part)
        self.recvs = lambda place: recvs(place * SLICES + part)
        self.width, self.experts = width, experts

    def copy(self, hop):
        bit, mask = hop
        team = self.team
        block = team.column(mask | (1 << bit))
        return pltpu.make_async_remote_copy(
            src_ref=self.ref.at[slice_of(block, self.size, self.part)],
            dst_ref=self.landing(team.place[hop]),
            send_sem=self.sends(team.place[hop]),
            recv_sem=self.recvs(team.place[hop]),
            device_id={"tp": flipped(team.t, bit)},
            device_id_type=MESH,
        )

    def send(self, bit):
        for hop in self.team.hops:
            if hop[0] == bit:
                self.copy(hop).start()

    def add(self, bit):
        for hop in self.team.hops:
            if hop[0] == bit:
                self.copy(hop).wait_recv()
                add_blocks(
                    self.ref,
                    slice_of(self.team.column(hop[1]), self.size, self.part),
                    self.landing(self.team.place[hop]),
                    self.width,
                    self.experts,
                )

    def drain(self):
        for hop in self.team.hops:
            self.copy(hop).wait_send()


def gather_all(team, ref, size, sends, recvs):
    slices = [
        TpGather(team, ref, size, lambda p: sends.at[p], lambda p: recvs.at[p], part)
        for part in range(SLICES)
    ]
    for phase in ("begin", "relay", "arrive", "drain"):
        for one in slices:
            getattr(one, phase)()


def scatter_all(team, ref, size, landing, sends, recvs, width):
    slices = [
        TpScatter(
            team, ref, size, lambda p: landing.at[p], lambda p: sends.at[p], lambda p: recvs.at[p], width, 0, part
        )
        for part in range(SLICES)
    ]
    for one in slices:
        one.send(0)
    for bit in range(team.bits):
        for one in slices:
            one.add(bit)
            if bit + 1 < team.bits:
                one.send(bit + 1)
    return slices


def ring_copy(team, step, source, target, sends, recvs):
    ahead = lax.rem(team.s + team.sections + step, team.sections)
    return pltpu.make_async_remote_copy(
        src_ref=source,
        dst_ref=target,
        send_sem=sends.at[0],
        recv_sem=recvs.at[0],
        device_id={"section": ahead},
        device_id_type=MESH,
    )


def group_exchange(
    team, gathered, partial, landing, across, sems, size, width, experts, prepare, first, second, spare=None,
    gathering=True, reducing=True,
):
    ag_send, ag_recv, agz_send, agz_recv, rs_send, rs_recv, rsz_send, rsz_recv = sems
    count = team.fsdp

    def gather(i, part):
        return TpGather(
            team,
            gathered.at[team.row(i)],
            size,
            lambda place: ag_send.at[i, place],
            lambda place: ag_recv.at[i, place],
            part,
        )

    def scatter(i, part):
        return TpScatter(
            team,
            partial.at[team.row(i)],
            size,
            lambda place: landing.at[i, place],
            lambda place: rs_send.at[i, place],
            lambda place: rs_recv.at[i, place],
            width,
            experts,
            part,
        )

    parts = range(SLICES)
    share = size // SLICES

    def gather_across(i, part, arriving):
        source = team.row(i) if arriving else team.f
        block = gathered.at[source, slice_of(team.t, size, part)]
        return pltpu.make_async_remote_copy(
            src_ref=block,
            dst_ref=block,
            send_sem=agz_send.at[i, part],
            recv_sem=agz_recv.at[source, part],
            device_id={"fsdp": team.row(i)},
            device_id_type=MESH,
        )

    def scatter_across(i, part, arriving):
        source = team.row(i) if arriving else team.f
        return pltpu.make_async_remote_copy(
            src_ref=partial.at[team.row(i), slice_of(team.t, size, part)],
            dst_ref=across.at[source, pl.ds(part * share, share)],
            send_sem=rsz_send.at[i, part],
            recv_sem=rsz_recv.at[source, part],
            device_id={"fsdp": team.row(i)},
            device_id_type=MESH,
        )

    def relay_across(i):
        for part in parts:
            gather_across(i, part, True).wait_recv()
            gather(i, part).begin()

    if gathering:
        for part in parts:
            gather(0, part).begin()
        for i in range(1, min(count, 3)):
            for part in parts:
                gather_across(i, part, False).start()
        for part in parts:
            gather(0, part).relay()
        for i in range(3, count):
            for part in parts:
                gather_across(i, part, False).start()
    prepare()
    if gathering and count > 1:
        relay_across(1)

    def sum_stages(i):
        for bit in range(team.bits):
            done = i - 1 - bit

            @pl.when((done >= min(bit, 1)) & (done < count))
            def _():
                for part in parts:
                    scatter(done, part).add(bit)

                    @pl.when(done > 0)
                    def _():
                        if bit + 1 < team.bits:
                            scatter(done, part).send(bit + 1)
                        else:
                            scatter_across(done, part, False).start()

    def step(i, carry):
        @pl.when(i < count)
        def _():
            if gathering:
                for part in parts:
                    gather(i, part).arrive()
            first(team.row(i))

        if gathering:

            @pl.when(i + 2 < count)
            def _():
                relay_across(i + 2)

        if reducing:
            sum_stages(i)

        if gathering:

            @pl.when(i + 1 < count)
            def _():
                for part in parts:
                    gather(i + 1, part).relay()

        if reducing:

            @pl.when(i < count)
            def _():
                second(team.row(i))
                for part in parts:
                    scatter(i, part).send(0)

            if team.bits > 1:

                @pl.when(i == count)
                def _():
                    for part in parts:
                        scatter(0, part).send(1)

        if spare is not None:

            @pl.when(i >= count)
            def _():
                spare(i - count)

        return carry

    lax.fori_loop(0, count + (team.bits if reducing else 0), step, 0)

    def finish(i, carry):
        for part in parts:
            if gathering:
                gather_across(i, part, False).wait_send()
            if reducing:
                scatter_across(i, part, False).wait_send()
        return carry

    def settle(i, carry):
        for part in parts:
            if gathering:
                gather(i, part).drain()
            if reducing:
                scatter(i, part).drain()
        return carry

    if not reducing:
        lax.fori_loop(1, count, finish, 0)
        lax.fori_loop(0, count, settle, 0)
        return None, None
    for bit in range(1, team.bits):
        for part in parts:
            scatter(0, part).add(bit)
            if bit + 1 < team.bits:
                scatter(0, part).send(bit + 1)
    if spare is not None:
        spare(team.bits)

    total = partial[team.f, rows_of(team.t, size)].astype(jnp.float32)
    for i in range(1, count):
        for part in parts:
            scatter_across(i, part, True).wait_recv()
        total = total + across[team.row(i)].astype(jnp.float32)
    lax.fori_loop(1, count, finish, 0)
    lax.fori_loop(0, count, settle, 0)
    return total[:, :width], (total[:, width:] if total.shape[1] > width else None)


def group_sems(team_sizes):
    _, fsdp, tp = team_sizes
    dma = pltpu.SemaphoreType.DMA
    return [
        dma((fsdp, SLICES * tp)), dma((fsdp, SLICES * tp)), dma((fsdp, SLICES)), dma((fsdp, SLICES)),
        dma((fsdp, SLICES * tp)), dma((fsdp, SLICES * tp)), dma((fsdp, SLICES)), dma((fsdp, SLICES)),
    ]


def moe_gather(sizes, partial_out, residual, gain_two, number):
    sections, fsdp, tp = sizes
    rows, width = residual.shape
    band = tp * rows
    bf16, f32 = jnp.bfloat16, jnp.float32
    dma = pltpu.SemaphoreType.DMA

    def kernel(part_ref, res_ref, two_ref, all_hbm, state_ref, sums, sums_in, all_ref, tr_send, tr_recv, all_sem, *sems):
        team = Team(sizes)

        def all_out(row):
            return pltpu.make_async_copy(all_ref.at[row], all_hbm.at[row], all_sem.at[row])

        sums[...] = part_ref[...]
        greet(team, True, 0)
        reduce = scatter_all(team, sums, rows, sums_in, tr_send, tr_recv, width)
        state = res_ref[...].astype(f32) + branch_scale * sums[rows_of(team.t, rows)].astype(f32)
        state_ref[...] = state
        scaled, _, _ = norm_rows(state, two_ref[...])
        all_ref[team.f, rows_of(team.t, rows)] = scaled.astype(bf16)
        group_exchange(
            team, all_ref, None, None, None, sems, rows, width, 0,
            lambda: None, lambda row: all_out(row).start(), None, reducing=False,
        )
        for one in reduce:
            one.drain()
        for row in range(fsdp):
            all_out(row).wait()

    return pl.pallas_call(
        kernel,
        out_shape=[
            jax.ShapeDtypeStruct((fsdp, band, width), bf16),
            jax.ShapeDtypeStruct((rows, width), f32),
        ],
        in_specs=[WHOLE_VMEM] * 3,
        out_specs=[pl.BlockSpec(memory_space=pl.ANY), WHOLE_VMEM],
        scratch_shapes=[
            pltpu.VMEM((band, width), bf16),
            pltpu.VMEM((tp, rows, width), bf16),
            pltpu.VMEM((fsdp, band, width), bf16),
            dma((SLICES * tp,)), dma((SLICES * tp,)), dma((fsdp,)),
        ]
        + group_sems(sizes),
        compiler_params=comm_params(number),
        name="moe_gather",
    )(partial_out, residual, gain_two)


def share_parts(share, experts):
    lane = lax.broadcasted_iota(jnp.int32, share.shape, 1)
    high = share.astype(jnp.bfloat16)
    rest = share - high.astype(jnp.float32)
    middle = rest.astype(jnp.bfloat16)
    low = (rest - middle.astype(jnp.float32)).astype(jnp.bfloat16)
    zero = jnp.zeros_like(high)
    return jnp.where(
        lane < experts,
        high,
        jnp.where(lane < 2 * experts, middle, jnp.where(lane < 3 * experts, low, zero)),
    )


def chunks(length, body, size=1024):
    size = min(size, length)

    def step(c, carry):
        body(pl.multiple_of(c * size, size), size)
        return carry

    lax.fori_loop(0, length // size, step, 0)


def product(left, right):
    return jnp.dot(left, right, preferred_element_type=jnp.float32)


def product_turned(left, right):
    return lax.dot_general(
        left, right, (((1,), (1,)), ((), ())), preferred_element_type=jnp.float32
    )


def product_over_rows(left, right):
    return lax.dot_general(
        left, right, (((0,), (0,)), ((), ())), preferred_element_type=jnp.float32
    )


def comm_params(number):
    return pltpu.CompilerParams(
        collective_id=number, has_side_effects=True, vmem_limit_bytes=VMEM_LIMIT
    )


def begin_layer(sizes, layer_in, gain, number):
    rows, width = layer_in.shape
    tp = sizes[2]

    def kernel(in_ref, gain_ref, out_ref, sends, recvs):
        team = Team(sizes)
        greet(team, False, 0)
        scaled, _, _ = norm_rows(in_ref[...].astype(jnp.float32), gain_ref[...])
        out_ref[rows_of(team.t, rows)] = scaled.astype(jnp.bfloat16)
        gather_all(team, out_ref, rows, sends, recvs)

    return pl.pallas_call(
        kernel,
        out_shape=jax.ShapeDtypeStruct((tp * rows, width), jnp.bfloat16),
        in_specs=[WHOLE_VMEM] * 2,
        out_specs=WHOLE_VMEM,
        scratch_shapes=[pltpu.SemaphoreType.DMA((SLICES * tp,)), pltpu.SemaphoreType.DMA((SLICES * tp,))],
        compiler_params=comm_params(number),
    )(layer_in, gain)


def moe_forward(sizes, partial_out, residual, chosen, weights, fresh, experts, ready, number):
    router, gain_one, gain_two, gate_up, down, spread_map = weights
    sections, fsdp, tp = sizes
    rows, width = residual.shape
    band = tp * rows
    hidden = down.shape[0]
    copies = LANES // experts
    tail = fresh is not None
    bf16, f32 = jnp.bfloat16, jnp.float32
    shapes = [
        jax.ShapeDtypeStruct((fsdp, band, width), bf16),
        jax.ShapeDtypeStruct((fsdp, band, 2 * hidden), bf16),
        jax.ShapeDtypeStruct((fsdp, band, LANES), f32),
        jax.ShapeDtypeStruct((rows, width), f32),
        jax.ShapeDtypeStruct((rows, width), bf16),
    ]
    if ready:
        shapes = shapes[1:3] + shapes[4:]
    if tail:
        shapes += [
            jax.ShapeDtypeStruct((rows, width), bf16),
            jax.ShapeDtypeStruct((band, width), bf16),
        ]
    dma = pltpu.SemaphoreType.DMA
    scratch = [
        pltpu.VMEM((band, width), bf16),
        pltpu.VMEM((tp, rows, width), bf16),
        pltpu.VMEM((fsdp, band, width), bf16),
        pltpu.VMEM((fsdp, tp - 1, rows, width), bf16),
        pltpu.VMEM((fsdp, rows, width), bf16),
        pltpu.VMEM((band, hidden), bf16),
        pltpu.VMEM((band, LANES), bf16),
        pltpu.VMEM((rows, width), bf16),
        pltpu.VMEM((width, 2 * hidden), bf16),
        pltpu.VMEM((hidden, width), bf16),
        pltpu.VMEM((fsdp, band, width), bf16),
        pltpu.VMEM((fsdp, band, 2 * hidden), bf16),
        dma((SLICES * tp,)), dma((SLICES * tp,)), dma((SLICES * tp,)), dma((SLICES * tp,)), dma((1,)), dma((1,)),
        dma((2,)), dma((fsdp,)), dma((fsdp,)),
    ] + group_sems(sizes)
    own, out = WHOLE_VMEM, pl.BlockSpec(memory_space=pl.ANY)

    def kernel(*refs):
        part_ref, res_ref, chosen_ref, router_ref, one_ref, two_ref, both_hbm, down_hbm, map_ref = refs[:9]
        refs = refs[9:]
        if tail:
            fresh_ref, refs = refs[0], refs[1:]
        if ready:
            all_hbm, state_ref = part_ref, res_ref
            pre_hbm, share_ref, result_ref = refs[:3]
            refs = refs[3:]
        else:
            all_hbm, pre_hbm, share_ref, state_ref, result_ref = refs[:5]
            refs = refs[5:]
        if tail:
            next_ref, attn_ref = refs[:2]
            refs = refs[2:]
        sums, sums_in, partial, landing, across, weighted, parts, moved = refs[:8]
        both_ref, down_ref, all_ref, pre_ref = refs[8:12]
        tr_send, tr_recv, tg_send, tg_recv, sec_send, sec_recv, load_sem, all_sem, pre_sem = refs[12:21]
        sems = refs[21:]
        team = Team(sizes)
        loads = [
            pltpu.make_async_copy(both_hbm, both_ref, load_sem.at[0]),
            pltpu.make_async_copy(down_hbm, down_ref, load_sem.at[1]),
        ]
        for load in loads:
            load.start()

        def all_out(row):
            if ready:
                return pltpu.make_async_copy(all_hbm.at[row], all_ref.at[row], all_sem.at[row])
            return pltpu.make_async_copy(all_ref.at[row], all_hbm.at[row], all_sem.at[row])

        def pre_out(row):
            return pltpu.make_async_copy(pre_ref.at[row], pre_hbm.at[row], pre_sem.at[row])

        def prepare():
            for load in loads:
                load.wait()
            if ready:
                for row in range(fsdp):
                    all_out(row).wait()

        if ready:
            for row in range(fsdp):
                all_out(row).start()
        else:
            sums[...] = part_ref[...]
        greet(team, True, 1 if tail else 0)
        reduce = []
        if not ready:
            reduce = scatter_all(team, sums, rows, sums_in, tr_send, tr_recv, width)
            state = res_ref[...].astype(f32) + branch_scale * sums[rows_of(team.t, rows)].astype(f32)
            state_ref[...] = state
            scaled, _, _ = norm_rows(state, two_ref[...])
            all_ref[team.f, rows_of(team.t, rows)] = scaled.astype(bf16)

        def first(row):
            if not ready:
                all_out(row).start()
            logits = product(all_ref[row], router_ref[...])
            logits = jnp.where(chosen_ref[row].astype(f32) > 0.5, logits, masked_score)
            grown = jnp.exp(logits - jnp.max(logits, axis=-1, keepdims=True))
            total = jnp.sum(grown, axis=-1, keepdims=True) * (1.0 / copies)
            share = grown / total
            share_ref[row] = share
            parts[...] = share_parts(share, experts)

            def piece(start, size):
                here, there = pl.ds(start, size), pl.ds(pl.multiple_of(hidden + start, size), size)
                gate = product(all_ref[row], both_ref[:, here])
                up = product(all_ref[row], both_ref[:, there])
                pre_ref[row, :, here] = gate.astype(bf16)
                pre_ref[row, :, there] = up.astype(bf16)
                wide = product(parts[...], map_ref[:, here])
                weighted[:, here] = (wide * (gate * jax.nn.sigmoid(gate) * up)).astype(bf16)

            chunks(hidden, piece)
            pre_out(row).start()

        def second(row):
            def piece(start, size):
                here = pl.ds(start, size)
                partial[row, :, here] = product(weighted[...], down_ref[:, here]).astype(bf16)

            chunks(width, piece)

        total, _ = group_exchange(
            team, all_ref, partial, landing, across, sems, rows, width, experts, prepare, first, second,
            gathering=not ready,
        )
        result_ref[...] = (state_ref[...] + branch_scale * total).astype(bf16)
        for one in reduce:
            one.drain()
        if tail:
            move = ring_copy(team, 1, result_ref, moved, sec_send, sec_recv)
            move.start()
            move.wait_recv()
            layer_in = jnp.where(team.s == 0, fresh_ref[...], moved[...])
            next_ref[...] = layer_in
            scaled, _, _ = norm_rows(layer_in.astype(f32), one_ref[...])
            attn_ref[rows_of(team.t, rows)] = scaled.astype(bf16)
            gather_all(team, attn_ref, rows, tg_send, tg_recv)
            move.wait_send()
        for row in range(fsdp):
            if not ready:
                all_out(row).wait()
            pre_out(row).wait()

    args = [partial_out, residual, chosen, router, gain_one, gain_two, gate_up, down, spread_map]
    if tail:
        args.append(fresh)
    return pl.pallas_call(
        kernel,
        out_shape=shapes,
        in_specs=[out if ready else own] + [own] * 5 + [out] * 2 + [own] * (len(args) - 8),
        out_specs=[out] * (1 if ready else 2) + [own] * (len(shapes) - (1 if ready else 2)),
        scratch_shapes=scratch,
        compiler_params=comm_params(number),
        name="moe_forward",
    )(*args)


def moe_backward(sizes, upstream, state, share, pre, moe_in, weights, experts, sums, final, number):
    router, gain_two, gate_up, down, spread_map, pick_map = weights
    sections, fsdp, tp = sizes
    rows, width = upstream.shape
    band = tp * rows
    hidden = down.shape[0]
    bf16, f32 = jnp.bfloat16, jnp.float32
    leaving = bf16 if final else f32
    shapes = [
        jax.ShapeDtypeStruct((width, 2 * hidden), leaving),
        jax.ShapeDtypeStruct((hidden, width), f32),
        jax.ShapeDtypeStruct((rows, LANES), bf16),
        jax.ShapeDtypeStruct((1, width), f32),
        jax.ShapeDtypeStruct((rows, width), f32),
        jax.ShapeDtypeStruct((band, width), bf16),
    ]
    dma = pltpu.SemaphoreType.DMA
    wider = width + LANES
    both_units = team_units(tp)
    both_step = 2 * hidden // both_units
    loops = [both_step // chunk_size(both_step), width // chunk_size(width)]
    both_size, down_size = chunk_size(both_step), chunk_size(width)
    scratch = [
        pltpu.VMEM((fsdp, band, wider), bf16),
        pltpu.VMEM((fsdp, tp - 1, rows, wider), bf16),
        pltpu.VMEM((fsdp, rows, wider), bf16),
        pltpu.VMEM((band, LANES), bf16),
        pltpu.VMEM((band, LANES), f32),
        pltpu.VMEM((width, 2 * hidden), bf16),
        pltpu.VMEM((hidden, width), bf16),
        pltpu.VMEM((fsdp, band, 2 * hidden), bf16),
        pltpu.VMEM((fsdp, band, width), bf16),
        pltpu.VMEM((fsdp, band, 2 * hidden), bf16),
        pltpu.VMEM((fsdp, band, hidden), bf16),
        pltpu.VMEM((fsdp, band, width), bf16),
        pltpu.VMEM((width, 2 * hidden), f32),
        pltpu.VMEM((hidden, width), f32),
        pltpu.VMEM((width, 2 * hidden) if final else (16, LANES), bf16),
        dma((SLICES * tp,)), dma((SLICES * tp,)), dma((5,)), dma((fsdp,)), dma((2,)),
    ] + group_sems(sizes)
    own, out = WHOLE_VMEM, pl.BlockSpec(memory_space=pl.ANY)
    adding = sums is not None

    def kernel(*refs):
        up_ref, state_ref, share_ref, pre_hbm, router_ref, gain_ref, both_hbm, down_hbm, map_ref, pick_ref, in_hbm = refs[:11]
        refs = refs[11:]
        if adding:
            both_old, down_old = refs[:2]
            refs = refs[2:]
        both_out, down_out, logit_ref, gain_out, state_out, attn_ref = refs[:6]
        partial, landing, across, parts, share_sum, both_ref, down_ref, pre_ref, all_ref, grad_ref, weighted_ref = refs[6:17]
        in_ref, both_sum, down_sum, both_low, tg_send, tg_recv, load_sem, pre_sem, out_sem = refs[17:26]
        sems = refs[26:]
        team = Team(sizes)
        loads = [
            pltpu.make_async_copy(down_hbm, down_ref, load_sem.at[0]),
            pltpu.make_async_copy(both_hbm, both_ref, load_sem.at[1]),
        ]
        later = [pltpu.make_async_copy(in_hbm, in_ref, load_sem.at[2])]
        if adding:
            later += [
                pltpu.make_async_copy(both_old, both_sum, load_sem.at[3]),
                pltpu.make_async_copy(down_old, down_sum, load_sem.at[4]),
            ]
        outs = [
            pltpu.make_async_copy(both_low if final else both_sum, both_out, out_sem.at[0]),
            pltpu.make_async_copy(down_sum, down_out, out_sem.at[1]),
        ]

        def pre_in(row):
            return pltpu.make_async_copy(pre_hbm.at[row], pre_ref.at[row], pre_sem.at[row])

        loads[0].start()
        for i in range(fsdp):
            pre_in(i).start()
        loads[1].start()
        for load in later:
            load.start()

        def prepare():
            for load in loads:
                load.wait()
            for i in range(fsdp):
                pre_in(i).wait()

        def spare(unit):
            @pl.when(unit == 0)
            def _():
                for load in later:
                    load.wait()

            if isinstance(unit, int):
                left, right, total, size = weighted_ref, all_ref, down_sum, down_size
                start, count = 0, loops[1]
            else:
                left, right, total, size = in_ref, grad_ref, both_sum, both_size
                start, count = unit * both_step, loops[0]

            def turn(c, carry):
                here = pl.ds(pl.multiple_of(start + c * size, size), size)
                made = lax.dot_general(
                    left[...].reshape(fsdp * band, left.shape[2]),
                    right[:, :, here].reshape(fsdp * band, size),
                    (((0,), (0,)), ((), ())),
                    preferred_element_type=f32,
                )
                if adding:
                    made = made + total[:, here]
                if final and total is both_sum:
                    both_low[:, here] = made.astype(bf16)
                else:
                    total[:, here] = made
                return carry

            lax.fori_loop(0, count, turn, 0)
            if isinstance(unit, int):
                for done in outs:
                    done.start()

        greet(team, True, 0)
        all_ref[team.f, rows_of(team.t, rows)] = (branch_scale * up_ref[...]).astype(bf16)

        def first(row):
            parts[...] = share_parts(share_ref[row], experts)
            share_sum[...] = jnp.zeros_like(share_sum)

            def piece(start, size):
                here, there = pl.ds(start, size), pl.ds(pl.multiple_of(hidden + start, size), size)
                hidden_grad = product_turned(all_ref[row], down_ref[here])
                gate = pre_ref[row, :, here].astype(f32)
                up = pre_ref[row, :, there].astype(f32)
                wide = product(parts[...], map_ref[:, here])
                sigmoid_gate = jax.nn.sigmoid(gate)
                swish = gate * sigmoid_gate
                value = swish * up
                weighted_ref[row, :, here] = (wide * value).astype(bf16)
                both = hidden_grad * value
                high = both.astype(bf16)
                low = (both - high.astype(f32)).astype(bf16)
                share_sum[...] += product(high, pick_ref[here]) + product(low, pick_ref[here])
                scaled = wide * hidden_grad
                grad_ref[row, :, here] = (
                    scaled * up * sigmoid_gate * (1.0 + gate * (1.0 - sigmoid_gate))
                ).astype(bf16)
                grad_ref[row, :, there] = (scaled * swish).astype(bf16)

            chunks(hidden, piece)

        def second(row):
            def piece(start, size):
                here = pl.ds(start, size)
                partial[row, :, here] = product_turned(grad_ref[row], both_ref[here]).astype(bf16)

            chunks(width, piece)
            lane = lax.broadcasted_iota(jnp.int32, (band, LANES), 1)
            partial[row, :, width:] = parted(share_sum[...], lane < experts, lane < 2 * experts)

        total, extra = group_exchange(
            team, all_ref, partial, landing, across, sems, rows, width, experts, prepare, first, second, spare
        )
        lane = lax.broadcasted_iota(jnp.int32, (rows, LANES), 1)
        valid = lane < experts
        share_grad = extra + pltpu.roll(extra, LANES - experts, 1)
        own_share = jnp.where(valid, share_ref[team.f, rows_of(team.t, rows)], 0.0)
        inner = jnp.sum(own_share * share_grad, axis=-1, keepdims=True)
        logit_grad = (own_share * (share_grad - inner)).astype(bf16)
        logit_ref[...] = logit_grad
        norm_grad = total + product_turned(logit_grad, router_ref[...])
        _, normed, inverse = norm_rows(state_ref[...], gain_ref[...])
        back, gain_grad = norm_back(norm_grad, normed, inverse, gain_ref[...])
        gain_out[...] = gain_grad
        state_grad = up_ref[...] + back
        state_out[...] = state_grad
        attn_ref[rows_of(team.t, rows)] = (branch_scale * state_grad).astype(bf16)
        gather_all(team, attn_ref, rows, tg_send, tg_recv)
        for done in outs:
            done.wait()

    args = [upstream, state, share, pre, router, gain_two, gate_up, down, spread_map, pick_map, moe_in]
    if adding:
        args += list(sums)
    return pl.pallas_call(
        kernel,
        out_shape=shapes,
        in_specs=[own] * 3 + [out] + [own] * 2 + [out] * 2 + [own] * 2 + [out] * (len(args) - 10),
        out_specs=[out] * 2 + [own] * 4,
        scratch_shapes=scratch,
        compiler_params=comm_params(number),
        name="moe_backward",
    )(*args)


def team_units(tp):
    return tp.bit_length() - 1


def chunk_size(length, most=512):
    return min(length, most)


def end_layer(sizes, attn_grad, kept, out_twice, w_qkv, layer_in, state_grad, gain, number):
    queries, keys, values, bias, turn = kept
    tp = sizes[2]
    rows, width = layer_in.shape
    band = tp * rows
    kv_heads = keys.shape[1] // LANES
    each = queries.shape[1] // keys.shape[1]
    qkv_width = w_qkv.shape[1]
    query_width = queries.shape[1] * HEAD_SIZE // LANES
    key_width = keys.shape[1] * HEAD_SIZE // LANES
    held = LANES // HEAD_SIZE
    bf16, f32 = jnp.bfloat16, jnp.float32
    dma = pltpu.SemaphoreType.DMA

    def kernel(
        attn_ref, q_ref, k_ref, v_ref, bias_ref, turn_ref, twice_ref, qkv_ref, in_ref, grad_ref, gain_ref,
        out_ref, gain_out, arrived_ref, made_ref,
        heads, sums, sums_in, leaving, tr_send, tr_recv, sec_send, sec_recv,
    ):
        team = Team(sizes)
        barrier = pltpu.get_barrier_semaphore()
        for bit in range(team.bits):
            pl.semaphore_signal(
                barrier, inc=1, device_id={"tp": flipped(team.t, bit)}, device_id_type=MESH
            )
        pl.semaphore_signal(
            barrier,
            inc=1,
            device_id={"section": lax.rem(team.s + 1, team.sections)},
            device_id_type=MESH,
        )
        heads[...] = product_turned(attn_ref[...], twice_ref[...]).astype(bf16)
        lane = lax.broadcasted_iota(jnp.int32, (band, LANES), 1)
        turning = turn_ref[...]

        def turned_back(array):
            array = array * turning
            return array + pltpu.roll(array, HEAD_SIZE, 1)

        def place(start, parts):
            for number in range(0, len(parts), held):
                block = parts[number]
                for other in range(1, held):
                    block = jnp.where(lane < other * HEAD_SIZE, block, parts[number + other])
                where = start + number * HEAD_SIZE
                made_ref[:, where : where + LANES] = block.astype(bf16)

        def lanes_of(number):
            return slice(number * LANES, (number + 1) * LANES)

        query_parts, key_parts, value_parts = [], [], []
        for g in range(kv_heads):
            key, value = k_ref[:, lanes_of(g)], v_ref[:, lanes_of(g)]
            key_sum = jnp.zeros((band, LANES), f32)
            value_sum = jnp.zeros((band, LANES), f32)
            for h in range(g * each, (g + 1) * each):
                query, head = q_ref[:, lanes_of(h)], heads[:, lanes_of(h)]
                scores = product_turned(query, key) * (0.5 * score_scale) + bias_ref[...]
                grown = jnp.exp(scores - jnp.max(scores, axis=-1, keepdims=True))
                weight = grown / jnp.sum(grown, axis=-1, keepdims=True)
                value_sum += product_over_rows(weight.astype(bf16), head)
                weight_grad = product_turned(head, value)
                inner = jnp.sum(weight * weight_grad, axis=-1, keepdims=True)
                score_grad = (weight * (weight_grad - inner) * score_scale).astype(bf16)
                query_parts.append(turned_back(product(score_grad, key)))
                key_sum += product_over_rows(score_grad, query)
            key_parts.append(turned_back(key_sum))
            value_parts.append(value_sum)
        place(0, query_parts)
        place(query_width, key_parts)
        place(query_width + key_width, value_parts)
        sums[...] = product_turned(made_ref[...], qkv_ref[...]).astype(bf16)
        pl.semaphore_wait(barrier, team.bits + 1)
        reduce = scatter_all(team, sums, rows, sums_in, tr_send, tr_recv, width)
        norm_grad = sums[rows_of(team.t, rows)].astype(f32)
        _, normed, inverse = norm_rows(in_ref[...].astype(f32), gain_ref[...])
        back, gain_grad = norm_back(norm_grad, normed, inverse, gain_ref[...])
        result = grad_ref[...] + back
        leaving[...] = result.astype(bf16)
        move = ring_copy(team, -1, leaving, arrived_ref, sec_send, sec_recv)
        move.start()
        gain_out[...] = gain_grad
        out_ref[...] = result
        for one in reduce:
            one.drain()
        move.wait()

    return pl.pallas_call(
        kernel,
        out_shape=[
            jax.ShapeDtypeStruct((rows, width), f32),
            jax.ShapeDtypeStruct((1, width), f32),
            jax.ShapeDtypeStruct((rows, width), bf16),
            jax.ShapeDtypeStruct((band, qkv_width), bf16),
        ],
        in_specs=[WHOLE_VMEM] * 11,
        out_specs=[WHOLE_VMEM] * 4,
        scratch_shapes=[
            pltpu.VMEM((band, queries.shape[1]), bf16),
            pltpu.VMEM((band, width), bf16),
            pltpu.VMEM((tp, rows, width), bf16),
            pltpu.VMEM((rows, width), bf16),
            dma((SLICES * tp,)), dma((SLICES * tp,)), dma((1,)), dma((1,)),
        ],
        compiler_params=comm_params(number),
        name="end_layer",
    )(attn_grad, queries, keys, values, bias, turn, out_twice, w_qkv, layer_in, state_grad, gain)


def plain_copy(array, steps):
    rows, width = array.shape

    def kernel(in_ref, out_ref, token_ref):
        out_ref[...] = in_ref[...]
        token_ref[...] = jnp.zeros_like(token_ref)

    block = pl.BlockSpec((rows // steps, width), lambda i: (i, 0))
    return pl.pallas_call(
        kernel,
        grid=(steps,),
        out_shape=[
            jax.ShapeDtypeStruct(array.shape, array.dtype),
            jax.ShapeDtypeStruct((8, LANES), jnp.float32),
        ],
        in_specs=[block],
        out_specs=[block, pl.BlockSpec((8, LANES), lambda i: (0, 0))],
        name="plain_copy",
    )(array)


def order_map(inputs, outputs, count, part, turned):
    across = count * part
    source = lax.broadcasted_iota(jnp.int32, (inputs, outputs), 1 if turned else 0)
    target = lax.broadcasted_iota(jnp.int32, (inputs, outputs), 0 if turned else 1)
    e, rest = lax.div(source, across), lax.rem(source, across)
    f, h = lax.div(rest, part), lax.rem(rest, part)
    return (f * LANES + e * part + h == target).astype(jnp.bfloat16)


def block_steps(blocks):
    for steps in (2, 1):
        if blocks % steps == 0:
            return steps


def outgoing_experts(w_gate, w_up, count):
    experts, depth, hidden = w_gate.shape
    part = hidden // count
    bunch = LANES // part
    across = bunch * hidden
    steps = block_steps(experts // bunch)
    each = experts // bunch // steps

    def kernel(gate_ref, up_ref, out_ref, table):
        @pl.when((pl.program_id(0) == 0) & (pl.program_id(1) == 0))
        def _():
            table[...] = order_map(across, count * LANES, count, part, False)

        def move(ref):
            for b in range(each):
                lanes = jnp.concatenate([ref[b * bunch + e] for e in range(bunch)], axis=1)
                moved = product(lanes, table[...]).astype(jnp.bfloat16)
                for f in range(count):
                    out_ref[f, :, b * LANES : (b + 1) * LANES] = moved[:, f * LANES : (f + 1) * LANES]

        @pl.when(pl.program_id(0) == 0)
        def _():
            move(gate_ref)

        @pl.when(pl.program_id(0) == 1)
        def _():
            move(up_ref)

    block = (each * bunch, depth, hidden)
    return pl.pallas_call(
        kernel,
        grid=(2, steps),
        out_shape=jax.ShapeDtypeStruct((count, depth, 2 * steps * each * LANES), jnp.bfloat16),
        in_specs=[
            pl.BlockSpec(block, lambda w, b: (jnp.where(w == 0, b, steps - 1), 0, 0)),
            pl.BlockSpec(block, lambda w, b: (jnp.where(w == 1, b, 0), 0, 0)),
        ],
        out_specs=pl.BlockSpec((count, depth, each * LANES), lambda w, b: (0, 0, w * steps + b)),
        scratch_shapes=[pltpu.VMEM((across, count * LANES), jnp.bfloat16)],
        compiler_params=pltpu.CompilerParams(vmem_limit_bytes=VMEM_LIMIT),
        name="outgoing_experts",
    )(w_gate, w_up)


def incoming_experts(both, experts, hidden):
    count, depth, width = both.shape
    part = hidden // count
    bunch = LANES // part
    across = bunch * hidden
    steps = block_steps(experts // bunch)
    each = experts // bunch // steps

    def kernel(in_ref, gate_ref, up_ref, table):
        @pl.when((pl.program_id(0) == 0) & (pl.program_id(1) == 0))
        def _():
            table[...] = order_map(count * LANES, across, count, part, True)

        def store(ref):
            for b in range(each):
                lanes = jnp.concatenate(
                    [in_ref[f, :, b * LANES : (b + 1) * LANES] for f in range(count)], axis=1
                )
                moved = product(lanes, table[...])
                for e in range(bunch):
                    ref[b * bunch + e] = moved[:, e * hidden : (e + 1) * hidden]

        @pl.when(pl.program_id(0) == 0)
        def _():
            store(gate_ref)

        @pl.when(pl.program_id(0) == 1)
        def _():
            store(up_ref)

    shape = jax.ShapeDtypeStruct((experts, depth, hidden), jnp.float32)
    block = (each * bunch, depth, hidden)
    return pl.pallas_call(
        kernel,
        grid=(2, steps),
        out_shape=[shape, shape],
        in_specs=[pl.BlockSpec((count, depth, each * LANES), lambda w, b: (0, 0, w * steps + b))],
        out_specs=[
            pl.BlockSpec(block, lambda w, b: (jnp.where(w == 0, b, steps - 1), 0, 0)),
            pl.BlockSpec(block, lambda w, b: (jnp.where(w == 1, b, 0), 0, 0)),
        ],
        scratch_shapes=[pltpu.VMEM((count * LANES, across), jnp.bfloat16)],
        compiler_params=pltpu.CompilerParams(vmem_limit_bytes=VMEM_LIMIT),
        name="incoming_experts",
    )(both)


def line_barrier(team, tp):
    barrier = pltpu.get_barrier_semaphore()
    count = 0
    for i in range(1, team.fsdp):
        pl.semaphore_signal(
            barrier,
            inc=1,
            device_id={"fsdp": lax.rem(team.f + i, team.fsdp)},
            device_id_type=MESH,
        )
        count += 1
    if tp:
        for bit in range(team.bits):
            pl.semaphore_signal(
                barrier, inc=1, device_id={"tp": flipped(team.t, bit)}, device_id_type=MESH
            )
            count += 1
    pl.semaphore_wait(barrier, count)


def gather_weights(sizes, matrix, small, number):
    fsdp = sizes[1]
    depth, width = matrix.shape
    dma = pltpu.SemaphoreType.DMA

    def kernel(matrix_ref, small_ref, all_ref, few_ref, held, *sems):
        up_send, up_recv, down_send, down_recv, few_send, few_recv, local, out_sem = sems
        team = Team(sizes)
        f = team.f
        mine = pltpu.make_async_copy(matrix_ref, held.at[f], local.at[0])
        mine.start()
        few_ref[f] = small_ref[...]
        line_barrier(team, False)

        def few(i, arriving):
            other = lax.rem(f + (fsdp - i if arriving else i), fsdp)
            part = few_ref.at[other if arriving else f]
            return pltpu.make_async_remote_copy(
                src_ref=part,
                dst_ref=part,
                send_sem=few_send.at[i],
                recv_sem=few_recv.at[i],
                device_id={"fsdp": other},
                device_id_type=MESH,
            )

        for i in range(1, fsdp):
            few(i, False).start()
        mine.wait()

        def hand(block, step):
            sends, recvs = (up_send, up_recv) if step > 0 else (down_send, down_recv)
            return pltpu.make_async_remote_copy(
                src_ref=held.at[block],
                dst_ref=held.at[block],
                send_sem=sends.at[block],
                recv_sem=recvs.at[block],
                device_id={"fsdp": lax.rem(f + step + fsdp, fsdp)},
                device_id_type=MESH,
            )

        def out(block):
            return pltpu.make_async_copy(held.at[block], all_ref.at[block], out_sem.at[block])

        @pl.when(f < fsdp - 1)
        def _():
            hand(f, 1).start()

        @pl.when(f > 0)
        def _():
            hand(f, -1).start()

        out(f).start()

        def step(i, carry):
            below, above = f - i, f + i

            @pl.when(below >= 0)
            def _():
                hand(below, 1).wait_recv()

                @pl.when(f < fsdp - 1)
                def _():
                    hand(below, 1).start()

                out(below).start()

            @pl.when(above < fsdp)
            def _():
                hand(above, -1).wait_recv()

                @pl.when(f > 0)
                def _():
                    hand(above, -1).start()

                out(above).start()

            return carry

        lax.fori_loop(1, fsdp, step, 0)

        def finish(g, carry):
            @pl.when((g <= f) & (f < fsdp - 1))
            def _():
                hand(g, 1).wait_send()

            @pl.when((g >= f) & (f > 0))
            def _():
                hand(g, -1).wait_send()

            out(g).wait()
            return carry

        lax.fori_loop(0, fsdp, finish, 0)
        for i in range(1, fsdp):
            few(i, True).wait_recv()
            few(i, False).wait_send()

    anywhere = pl.BlockSpec(memory_space=pl.ANY)
    return pl.pallas_call(
        kernel,
        out_shape=[
            jax.ShapeDtypeStruct((fsdp, depth, width), matrix.dtype),
            jax.ShapeDtypeStruct((fsdp,) + small.shape, small.dtype),
        ],
        in_specs=[anywhere, WHOLE_VMEM],
        out_specs=[anywhere, WHOLE_VMEM],
        scratch_shapes=[pltpu.VMEM((fsdp, depth, width), matrix.dtype)]
        + [dma((fsdp,)) for _ in range(6)]
        + [dma((1,)), dma((fsdp,))],
        compiler_params=comm_params(number),
        name="gather_weights",
    )(matrix, small)


def reduce_weights(sizes, matrix, small, number):
    tp, fsdp = sizes[2], sizes[1]
    _, depth, width = matrix.shape
    count_rows = small.shape[0]
    portion = small.shape[1] // fsdp
    bits = tp.bit_length() - 1
    bf16, f32 = jnp.bfloat16, jnp.float32
    dma = pltpu.SemaphoreType.DMA

    def kernel(matrix_ref, small_ref, sum_ref, few_ref, up, down, up_in, down_in, few_sum, few_tp, few_cut, few_in, *sems):
        up_send, up_recv, down_send, down_recv, tp_send, tp_recv, few_send, few_recv = sems
        team = Team(sizes)
        f = team.f
        line_barrier(team, True)

        def pass_on(g, step):
            sends, recvs = (up_send, up_recv) if step > 0 else (down_send, down_recv)
            return pltpu.make_async_remote_copy(
                src_ref=(up if step > 0 else down).at[g],
                dst_ref=(up_in if step > 0 else down_in).at[g],
                send_sem=sends.at[g],
                recv_sem=recvs.at[g],
                device_id={"fsdp": lax.rem(f + step + fsdp, fsdp)},
                device_id_type=MESH,
            )

        def tp_copy(bit):
            return pltpu.make_async_remote_copy(
                src_ref=few_sum.at[bit],
                dst_ref=few_tp.at[bit],
                send_sem=tp_send.at[bit],
                recv_sem=tp_recv.at[bit],
                device_id={"tp": flipped(team.t, bit)},
                device_id_type=MESH,
            )

        few_sum[0] = small_ref[...]

        def step(i, carry):
            high, low = fsdp - 1 - i, i

            @pl.when(high > f)
            def _():
                @pl.when(f == 0)
                def _():
                    up[high] = matrix_ref[high]

                @pl.when(f > 0)
                def _():
                    pass_on(high, 1).wait_recv()
                    up[high] = (matrix_ref[high].astype(f32) + up_in[high].astype(f32)).astype(bf16)

                pass_on(high, 1).start()

            @pl.when(low < f)
            def _():
                @pl.when(f == fsdp - 1)
                def _():
                    down[low] = matrix_ref[low]

                @pl.when(f < fsdp - 1)
                def _():
                    pass_on(low, -1).wait_recv()
                    down[low] = (matrix_ref[low].astype(f32) + down_in[low].astype(f32)).astype(bf16)

                pass_on(low, -1).start()

            return carry

        lax.fori_loop(0, fsdp - 1, step, 0)
        for bit in range(bits):
            tp_copy(bit).start()
            tp_copy(bit).wait_recv()
            few_sum[bit + 1] = few_sum[bit] + few_tp[bit]
        for g in range(fsdp):
            few_cut[g] = few_sum[bits, :, g * portion : (g + 1) * portion]

        def few(i, arriving):
            other = lax.rem(f + (fsdp - i if arriving else i), fsdp)
            return pltpu.make_async_remote_copy(
                src_ref=few_cut.at[other],
                dst_ref=few_in.at[i],
                send_sem=few_send.at[i],
                recv_sem=few_recv.at[i],
                device_id={"fsdp": other},
                device_id_type=MESH,
            )

        for i in range(1, fsdp):
            few(i, False).start()
        sum_ref[...] = matrix_ref[f].astype(f32)

        @pl.when(f > 0)
        def _():
            pass_on(f, 1).wait_recv()
            sum_ref[...] += up_in[f].astype(f32)

        @pl.when(f < fsdp - 1)
        def _():
            pass_on(f, -1).wait_recv()
            sum_ref[...] += down_in[f].astype(f32)

        total = few_cut[f]
        for i in range(1, fsdp):
            few(i, True).wait_recv()
            total = total + few_in[i]
        few_ref[...] = total

        def finish(g, carry):
            @pl.when(g > f)
            def _():
                pass_on(g, 1).wait_send()

            @pl.when(g < f)
            def _():
                pass_on(g, -1).wait_send()

            return carry

        lax.fori_loop(0, fsdp, finish, 0)
        for i in range(1, fsdp):
            few(i, False).wait_send()
        for bit in range(bits):
            tp_copy(bit).wait_send()

    return pl.pallas_call(
        kernel,
        out_shape=[
            jax.ShapeDtypeStruct((depth, width), f32),
            jax.ShapeDtypeStruct((count_rows, portion), f32),
        ],
        in_specs=[WHOLE_VMEM] * 2,
        out_specs=[WHOLE_VMEM] * 2,
        scratch_shapes=[pltpu.VMEM((fsdp, depth, width), bf16) for _ in range(4)]
        + [
            pltpu.VMEM((bits + 1,) + small.shape, f32),
            pltpu.VMEM((bits,) + small.shape, f32),
            pltpu.VMEM((fsdp, count_rows, portion), f32),
            pltpu.VMEM((fsdp, count_rows, portion), f32),
        ]
        + [dma((fsdp,)) for _ in range(4)]
        + [dma((tp,)), dma((tp,)), dma((fsdp,)), dma((fsdp,))],
        compiler_params=comm_params(number),
        name="reduce_weights",
    )(matrix, small)


def exchange(blocks):
    return lax.all_to_all(blocks, "fsdp", split_axis=0, concat_axis=0, tiled=True)


def attention_forward(attn_in, segment, w_qkv, w_output):
    query_width = w_output.shape[0]
    key_width = (w_qkv.shape[1] - query_width) // 2
    key_value_heads = key_width // HEAD_SIZE
    count_of_tokens = attn_in.shape[0]
    permitted_mask = allowed_pairs(segment)
    cosine, sine = rope_tables(permitted_mask)
    qkv = jnp.dot(attn_in, w_qkv, preferred_element_type=jnp.float32)
    turned = rotate(
        qkv[:, : query_width + key_width].reshape(count_of_tokens, -1, HEAD_SIZE), cosine, sine
    ).astype(jnp.bfloat16)
    query_rows = turned[:, : query_width // HEAD_SIZE].reshape(
        count_of_tokens, key_value_heads, QUERY_HEADS // KEY_VALUE_HEADS, HEAD_SIZE
    )
    key_matrix = turned[:, query_width // HEAD_SIZE :]
    value_matrix = (
        qkv[:, query_width + key_width :]
        .astype(jnp.bfloat16)
        .reshape(count_of_tokens, key_value_heads, HEAD_SIZE)
    )
    attended = attend(query_rows, key_matrix, value_matrix, permitted_mask)
    mixed_heads = attended.reshape(count_of_tokens, -1)
    partial = jnp.dot(mixed_heads, w_output, preferred_element_type=jnp.float32)
    half = HEAD_SIZE // 2
    beside = jnp.concatenate([turned, turned[..., half:], turned[..., :half]], axis=-1)
    heads = query_width // HEAD_SIZE
    queries = beside[:, :heads].reshape(count_of_tokens, -1)
    keys = beside[:, heads:].reshape(count_of_tokens, -1)
    values = jnp.concatenate([value_matrix, jnp.zeros_like(value_matrix)], axis=-1)
    bias = jnp.where(permitted_mask, 0.0, masked_score).astype(jnp.float32)
    turn = jnp.concatenate([cosine, cosine, sine, -sine], axis=-1)[:, 0]
    kept = (queries, keys, values.reshape(count_of_tokens, -1), bias, turn)
    return (partial.astype(jnp.bfloat16), kept, mixed_heads)


def summed_product(pairs):
    left = jnp.concatenate([pair[0] for pair in pairs], axis=0)
    right = jnp.concatenate([pair[1] for pair in pairs], axis=0)
    return lax.dot_general(
        left, right, (((0,), (0,)), ((), ())), preferred_element_type=jnp.float32
    )


def per_device(
    sizes,
    inputs,
    segment_ids,
    routes,
    w_query,
    key_weight,
    value_weight,
    w_output,
    w_router,
    gain_attn,
    gain_moe,
    w_gate,
    w_up,
    w_down,
    out_grad,
):
    section_count, fsdp_count, tp_count = sizes
    section_index = lax.axis_index("section")
    micro_count, local_rows, model_width = inputs.shape
    depth = w_query.shape[1]
    expert_count = w_router.shape[2]
    hidden_units = w_gate.shape[3]
    own_units = hidden_units // fsdp_count
    hidden = expert_count * own_units
    copies = LANES // expert_count
    query_width = w_query.shape[2]
    key_width = key_weight.shape[2]
    qkv_width = query_width + 2 * key_width
    flat_output = w_output[0].reshape(depth, -1)
    matrix = jnp.concatenate(
        [w_query[0], key_weight[0], value_weight[0], flat_output], axis=1
    )
    few = jnp.concatenate(
        [w_router[0].T, gain_attn.astype(jnp.bfloat16), gain_moe.astype(jnp.bfloat16)], axis=0
    )
    few_rows = -(-few.shape[0] // 16) * 16
    few = jnp.pad(few, ((0, few_rows - few.shape[0]), (0, 0)))
    expert_ids = jnp.arange(expert_count, dtype=jnp.int32)
    chosen_rows = jnp.any(routes[0][..., None] == expert_ids, axis=2).astype(jnp.bfloat16)
    chosen_shape = chosen_rows.shape
    few = jnp.concatenate([few, chosen_rows.reshape(-1, few.shape[1])], axis=0)
    both_out = outgoing_experts(w_gate[0], w_up[0], fsdp_count)
    matrix, few = gather_weights(sizes, matrix, few, 5)
    matrix, few, both_out = lax.optimization_barrier((matrix, few, both_out))
    gate_up = exchange(both_out).reshape(model_width, 2 * hidden)
    matrix = matrix.reshape(model_width, -1)
    chosen_rows = few[:, few_rows:].reshape((fsdp_count,) + chosen_shape)
    few = few[:, :few_rows].transpose(1, 0, 2).reshape(few_rows, model_width)
    w_qkv = matrix[:, :qkv_width]
    out_full = matrix[:, qkv_width:].reshape(-1, model_width)
    out_heads = out_full.reshape(-1, 1, HEAD_SIZE, model_width)
    out_twice = jnp.tile(out_heads, (1, LANES // HEAD_SIZE, 1, 1)).reshape(-1, model_width)
    router = jnp.tile(few[:expert_count].T, (1, copies))
    gain_one = few[expert_count].astype(jnp.float32)[None]
    gain_two = few[expert_count + 1].astype(jnp.float32)[None]
    down = w_down[0].reshape(hidden, model_width)
    lane = jnp.arange(LANES, dtype=jnp.int32)
    owner = jnp.arange(hidden, dtype=jnp.int32) // own_units
    match = (lane % expert_count)[:, None] == owner[None, :]
    spread_map = (match & (lane < 3 * expert_count)[:, None]).astype(jnp.bfloat16)
    pick_map = (match & (lane < 2 * expert_count)[:, None]).astype(jnp.bfloat16).T
    chosen_rows = jnp.tile(chosen_rows, (1, 1, 1, copies))
    segment_rows = segment_ids[:, 0, :]
    tick_count = micro_count + section_count - 1
    outputs = jnp.zeros((micro_count, local_rows, model_width), jnp.bfloat16)
    history = []
    layer_in = jnp.where(section_index == 0, inputs[0], jnp.zeros_like(inputs[0]))
    attn_in = begin_layer(sizes, layer_in, gain_one, 0)
    for tick_step in range(tick_count):
        mb_index = tick_step - section_index
        active = (mb_index >= 0) & (mb_index < micro_count)
        mb_pick = jnp.clip(mb_index, 0, micro_count - 1)
        segment = lax.dynamic_index_in_dim(segment_rows, mb_pick, 0, keepdims=False)
        chosen = lax.dynamic_index_in_dim(chosen_rows, mb_pick, 1, keepdims=False)
        partial, kept, mixed_heads = attention_forward(attn_in, segment, w_qkv, out_full)
        last = tick_step == tick_count - 1
        fresh = None if last else inputs[min(tick_step + 1, micro_count - 1)]
        weights = (router, gain_one, gain_two, gate_up, down, spread_map)
        if tick_step == 0 and not last:
            moe_in, state = moe_gather(sizes, partial, layer_in, gain_two, 9)
            made = moe_forward(
                sizes, moe_in, state, chosen, weights, fresh, expert_count, True, 10
            )
            made = [moe_in, made[0], made[1], state] + list(made[2:])
        else:
            made = moe_forward(
                sizes, partial, layer_in, chosen, weights, fresh, expert_count, False, 2 if last else 1
            )
        moe_in, pre, share, state, result = made[:5]
        history.append((attn_in, layer_in, kept, mixed_heads, moe_in, pre, share, state))
        outputs = jnp.where(
            active, lax.dynamic_update_index_in_dim(outputs, result, mb_pick, 0), outputs
        )
        if not last:
            layer_in, attn_in = made[5:]
    input_grads = jnp.zeros((micro_count, local_rows, model_width), jnp.float32)
    gain_sums = None
    all_terms = []
    arrived = None
    place = (lax.axis_index("fsdp"), lax.axis_index("tp") * local_rows, 0)
    for tick_step in range(tick_count):
        mb_index = micro_count + section_count - 2 - tick_step - section_index
        active = (mb_index >= 0) & (mb_index < micro_count)
        mb_pick = jnp.clip(mb_index, 0, micro_count - 1)
        upstream = out_grad[max(micro_count - 1 - tick_step, 0)].astype(jnp.float32)
        if arrived is None:
            arrived = jnp.zeros_like(upstream)
        upstream = jnp.where(
            section_index == section_count - 1, upstream, arrived.astype(jnp.float32)
        )
        upstream = jnp.where(active, upstream, jnp.zeros_like(upstream))
        attn_in, layer_in, kept, mixed_heads, moe_in, pre, share, state = history[tick_count - 1 - tick_step]
        last = tick_step == tick_count - 1
        both_sum, down_sum, logit_grad, gain_two_part, state_grad, attn_grad = moe_backward(
            sizes,
            upstream,
            state,
            share,
            pre,
            moe_in,
            (router, gain_two, gate_up, down, spread_map, pick_map),
            expert_count,
            None if tick_step == 0 else (both_sum, down_sum),
            last,
            7 if tick_step == 0 else 8 if last else 3,
        )
        if last:
            both_sum = exchange(both_sum.reshape(fsdp_count, depth, 2 * hidden))
        grad_out, gain_one_part, arrived, qkv_grad = end_layer(
            sizes, attn_grad, kept, out_twice, w_qkv, layer_in, state_grad, gain_one, 4
        )
        input_grads = jnp.where(
            active, lax.dynamic_update_index_in_dim(input_grads, grad_out, mb_pick, 0), input_grads
        )
        gains = (gain_one_part, gain_two_part)
        gain_sums = gains if gain_sums is None else tuple(a + b for a, b in zip(gain_sums, gains))
        own_rows = lax.dynamic_slice(moe_in, place, (1, local_rows, model_width))[0]
        all_terms.append(
            (
                active,
                (
                    (attn_in, qkv_grad),
                    (mixed_heads, attn_grad),
                    (logit_grad[:, :expert_count], own_rows),
                ),
            )
        )
    chosen_terms = []
    for first in range(micro_count):
        picked = all_terms[first][1]
        for active, terms in all_terms[first + micro_count :: micro_count]:
            picked = jax.tree.map(lambda a, b: jnp.where(active, b, a), picked, terms)
        chosen_terms.append(picked)
    qkv_pairs, output_pairs, router_pairs = zip(*chosen_terms)
    gate_shard, up_shard = incoming_experts(both_sum, expert_count, hidden_units)
    down_shard = down_sum.reshape(expert_count, own_units, model_width)
    small = jnp.concatenate([summed_product(router_pairs)] + list(gain_sums), axis=0)
    small = jnp.pad(small, ((0, few_rows - small.shape[0]), (0, 0)))
    matrix_grad = jnp.concatenate(
        [summed_product(qkv_pairs), summed_product(output_pairs).reshape(model_width, -1)], axis=1
    ).astype(jnp.bfloat16)
    down_sum, token = plain_copy(down_sum, 4)
    token, matrix_grad = lax.optimization_barrier((token, matrix_grad))
    matrix_grad, few_grad = reduce_weights(
        sizes, matrix_grad.reshape(fsdp_count, depth, -1), small, 6
    )
    shard_sums = (
        matrix_grad[:, :query_width],
        matrix_grad[:, query_width : query_width + key_width],
        matrix_grad[:, query_width + key_width : qkv_width],
        matrix_grad[:, qkv_width:].reshape(-1, model_width),
        few_grad[:expert_count].T,
        few_grad[expert_count],
        few_grad[expert_count + 1],
        gate_shard,
        up_shard,
        down_shard,
    )
    return (outputs[None], input_grads[None]) + tuple((part[None] for part in shard_sums))


def solution(mesh):
    in_specs = (
        P(None, ("fsdp", "tp"), None),
        P(None, "fsdp", None),
        P("section", None, "fsdp", None),
        P("section", "fsdp", "tp"),
        P("section", "fsdp", "tp"),
        P("section", "fsdp", "tp"),
        P("section", ("tp", "fsdp"), None),
        P("section", "fsdp", None),
        P("section", "fsdp"),
        P("section", "fsdp"),
        P("section", None, "fsdp", "tp"),
        P("section", None, "fsdp", "tp"),
        P("section", None, ("tp", "fsdp"), None),
        P(None, ("fsdp", "tp"), None),
    )
    out_specs = (
        P("section", None, ("fsdp", "tp"), None),
        P("section", None, ("fsdp", "tp"), None),
        P("section", "fsdp", "tp"),
        P("section", "fsdp", "tp"),
        P("section", "fsdp", "tp"),
        P("section", ("tp", "fsdp"), None),
        P("section", "fsdp", None),
        P("section", "fsdp"),
        P("section", "fsdp"),
        P("section", None, "fsdp", "tp"),
        P("section", None, "fsdp", "tp"),
        P("section", None, ("tp", "fsdp"), None),
    )
    sizes = tuple(mesh.shape[axis] for axis in ("section", "fsdp", "tp"))
    return jax.shard_map(
        functools.partial(per_device, sizes), mesh=mesh, in_specs=in_specs, out_specs=out_specs, check_vma=False
    )
```

```python
import functools

import jax
import jax.numpy as jnp
from jax import lax
from jax.experimental import pallas as pl
from jax.experimental.pallas import tpu as pltpu
from jax.sharding import PartitionSpec as P

QUERY_HEADS = 16
KEY_VALUE_HEADS = 8
HEAD_SIZE = 64


norm_eps = 1e-06
branch_scale = 0.22
score_scale = 0.015625
rope_base = 10000.0
masked_score = -1e30


def norm_rows(vectors, gain_vec):
    inverse = lax.rsqrt(jnp.mean(vectors * vectors, axis=-1, keepdims=True) + norm_eps)
    normed = vectors * inverse
    return (normed * gain_vec, normed, inverse)


def norm_back(upstream, normed, inverse, gain_vec):
    scaled_grad = upstream * gain_vec
    gain_grad = jnp.sum(upstream * normed, axis=0, keepdims=True)
    inner_mean = jnp.mean(scaled_grad * normed, axis=-1, keepdims=True)
    return (inverse * (scaled_grad - normed * inner_mean), gain_grad)


def rope_tables(permitted_mask):
    offsets = (jnp.sum(permitted_mask.astype(jnp.int32), axis=1) - 1).astype(jnp.float32)
    half_dim = HEAD_SIZE // 2
    frequency = rope_base ** (-(jnp.arange(half_dim, dtype=jnp.float32) * 2.0 / HEAD_SIZE))
    angles = offsets[:, None] * frequency[None, :]
    return (jnp.cos(angles)[:, None, :], jnp.sin(angles)[:, None, :])


def rotate(vectors, cosine, sine):
    half_dim = vectors.shape[-1] // 2
    front_half = vectors[..., :half_dim]
    back_half = vectors[..., half_dim:]
    return jnp.concatenate(
        [front_half * cosine - back_half * sine, back_half * cosine + front_half * sine], axis=-1
    )


def allowed_pairs(segment):
    position = jnp.arange(segment.shape[0], dtype=jnp.int32)
    return (segment[:, None] == segment[None, :]) & (position[None, :] <= position[:, None])


def attend(query_rows, key_matrix, value_matrix, permitted_mask):
    scores = (
        jnp.einsum("qhgd,khd->hgqk", query_rows, key_matrix, preferred_element_type=jnp.float32)
        * score_scale
    )
    scores = jnp.where(permitted_mask[None, None], scores, masked_score)
    row_max = jnp.max(scores, axis=-1, keepdims=True)
    log_sum_exp = row_max + jnp.log(jnp.sum(jnp.exp(scores - row_max), axis=-1, keepdims=True))
    weights_low = jnp.exp(scores - log_sum_exp).astype(jnp.bfloat16)
    attended = jnp.einsum(
        "hgqk,khd->qhgd", weights_low, value_matrix, preferred_element_type=jnp.float32
    )
    return attended.astype(jnp.bfloat16)


MESH = pl.DeviceIdType.MESH
LANES = 128
VMEM_LIMIT = 60 * 1024 * 1024
WHOLE_VMEM = pl.BlockSpec(memory_space=pltpu.VMEM)


def flipped(index, bit):
    step = 1 << bit
    return index + step - 2 * step * lax.rem(lax.div(index, step), 2)


def crossed(index, mask, bits):
    for bit in range(bits):
        if (mask >> bit) & 1:
            index = flipped(index, bit)
    return index


class Team:
    def __init__(self, sizes):
        self.sections, self.fsdp, self.tp = sizes
        self.bits = self.tp.bit_length() - 1
        assert 1 << self.bits == self.tp
        self.s = lax.axis_index("section")
        self.f = lax.axis_index("fsdp")
        self.t = lax.axis_index("tp")
        self.hops = [
            (bit, mask)
            for bit in reversed(range(self.bits))
            for mask in range(0, self.tp, 2 << bit)
        ]
        self.place = {hop: number for number, hop in enumerate(self.hops)}

    def row(self, i):
        above = self.fsdp - 1 - self.f
        short = jnp.minimum(self.f, above)
        paired = i <= 2 * short
        distance = jnp.where(paired, lax.div(i + 1, 2), i - short)
        upward = jnp.where(paired, lax.rem(i, 2) == 1, self.f < above)
        return jnp.where(upward, self.f + distance, self.f - distance)

    def column(self, mask):
        return crossed(self.t, mask, self.bits)


def greet(team, fsdp, section_step):
    barrier = pltpu.get_barrier_semaphore()
    count = 0
    if fsdp:
        for i in range(1, team.fsdp):
            pl.semaphore_signal(
                barrier,
                inc=1,
                device_id={"fsdp": lax.rem(team.f + i, team.fsdp)},
                device_id_type=MESH,
            )
            count += 1
    for bit in range(team.bits):
        pl.semaphore_signal(
            barrier, inc=1, device_id={"tp": flipped(team.t, bit)}, device_id_type=MESH
        )
        count += 1
    if section_step:
        behind = lax.rem(team.s + team.sections - section_step, team.sections)
        pl.semaphore_signal(
            barrier, inc=1, device_id={"section": behind}, device_id_type=MESH
        )
        count += 1
    pl.semaphore_wait(barrier, count)


def rows_of(block, size):
    return pl.ds(pl.multiple_of(block * size, size), size)


SLICES = 4


def slice_of(block, size, part):
    share = size // SLICES
    return pl.ds(pl.multiple_of(block * size + part * share, share), share)


class TpGather:
    def __init__(self, team, ref, size, sends, recvs, part):
        self.team, self.ref, self.size, self.part = team, ref, size, part
        self.sends = lambda place: sends(place * SLICES + part)
        self.recvs = lambda place: recvs(place * SLICES + part)

    def copy(self, hop, arriving):
        bit, mask = hop
        team = self.team
        block = team.column(mask | ((1 << bit) if arriving else 0))
        part = self.ref.at[slice_of(block, self.size, self.part)]
        return pltpu.make_async_remote_copy(
            src_ref=part,
            dst_ref=part,
            send_sem=self.sends(team.place[hop]),
            recv_sem=self.recvs(team.place[hop]),
            device_id={"tp": flipped(team.t, bit)},
            device_id_type=MESH,
        )

    def begin(self):
        for bit in reversed(range(self.team.bits)):
            self.copy((bit, 0), False).start()

    def relay(self):
        for hop in self.team.hops:
            bit, mask = hop
            if bit:
                self.copy(hop, True).wait_recv()
                for lower in reversed(range(bit)):
                    self.copy((lower, mask | (1 << bit)), False).start()

    def arrive(self):
        for hop in self.team.hops:
            if hop[0] == 0:
                self.copy(hop, True).wait_recv()

    def drain(self):
        for hop in self.team.hops:
            self.copy(hop, False).wait_send()


def add_blocks(target, rows, other, width, experts):
    wide = target[rows, :width].astype(jnp.float32) + other[:, :width].astype(jnp.float32)
    target[rows, :width] = wide.astype(target.dtype)
    if target.shape[1] > width:
        both = target[rows, width:].astype(jnp.float32) + other[:, width:].astype(jnp.float32)
        target[rows, width:] = two_parts(both, experts)


def two_parts(both, experts):
    lane = lax.broadcasted_iota(jnp.int32, both.shape, 1)
    first = lane < experts
    full = both + jnp.where(
        first, pltpu.roll(both, LANES - experts, 1), pltpu.roll(both, experts, 1)
    )
    return parted(full, first, lane < 2 * experts)


def parted(full, first, second):
    high = full.astype(jnp.bfloat16)
    low = (full - high.astype(jnp.float32)).astype(jnp.bfloat16)
    zero = jnp.zeros_like(high)
    return jnp.where(first, high, jnp.where(second, low, zero))


class TpScatter:
    def __init__(self, team, ref, size, landing, sends, recvs, width, experts, part):
        share = size // SLICES
        self.team, self.ref, self.size, self.part = team, ref, size, part
        self.landing = lambda place: landing(place).at[pl.ds(part * share, share)]
        self.sends = lambda place: sends(place * SLICES + part)
        self.recvs = lambda place: recvs(place * SLICES + part)
        self.width, self.experts = width, experts

    def copy(self, hop):
        bit, mask = hop
        team = self.team
        block = team.column(mask | (1 << bit))
        return pltpu.make_async_remote_copy(
            src_ref=self.ref.at[slice_of(block, self.size, self.part)],
            dst_ref=self.landing(team.place[hop]),
            send_sem=self.sends(team.place[hop]),
            recv_sem=self.recvs(team.place[hop]),
            device_id={"tp": flipped(team.t, bit)},
            device_id_type=MESH,
        )

    def send(self, bit):
        for hop in self.team.hops:
            if hop[0] == bit:
                self.copy(hop).start()

    def add(self, bit):
        for hop in self.team.hops:
            if hop[0] == bit:
                self.copy(hop).wait_recv()
                add_blocks(
                    self.ref,
                    slice_of(self.team.column(hop[1]), self.size, self.part),
                    self.landing(self.team.place[hop]),
                    self.width,
                    self.experts,
                )

    def drain(self):
        for hop in self.team.hops:
            self.copy(hop).wait_send()


def gather_all(team, ref, size, sends, recvs):
    slices = [
        TpGather(team, ref, size, lambda p: sends.at[p], lambda p: recvs.at[p], part)
        for part in range(SLICES)
    ]
    for phase in ("begin", "relay", "arrive", "drain"):
        for one in slices:
            getattr(one, phase)()


def scatter_all(team, ref, size, landing, sends, recvs, width):
    slices = [
        TpScatter(
            team, ref, size, lambda p: landing.at[p], lambda p: sends.at[p], lambda p: recvs.at[p], width, 0, part
        )
        for part in range(SLICES)
    ]
    for one in slices:
        one.send(0)
    for bit in range(team.bits):
        for one in slices:
            one.add(bit)
            if bit + 1 < team.bits:
                one.send(bit + 1)
    return slices


def ring_copy(team, step, source, target, sends, recvs):
    ahead = lax.rem(team.s + team.sections + step, team.sections)
    return pltpu.make_async_remote_copy(
        src_ref=source,
        dst_ref=target,
        send_sem=sends.at[0],
        recv_sem=recvs.at[0],
        device_id={"section": ahead},
        device_id_type=MESH,
    )


def group_exchange(team, gathered, partial, landing, across, sems, size, width, experts, prepare, first, second, spare=None):
    ag_send, ag_recv, agz_send, agz_recv, rs_send, rs_recv, rsz_send, rsz_recv = sems
    count = team.fsdp

    def gather(i, part):
        return TpGather(
            team,
            gathered.at[team.row(i)],
            size,
            lambda place: ag_send.at[i, place],
            lambda place: ag_recv.at[i, place],
            part,
        )

    def scatter(i, part):
        return TpScatter(
            team,
            partial.at[team.row(i)],
            size,
            lambda place: landing.at[i, place],
            lambda place: rs_send.at[i, place],
            lambda place: rs_recv.at[i, place],
            width,
            experts,
            part,
        )

    parts = range(SLICES)
    share = size // SLICES

    def gather_across(i, part, arriving):
        source = team.row(i) if arriving else team.f
        block = gathered.at[source, slice_of(team.t, size, part)]
        return pltpu.make_async_remote_copy(
            src_ref=block,
            dst_ref=block,
            send_sem=agz_send.at[i, part],
            recv_sem=agz_recv.at[source, part],
            device_id={"fsdp": team.row(i)},
            device_id_type=MESH,
        )

    def scatter_across(i, part, arriving):
        source = team.row(i) if arriving else team.f
        return pltpu.make_async_remote_copy(
            src_ref=partial.at[team.row(i), slice_of(team.t, size, part)],
            dst_ref=across.at[source, pl.ds(part * share, share)],
            send_sem=rsz_send.at[i, part],
            recv_sem=rsz_recv.at[source, part],
            device_id={"fsdp": team.row(i)},
            device_id_type=MESH,
        )

    def relay_across(i):
        for part in parts:
            gather_across(i, part, True).wait_recv()
            gather(i, part).begin()

    for part in parts:
        gather(0, part).begin()
    for i in range(1, min(count, 3)):
        for part in parts:
            gather_across(i, part, False).start()
    for part in parts:
        gather(0, part).relay()
    for i in range(3, count):
        for part in parts:
            gather_across(i, part, False).start()
    prepare()
    if count > 1:
        relay_across(1)

    def step(i, carry):
        @pl.when(i < count)
        def _():
            for part in parts:
                gather(i, part).arrive()
            first(team.row(i))

        @pl.when(i + 2 < count)
        def _():
            relay_across(i + 2)

        for bit in range(team.bits):
            done = i - 1 - bit

            @pl.when((done >= min(bit, 1)) & (done < count))
            def _():
                for part in parts:
                    scatter(done, part).add(bit)

                    @pl.when(done > 0)
                    def _():
                        if bit + 1 < team.bits:
                            scatter(done, part).send(bit + 1)
                        else:
                            scatter_across(done, part, False).start()

        @pl.when(i + 1 < count)
        def _():
            for part in parts:
                gather(i + 1, part).relay()

        @pl.when(i < count)
        def _():
            second(team.row(i))
            for part in parts:
                scatter(i, part).send(0)

        if team.bits > 1:

            @pl.when(i == count)
            def _():
                for part in parts:
                    scatter(0, part).send(1)

        if spare is not None:

            @pl.when(i >= count)
            def _():
                spare(i - count)

        return carry

    lax.fori_loop(0, count + team.bits, step, 0)
    for bit in range(1, team.bits):
        for part in parts:
            scatter(0, part).add(bit)
            if bit + 1 < team.bits:
                scatter(0, part).send(bit + 1)
    if spare is not None:
        spare(team.bits)

    def finish(i, carry):
        for part in parts:
            gather_across(i, part, False).wait_send()
            scatter_across(i, part, False).wait_send()
        return carry

    def settle(i, carry):
        for part in parts:
            gather(i, part).drain()
            scatter(i, part).drain()
        return carry

    total = partial[team.f, rows_of(team.t, size)].astype(jnp.float32)
    for i in range(1, count):
        for part in parts:
            scatter_across(i, part, True).wait_recv()
        total = total + across[team.row(i)].astype(jnp.float32)
    lax.fori_loop(1, count, finish, 0)
    lax.fori_loop(0, count, settle, 0)
    return total[:, :width], (total[:, width:] if total.shape[1] > width else None)


def group_sems(team_sizes):
    _, fsdp, tp = team_sizes
    dma = pltpu.SemaphoreType.DMA
    return [
        dma((fsdp, SLICES * tp)), dma((fsdp, SLICES * tp)), dma((fsdp, SLICES)), dma((fsdp, SLICES)),
        dma((fsdp, SLICES * tp)), dma((fsdp, SLICES * tp)), dma((fsdp, SLICES)), dma((fsdp, SLICES)),
    ]


def share_parts(share, experts):
    lane = lax.broadcasted_iota(jnp.int32, share.shape, 1)
    high = share.astype(jnp.bfloat16)
    rest = share - high.astype(jnp.float32)
    middle = rest.astype(jnp.bfloat16)
    low = (rest - middle.astype(jnp.float32)).astype(jnp.bfloat16)
    zero = jnp.zeros_like(high)
    return jnp.where(
        lane < experts,
        high,
        jnp.where(lane < 2 * experts, middle, jnp.where(lane < 3 * experts, low, zero)),
    )


def chunks(length, body, size=1024):
    size = min(size, length)

    def step(c, carry):
        body(pl.multiple_of(c * size, size), size)
        return carry

    lax.fori_loop(0, length // size, step, 0)


def product(left, right):
    return jnp.dot(left, right, preferred_element_type=jnp.float32)


def product_turned(left, right):
    return lax.dot_general(
        left, right, (((1,), (1,)), ((), ())), preferred_element_type=jnp.float32
    )


def product_over_rows(left, right):
    return lax.dot_general(
        left, right, (((0,), (0,)), ((), ())), preferred_element_type=jnp.float32
    )


def comm_params(number):
    return pltpu.CompilerParams(
        collective_id=number, has_side_effects=True, vmem_limit_bytes=VMEM_LIMIT
    )


def begin_layer(sizes, layer_in, gain, number):
    rows, width = layer_in.shape
    tp = sizes[2]

    def kernel(in_ref, gain_ref, out_ref, sends, recvs):
        team = Team(sizes)
        greet(team, False, 0)
        scaled, _, _ = norm_rows(in_ref[...].astype(jnp.float32), gain_ref[...])
        out_ref[rows_of(team.t, rows)] = scaled.astype(jnp.bfloat16)
        gather_all(team, out_ref, rows, sends, recvs)

    return pl.pallas_call(
        kernel,
        out_shape=jax.ShapeDtypeStruct((tp * rows, width), jnp.bfloat16),
        in_specs=[WHOLE_VMEM] * 2,
        out_specs=WHOLE_VMEM,
        scratch_shapes=[pltpu.SemaphoreType.DMA((SLICES * tp,)), pltpu.SemaphoreType.DMA((SLICES * tp,))],
        compiler_params=comm_params(number),
    )(layer_in, gain)


def moe_forward(sizes, partial_out, residual, chosen, weights, fresh, experts, number):
    router, gain_one, gain_two, gate_up, down, spread_map = weights
    sections, fsdp, tp = sizes
    rows, width = residual.shape
    band = tp * rows
    hidden = down.shape[0]
    copies = LANES // experts
    tail = fresh is not None
    bf16, f32 = jnp.bfloat16, jnp.float32
    shapes = [
        jax.ShapeDtypeStruct((fsdp, band, width), bf16),
        jax.ShapeDtypeStruct((fsdp, band, 2 * hidden), bf16),
        jax.ShapeDtypeStruct((fsdp, band, LANES), f32),
        jax.ShapeDtypeStruct((rows, width), f32),
        jax.ShapeDtypeStruct((rows, width), bf16),
    ]
    if tail:
        shapes += [
            jax.ShapeDtypeStruct((rows, width), bf16),
            jax.ShapeDtypeStruct((band, width), bf16),
        ]
    dma = pltpu.SemaphoreType.DMA
    scratch = [
        pltpu.VMEM((band, width), bf16),
        pltpu.VMEM((tp, rows, width), bf16),
        pltpu.VMEM((fsdp, band, width), bf16),
        pltpu.VMEM((fsdp, tp - 1, rows, width), bf16),
        pltpu.VMEM((fsdp, rows, width), bf16),
        pltpu.VMEM((band, hidden), bf16),
        pltpu.VMEM((band, LANES), bf16),
        pltpu.VMEM((rows, width), bf16),
        pltpu.VMEM((width, 2 * hidden), bf16),
        pltpu.VMEM((hidden, width), bf16),
        pltpu.VMEM((fsdp, band, width), bf16),
        pltpu.VMEM((fsdp, band, 2 * hidden), bf16),
        dma((SLICES * tp,)), dma((SLICES * tp,)), dma((SLICES * tp,)), dma((SLICES * tp,)), dma((1,)), dma((1,)),
        dma((2,)), dma((fsdp,)), dma((fsdp,)),
    ] + group_sems(sizes)
    own, out = WHOLE_VMEM, pl.BlockSpec(memory_space=pl.ANY)

    def kernel(*refs):
        part_ref, res_ref, chosen_ref, router_ref, one_ref, two_ref, both_hbm, down_hbm, map_ref = refs[:9]
        refs = refs[9:]
        if tail:
            fresh_ref, refs = refs[0], refs[1:]
        all_hbm, pre_hbm, share_ref, state_ref, result_ref = refs[:5]
        refs = refs[5:]
        if tail:
            next_ref, attn_ref = refs[:2]
            refs = refs[2:]
        sums, sums_in, partial, landing, across, weighted, parts, moved = refs[:8]
        both_ref, down_ref, all_ref, pre_ref = refs[8:12]
        tr_send, tr_recv, tg_send, tg_recv, sec_send, sec_recv, load_sem, all_sem, pre_sem = refs[12:21]
        sems = refs[21:]
        team = Team(sizes)
        loads = [
            pltpu.make_async_copy(both_hbm, both_ref, load_sem.at[0]),
            pltpu.make_async_copy(down_hbm, down_ref, load_sem.at[1]),
        ]
        for load in loads:
            load.start()

        def all_out(row):
            return pltpu.make_async_copy(all_ref.at[row], all_hbm.at[row], all_sem.at[row])

        def pre_out(row):
            return pltpu.make_async_copy(pre_ref.at[row], pre_hbm.at[row], pre_sem.at[row])

        def prepare():
            for load in loads:
                load.wait()

        sums[...] = part_ref[...]
        greet(team, True, 1 if tail else 0)
        reduce = scatter_all(team, sums, rows, sums_in, tr_send, tr_recv, width)
        state = res_ref[...].astype(f32) + branch_scale * sums[rows_of(team.t, rows)].astype(f32)
        state_ref[...] = state
        scaled, _, _ = norm_rows(state, two_ref[...])
        all_ref[team.f, rows_of(team.t, rows)] = scaled.astype(bf16)

        def first(row):
            all_out(row).start()
            logits = product(all_ref[row], router_ref[...])
            logits = jnp.where(chosen_ref[row].astype(f32) > 0.5, logits, masked_score)
            grown = jnp.exp(logits - jnp.max(logits, axis=-1, keepdims=True))
            total = jnp.sum(grown, axis=-1, keepdims=True) * (1.0 / copies)
            share = grown / total
            share_ref[row] = share
            parts[...] = share_parts(share, experts)

            def piece(start, size):
                here, there = pl.ds(start, size), pl.ds(pl.multiple_of(hidden + start, size), size)
                gate = product(all_ref[row], both_ref[:, here])
                up = product(all_ref[row], both_ref[:, there])
                pre_ref[row, :, here] = gate.astype(bf16)
                pre_ref[row, :, there] = up.astype(bf16)
                wide = product(parts[...], map_ref[:, here])
                weighted[:, here] = (wide * (gate * jax.nn.sigmoid(gate) * up)).astype(bf16)

            chunks(hidden, piece)
            pre_out(row).start()

        def second(row):
            def piece(start, size):
                here = pl.ds(start, size)
                partial[row, :, here] = product(weighted[...], down_ref[:, here]).astype(bf16)

            chunks(width, piece)

        total, _ = group_exchange(
            team, all_ref, partial, landing, across, sems, rows, width, experts, prepare, first, second
        )
        result_ref[...] = (state_ref[...] + branch_scale * total).astype(bf16)
        for one in reduce:
            one.drain()
        if tail:
            move = ring_copy(team, 1, result_ref, moved, sec_send, sec_recv)
            move.start()
            move.wait_recv()
            layer_in = jnp.where(team.s == 0, fresh_ref[...], moved[...])
            next_ref[...] = layer_in
            scaled, _, _ = norm_rows(layer_in.astype(f32), one_ref[...])
            attn_ref[rows_of(team.t, rows)] = scaled.astype(bf16)
            gather_all(team, attn_ref, rows, tg_send, tg_recv)
            move.wait_send()
        for row in range(fsdp):
            all_out(row).wait()
            pre_out(row).wait()

    args = [partial_out, residual, chosen, router, gain_one, gain_two, gate_up, down, spread_map]
    if tail:
        args.append(fresh)
    return pl.pallas_call(
        kernel,
        out_shape=shapes,
        in_specs=[own] * 6 + [out] * 2 + [own] * (len(args) - 8),
        out_specs=[out] * 2 + [own] * (len(shapes) - 2),
        scratch_shapes=scratch,
        compiler_params=comm_params(number),
        name="moe_forward",
    )(*args)


def moe_backward(sizes, upstream, state, share, pre, moe_in, weights, experts, sums, final, number):
    router, gain_two, gate_up, down, spread_map, pick_map = weights
    sections, fsdp, tp = sizes
    rows, width = upstream.shape
    band = tp * rows
    hidden = down.shape[0]
    bf16, f32 = jnp.bfloat16, jnp.float32
    leaving = bf16 if final else f32
    shapes = [
        jax.ShapeDtypeStruct((width, 2 * hidden), leaving),
        jax.ShapeDtypeStruct((hidden, width), f32),
        jax.ShapeDtypeStruct((rows, LANES), bf16),
        jax.ShapeDtypeStruct((1, width), f32),
        jax.ShapeDtypeStruct((rows, width), f32),
        jax.ShapeDtypeStruct((band, width), bf16),
    ]
    dma = pltpu.SemaphoreType.DMA
    wider = width + LANES
    both_units = team_units(tp)
    both_step = 2 * hidden // both_units
    loops = [both_step // chunk_size(both_step), width // chunk_size(width)]
    both_size, down_size = chunk_size(both_step), chunk_size(width)
    scratch = [
        pltpu.VMEM((fsdp, band, wider), bf16),
        pltpu.VMEM((fsdp, tp - 1, rows, wider), bf16),
        pltpu.VMEM((fsdp, rows, wider), bf16),
        pltpu.VMEM((band, LANES), bf16),
        pltpu.VMEM((band, LANES), f32),
        pltpu.VMEM((width, 2 * hidden), bf16),
        pltpu.VMEM((hidden, width), bf16),
        pltpu.VMEM((fsdp, band, 2 * hidden), bf16),
        pltpu.VMEM((fsdp, band, width), bf16),
        pltpu.VMEM((fsdp, band, 2 * hidden), bf16),
        pltpu.VMEM((fsdp, band, hidden), bf16),
        pltpu.VMEM((fsdp, band, width), bf16),
        pltpu.VMEM((width, 2 * hidden), f32),
        pltpu.VMEM((hidden, width), f32),
        pltpu.VMEM((width, 2 * hidden) if final else (16, LANES), bf16),
        dma((SLICES * tp,)), dma((SLICES * tp,)), dma((5,)), dma((fsdp,)), dma((2,)),
    ] + group_sems(sizes)
    own, out = WHOLE_VMEM, pl.BlockSpec(memory_space=pl.ANY)
    adding = sums is not None

    def kernel(*refs):
        up_ref, state_ref, share_ref, pre_hbm, router_ref, gain_ref, both_hbm, down_hbm, map_ref, pick_ref, in_hbm = refs[:11]
        refs = refs[11:]
        if adding:
            both_old, down_old = refs[:2]
            refs = refs[2:]
        both_out, down_out, logit_ref, gain_out, state_out, attn_ref = refs[:6]
        partial, landing, across, parts, share_sum, both_ref, down_ref, pre_ref, all_ref, grad_ref, weighted_ref = refs[6:17]
        in_ref, both_sum, down_sum, both_low, tg_send, tg_recv, load_sem, pre_sem, out_sem = refs[17:26]
        sems = refs[26:]
        team = Team(sizes)
        loads = [
            pltpu.make_async_copy(down_hbm, down_ref, load_sem.at[0]),
            pltpu.make_async_copy(both_hbm, both_ref, load_sem.at[1]),
        ]
        later = [pltpu.make_async_copy(in_hbm, in_ref, load_sem.at[2])]
        if adding:
            later += [
                pltpu.make_async_copy(both_old, both_sum, load_sem.at[3]),
                pltpu.make_async_copy(down_old, down_sum, load_sem.at[4]),
            ]
        outs = [
            pltpu.make_async_copy(both_low if final else both_sum, both_out, out_sem.at[0]),
            pltpu.make_async_copy(down_sum, down_out, out_sem.at[1]),
        ]

        def pre_in(row):
            return pltpu.make_async_copy(pre_hbm.at[row], pre_ref.at[row], pre_sem.at[row])

        loads[0].start()
        for i in range(fsdp):
            pre_in(i).start()
        loads[1].start()
        for load in later:
            load.start()

        def prepare():
            for load in loads:
                load.wait()
            for i in range(fsdp):
                pre_in(i).wait()

        def spare(unit):
            @pl.when(unit == 0)
            def _():
                for load in later:
                    load.wait()

            if isinstance(unit, int):
                left, right, total, size = weighted_ref, all_ref, down_sum, down_size
                start, count = 0, loops[1]
            else:
                left, right, total, size = in_ref, grad_ref, both_sum, both_size
                start, count = unit * both_step, loops[0]

            def turn(c, carry):
                here = pl.ds(pl.multiple_of(start + c * size, size), size)
                made = lax.dot_general(
                    left[...].reshape(fsdp * band, left.shape[2]),
                    right[:, :, here].reshape(fsdp * band, size),
                    (((0,), (0,)), ((), ())),
                    preferred_element_type=f32,
                )
                if adding:
                    made = made + total[:, here]
                if final and total is both_sum:
                    both_low[:, here] = made.astype(bf16)
                else:
                    total[:, here] = made
                return carry

            lax.fori_loop(0, count, turn, 0)
            if isinstance(unit, int):
                for done in outs:
                    done.start()

        greet(team, True, 0)
        all_ref[team.f, rows_of(team.t, rows)] = (branch_scale * up_ref[...]).astype(bf16)

        def first(row):
            parts[...] = share_parts(share_ref[row], experts)
            share_sum[...] = jnp.zeros_like(share_sum)

            def piece(start, size):
                here, there = pl.ds(start, size), pl.ds(pl.multiple_of(hidden + start, size), size)
                hidden_grad = product_turned(all_ref[row], down_ref[here])
                gate = pre_ref[row, :, here].astype(f32)
                up = pre_ref[row, :, there].astype(f32)
                wide = product(parts[...], map_ref[:, here])
                sigmoid_gate = jax.nn.sigmoid(gate)
                swish = gate * sigmoid_gate
                value = swish * up
                weighted_ref[row, :, here] = (wide * value).astype(bf16)
                both = hidden_grad * value
                high = both.astype(bf16)
                low = (both - high.astype(f32)).astype(bf16)
                share_sum[...] += product(high, pick_ref[here]) + product(low, pick_ref[here])
                scaled = wide * hidden_grad
                grad_ref[row, :, here] = (
                    scaled * up * sigmoid_gate * (1.0 + gate * (1.0 - sigmoid_gate))
                ).astype(bf16)
                grad_ref[row, :, there] = (scaled * swish).astype(bf16)

            chunks(hidden, piece)

        def second(row):
            def piece(start, size):
                here = pl.ds(start, size)
                partial[row, :, here] = product_turned(grad_ref[row], both_ref[here]).astype(bf16)

            chunks(width, piece)
            lane = lax.broadcasted_iota(jnp.int32, (band, LANES), 1)
            partial[row, :, width:] = parted(share_sum[...], lane < experts, lane < 2 * experts)

        total, extra = group_exchange(
            team, all_ref, partial, landing, across, sems, rows, width, experts, prepare, first, second, spare
        )
        lane = lax.broadcasted_iota(jnp.int32, (rows, LANES), 1)
        valid = lane < experts
        share_grad = extra + pltpu.roll(extra, LANES - experts, 1)
        own_share = jnp.where(valid, share_ref[team.f, rows_of(team.t, rows)], 0.0)
        inner = jnp.sum(own_share * share_grad, axis=-1, keepdims=True)
        logit_grad = (own_share * (share_grad - inner)).astype(bf16)
        logit_ref[...] = logit_grad
        norm_grad = total + product_turned(logit_grad, router_ref[...])
        _, normed, inverse = norm_rows(state_ref[...], gain_ref[...])
        back, gain_grad = norm_back(norm_grad, normed, inverse, gain_ref[...])
        gain_out[...] = gain_grad
        state_grad = up_ref[...] + back
        state_out[...] = state_grad
        attn_ref[rows_of(team.t, rows)] = (branch_scale * state_grad).astype(bf16)
        gather_all(team, attn_ref, rows, tg_send, tg_recv)
        for done in outs:
            done.wait()

    args = [upstream, state, share, pre, router, gain_two, gate_up, down, spread_map, pick_map, moe_in]
    if adding:
        args += list(sums)
    return pl.pallas_call(
        kernel,
        out_shape=shapes,
        in_specs=[own] * 3 + [out] + [own] * 2 + [out] * 2 + [own] * 2 + [out] * (len(args) - 10),
        out_specs=[out] * 2 + [own] * 4,
        scratch_shapes=scratch,
        compiler_params=comm_params(number),
        name="moe_backward",
    )(*args)


def team_units(tp):
    return tp.bit_length() - 1


def chunk_size(length, most=512):
    return min(length, most)


def end_layer(sizes, attn_grad, kept, out_twice, w_qkv, layer_in, state_grad, gain, number):
    queries, keys, values, bias, turn = kept
    tp = sizes[2]
    rows, width = layer_in.shape
    band = tp * rows
    kv_heads = keys.shape[1] // LANES
    each = queries.shape[1] // keys.shape[1]
    qkv_width = w_qkv.shape[1]
    query_width = queries.shape[1] * HEAD_SIZE // LANES
    key_width = keys.shape[1] * HEAD_SIZE // LANES
    held = LANES // HEAD_SIZE
    bf16, f32 = jnp.bfloat16, jnp.float32
    dma = pltpu.SemaphoreType.DMA

    def kernel(
        attn_ref, q_ref, k_ref, v_ref, bias_ref, turn_ref, twice_ref, qkv_ref, in_ref, grad_ref, gain_ref,
        out_ref, gain_out, arrived_ref, made_ref,
        heads, sums, sums_in, leaving, tr_send, tr_recv, sec_send, sec_recv,
    ):
        team = Team(sizes)
        barrier = pltpu.get_barrier_semaphore()
        for bit in range(team.bits):
            pl.semaphore_signal(
                barrier, inc=1, device_id={"tp": flipped(team.t, bit)}, device_id_type=MESH
            )
        pl.semaphore_signal(
            barrier,
            inc=1,
            device_id={"section": lax.rem(team.s + 1, team.sections)},
            device_id_type=MESH,
        )
        heads[...] = product_turned(attn_ref[...], twice_ref[...]).astype(bf16)
        lane = lax.broadcasted_iota(jnp.int32, (band, LANES), 1)
        turning = turn_ref[...]

        def turned_back(array):
            array = array * turning
            return array + pltpu.roll(array, HEAD_SIZE, 1)

        def place(start, parts):
            for number in range(0, len(parts), held):
                block = parts[number]
                for other in range(1, held):
                    block = jnp.where(lane < other * HEAD_SIZE, block, parts[number + other])
                where = start + number * HEAD_SIZE
                made_ref[:, where : where + LANES] = block.astype(bf16)

        def lanes_of(number):
            return slice(number * LANES, (number + 1) * LANES)

        query_parts, key_parts, value_parts = [], [], []
        for g in range(kv_heads):
            key, value = k_ref[:, lanes_of(g)], v_ref[:, lanes_of(g)]
            key_sum = jnp.zeros((band, LANES), f32)
            value_sum = jnp.zeros((band, LANES), f32)
            for h in range(g * each, (g + 1) * each):
                query, head = q_ref[:, lanes_of(h)], heads[:, lanes_of(h)]
                scores = product_turned(query, key) * (0.5 * score_scale) + bias_ref[...]
                grown = jnp.exp(scores - jnp.max(scores, axis=-1, keepdims=True))
                weight = grown / jnp.sum(grown, axis=-1, keepdims=True)
                value_sum += product_over_rows(weight.astype(bf16), head)
                weight_grad = product_turned(head, value)
                inner = jnp.sum(weight * weight_grad, axis=-1, keepdims=True)
                score_grad = (weight * (weight_grad - inner) * score_scale).astype(bf16)
                query_parts.append(turned_back(product(score_grad, key)))
                key_sum += product_over_rows(score_grad, query)
            key_parts.append(turned_back(key_sum))
            value_parts.append(value_sum)
        place(0, query_parts)
        place(query_width, key_parts)
        place(query_width + key_width, value_parts)
        sums[...] = product_turned(made_ref[...], qkv_ref[...]).astype(bf16)
        pl.semaphore_wait(barrier, team.bits + 1)
        reduce = scatter_all(team, sums, rows, sums_in, tr_send, tr_recv, width)
        norm_grad = sums[rows_of(team.t, rows)].astype(f32)
        _, normed, inverse = norm_rows(in_ref[...].astype(f32), gain_ref[...])
        back, gain_grad = norm_back(norm_grad, normed, inverse, gain_ref[...])
        result = grad_ref[...] + back
        leaving[...] = result.astype(bf16)
        move = ring_copy(team, -1, leaving, arrived_ref, sec_send, sec_recv)
        move.start()
        gain_out[...] = gain_grad
        out_ref[...] = result
        for one in reduce:
            one.drain()
        move.wait()

    return pl.pallas_call(
        kernel,
        out_shape=[
            jax.ShapeDtypeStruct((rows, width), f32),
            jax.ShapeDtypeStruct((1, width), f32),
            jax.ShapeDtypeStruct((rows, width), bf16),
            jax.ShapeDtypeStruct((band, qkv_width), bf16),
        ],
        in_specs=[WHOLE_VMEM] * 11,
        out_specs=[WHOLE_VMEM] * 4,
        scratch_shapes=[
            pltpu.VMEM((band, queries.shape[1]), bf16),
            pltpu.VMEM((band, width), bf16),
            pltpu.VMEM((tp, rows, width), bf16),
            pltpu.VMEM((rows, width), bf16),
            dma((SLICES * tp,)), dma((SLICES * tp,)), dma((1,)), dma((1,)),
        ],
        compiler_params=comm_params(number),
        name="end_layer",
    )(attn_grad, queries, keys, values, bias, turn, out_twice, w_qkv, layer_in, state_grad, gain)


def plain_copy(array, steps):
    rows, width = array.shape

    def kernel(in_ref, out_ref):
        out_ref[...] = in_ref[...]

    block = pl.BlockSpec((rows // steps, width), lambda i: (i, 0))
    return pl.pallas_call(
        kernel,
        grid=(steps,),
        out_shape=jax.ShapeDtypeStruct(array.shape, array.dtype),
        in_specs=[block],
        out_specs=block,
        name="plain_copy",
    )(array)


def order_map(inputs, outputs, count, part, turned):
    across = count * part
    source = lax.broadcasted_iota(jnp.int32, (inputs, outputs), 1 if turned else 0)
    target = lax.broadcasted_iota(jnp.int32, (inputs, outputs), 0 if turned else 1)
    e, rest = lax.div(source, across), lax.rem(source, across)
    f, h = lax.div(rest, part), lax.rem(rest, part)
    return (f * LANES + e * part + h == target).astype(jnp.bfloat16)


def block_steps(blocks):
    for steps in (2, 1):
        if blocks % steps == 0:
            return steps


def outgoing_experts(w_gate, w_up, count):
    experts, depth, hidden = w_gate.shape
    part = hidden // count
    bunch = LANES // part
    across = bunch * hidden
    steps = block_steps(experts // bunch)
    each = experts // bunch // steps

    def kernel(gate_ref, up_ref, out_ref, table):
        @pl.when((pl.program_id(0) == 0) & (pl.program_id(1) == 0))
        def _():
            table[...] = order_map(across, count * LANES, count, part, False)

        def move(ref):
            for b in range(each):
                lanes = jnp.concatenate([ref[b * bunch + e] for e in range(bunch)], axis=1)
                moved = product(lanes, table[...]).astype(jnp.bfloat16)
                for f in range(count):
                    out_ref[f, :, b * LANES : (b + 1) * LANES] = moved[:, f * LANES : (f + 1) * LANES]

        @pl.when(pl.program_id(0) == 0)
        def _():
            move(gate_ref)

        @pl.when(pl.program_id(0) == 1)
        def _():
            move(up_ref)

    block = (each * bunch, depth, hidden)
    return pl.pallas_call(
        kernel,
        grid=(2, steps),
        out_shape=jax.ShapeDtypeStruct((count, depth, 2 * steps * each * LANES), jnp.bfloat16),
        in_specs=[
            pl.BlockSpec(block, lambda w, b: (jnp.where(w == 0, b, steps - 1), 0, 0)),
            pl.BlockSpec(block, lambda w, b: (jnp.where(w == 1, b, 0), 0, 0)),
        ],
        out_specs=pl.BlockSpec((count, depth, each * LANES), lambda w, b: (0, 0, w * steps + b)),
        scratch_shapes=[pltpu.VMEM((across, count * LANES), jnp.bfloat16)],
        compiler_params=pltpu.CompilerParams(vmem_limit_bytes=VMEM_LIMIT),
        name="outgoing_experts",
    )(w_gate, w_up)


def incoming_experts(both, experts, hidden):
    count, depth, width = both.shape
    part = hidden // count
    bunch = LANES // part
    across = bunch * hidden
    steps = block_steps(experts // bunch)
    each = experts // bunch // steps

    def kernel(in_ref, gate_ref, up_ref, table):
        @pl.when((pl.program_id(0) == 0) & (pl.program_id(1) == 0))
        def _():
            table[...] = order_map(count * LANES, across, count, part, True)

        def store(ref):
            for b in range(each):
                lanes = jnp.concatenate(
                    [in_ref[f, :, b * LANES : (b + 1) * LANES] for f in range(count)], axis=1
                )
                moved = product(lanes, table[...])
                for e in range(bunch):
                    ref[b * bunch + e] = moved[:, e * hidden : (e + 1) * hidden]

        @pl.when(pl.program_id(0) == 0)
        def _():
            store(gate_ref)

        @pl.when(pl.program_id(0) == 1)
        def _():
            store(up_ref)

    shape = jax.ShapeDtypeStruct((experts, depth, hidden), jnp.float32)
    block = (each * bunch, depth, hidden)
    return pl.pallas_call(
        kernel,
        grid=(2, steps),
        out_shape=[shape, shape],
        in_specs=[pl.BlockSpec((count, depth, each * LANES), lambda w, b: (0, 0, w * steps + b))],
        out_specs=[
            pl.BlockSpec(block, lambda w, b: (jnp.where(w == 0, b, steps - 1), 0, 0)),
            pl.BlockSpec(block, lambda w, b: (jnp.where(w == 1, b, 0), 0, 0)),
        ],
        scratch_shapes=[pltpu.VMEM((count * LANES, across), jnp.bfloat16)],
        compiler_params=pltpu.CompilerParams(vmem_limit_bytes=VMEM_LIMIT),
        name="incoming_experts",
    )(both)


def line_barrier(team, tp):
    barrier = pltpu.get_barrier_semaphore()
    count = 0
    for i in range(1, team.fsdp):
        pl.semaphore_signal(
            barrier,
            inc=1,
            device_id={"fsdp": lax.rem(team.f + i, team.fsdp)},
            device_id_type=MESH,
        )
        count += 1
    if tp:
        for bit in range(team.bits):
            pl.semaphore_signal(
                barrier, inc=1, device_id={"tp": flipped(team.t, bit)}, device_id_type=MESH
            )
            count += 1
    pl.semaphore_wait(barrier, count)


def gather_weights(sizes, matrix, small, number):
    fsdp = sizes[1]
    depth, width = matrix.shape
    dma = pltpu.SemaphoreType.DMA

    def kernel(matrix_ref, small_ref, all_ref, few_ref, held, *sems):
        up_send, up_recv, down_send, down_recv, few_send, few_recv, local, out_sem = sems
        team = Team(sizes)
        f = team.f
        mine = pltpu.make_async_copy(matrix_ref, held.at[f], local.at[0])
        mine.start()
        few_ref[f] = small_ref[...]
        line_barrier(team, False)

        def few(i, arriving):
            other = lax.rem(f + (fsdp - i if arriving else i), fsdp)
            part = few_ref.at[other if arriving else f]
            return pltpu.make_async_remote_copy(
                src_ref=part,
                dst_ref=part,
                send_sem=few_send.at[i],
                recv_sem=few_recv.at[i],
                device_id={"fsdp": other},
                device_id_type=MESH,
            )

        for i in range(1, fsdp):
            few(i, False).start()
        mine.wait()

        def hand(block, step):
            sends, recvs = (up_send, up_recv) if step > 0 else (down_send, down_recv)
            return pltpu.make_async_remote_copy(
                src_ref=held.at[block],
                dst_ref=held.at[block],
                send_sem=sends.at[block],
                recv_sem=recvs.at[block],
                device_id={"fsdp": lax.rem(f + step + fsdp, fsdp)},
                device_id_type=MESH,
            )

        def out(block):
            return pltpu.make_async_copy(held.at[block], all_ref.at[block], out_sem.at[block])

        @pl.when(f < fsdp - 1)
        def _():
            hand(f, 1).start()

        @pl.when(f > 0)
        def _():
            hand(f, -1).start()

        out(f).start()

        def step(i, carry):
            below, above = f - i, f + i

            @pl.when(below >= 0)
            def _():
                hand(below, 1).wait_recv()

                @pl.when(f < fsdp - 1)
                def _():
                    hand(below, 1).start()

                out(below).start()

            @pl.when(above < fsdp)
            def _():
                hand(above, -1).wait_recv()

                @pl.when(f > 0)
                def _():
                    hand(above, -1).start()

                out(above).start()

            return carry

        lax.fori_loop(1, fsdp, step, 0)

        def finish(g, carry):
            @pl.when((g <= f) & (f < fsdp - 1))
            def _():
                hand(g, 1).wait_send()

            @pl.when((g >= f) & (f > 0))
            def _():
                hand(g, -1).wait_send()

            out(g).wait()
            return carry

        lax.fori_loop(0, fsdp, finish, 0)
        for i in range(1, fsdp):
            few(i, True).wait_recv()
            few(i, False).wait_send()

    anywhere = pl.BlockSpec(memory_space=pl.ANY)
    return pl.pallas_call(
        kernel,
        out_shape=[
            jax.ShapeDtypeStruct((fsdp, depth, width), matrix.dtype),
            jax.ShapeDtypeStruct((fsdp,) + small.shape, small.dtype),
        ],
        in_specs=[anywhere, WHOLE_VMEM],
        out_specs=[anywhere, WHOLE_VMEM],
        scratch_shapes=[pltpu.VMEM((fsdp, depth, width), matrix.dtype)]
        + [dma((fsdp,)) for _ in range(6)]
        + [dma((1,)), dma((fsdp,))],
        compiler_params=comm_params(number),
        name="gather_weights",
    )(matrix, small)


def reduce_weights(sizes, matrix, small, number):
    tp, fsdp = sizes[2], sizes[1]
    _, depth, width = matrix.shape
    count_rows = small.shape[0]
    portion = small.shape[1] // fsdp
    bits = tp.bit_length() - 1
    bf16, f32 = jnp.bfloat16, jnp.float32
    dma = pltpu.SemaphoreType.DMA

    def kernel(matrix_ref, small_ref, sum_ref, few_ref, up, down, up_in, down_in, few_sum, few_tp, few_cut, few_in, *sems):
        up_send, up_recv, down_send, down_recv, tp_send, tp_recv, few_send, few_recv = sems
        team = Team(sizes)
        f = team.f
        line_barrier(team, True)

        def pass_on(g, step):
            sends, recvs = (up_send, up_recv) if step > 0 else (down_send, down_recv)
            return pltpu.make_async_remote_copy(
                src_ref=(up if step > 0 else down).at[g],
                dst_ref=(up_in if step > 0 else down_in).at[g],
                send_sem=sends.at[g],
                recv_sem=recvs.at[g],
                device_id={"fsdp": lax.rem(f + step + fsdp, fsdp)},
                device_id_type=MESH,
            )

        def tp_copy(bit):
            return pltpu.make_async_remote_copy(
                src_ref=few_sum.at[bit],
                dst_ref=few_tp.at[bit],
                send_sem=tp_send.at[bit],
                recv_sem=tp_recv.at[bit],
                device_id={"tp": flipped(team.t, bit)},
                device_id_type=MESH,
            )

        few_sum[0] = small_ref[...]

        def step(i, carry):
            high, low = fsdp - 1 - i, i

            @pl.when(high > f)
            def _():
                @pl.when(f == 0)
                def _():
                    up[high] = matrix_ref[high]

                @pl.when(f > 0)
                def _():
                    pass_on(high, 1).wait_recv()
                    up[high] = (matrix_ref[high].astype(f32) + up_in[high].astype(f32)).astype(bf16)

                pass_on(high, 1).start()

            @pl.when(low < f)
            def _():
                @pl.when(f == fsdp - 1)
                def _():
                    down[low] = matrix_ref[low]

                @pl.when(f < fsdp - 1)
                def _():
                    pass_on(low, -1).wait_recv()
                    down[low] = (matrix_ref[low].astype(f32) + down_in[low].astype(f32)).astype(bf16)

                pass_on(low, -1).start()

            return carry

        lax.fori_loop(0, fsdp - 1, step, 0)
        for bit in range(bits):
            tp_copy(bit).start()
            tp_copy(bit).wait_recv()
            few_sum[bit + 1] = few_sum[bit] + few_tp[bit]
        for g in range(fsdp):
            few_cut[g] = few_sum[bits, :, g * portion : (g + 1) * portion]

        def few(i, arriving):
            other = lax.rem(f + (fsdp - i if arriving else i), fsdp)
            return pltpu.make_async_remote_copy(
                src_ref=few_cut.at[other],
                dst_ref=few_in.at[i],
                send_sem=few_send.at[i],
                recv_sem=few_recv.at[i],
                device_id={"fsdp": other},
                device_id_type=MESH,
            )

        for i in range(1, fsdp):
            few(i, False).start()
        sum_ref[...] = matrix_ref[f].astype(f32)

        @pl.when(f > 0)
        def _():
            pass_on(f, 1).wait_recv()
            sum_ref[...] += up_in[f].astype(f32)

        @pl.when(f < fsdp - 1)
        def _():
            pass_on(f, -1).wait_recv()
            sum_ref[...] += down_in[f].astype(f32)

        total = few_cut[f]
        for i in range(1, fsdp):
            few(i, True).wait_recv()
            total = total + few_in[i]
        few_ref[...] = total

        def finish(g, carry):
            @pl.when(g > f)
            def _():
                pass_on(g, 1).wait_send()

            @pl.when(g < f)
            def _():
                pass_on(g, -1).wait_send()

            return carry

        lax.fori_loop(0, fsdp, finish, 0)
        for i in range(1, fsdp):
            few(i, False).wait_send()
        for bit in range(bits):
            tp_copy(bit).wait_send()

    return pl.pallas_call(
        kernel,
        out_shape=[
            jax.ShapeDtypeStruct((depth, width), f32),
            jax.ShapeDtypeStruct((count_rows, portion), f32),
        ],
        in_specs=[WHOLE_VMEM] * 2,
        out_specs=[WHOLE_VMEM] * 2,
        scratch_shapes=[pltpu.VMEM((fsdp, depth, width), bf16) for _ in range(4)]
        + [
            pltpu.VMEM((bits + 1,) + small.shape, f32),
            pltpu.VMEM((bits,) + small.shape, f32),
            pltpu.VMEM((fsdp, count_rows, portion), f32),
            pltpu.VMEM((fsdp, count_rows, portion), f32),
        ]
        + [dma((fsdp,)) for _ in range(4)]
        + [dma((tp,)), dma((tp,)), dma((fsdp,)), dma((fsdp,))],
        compiler_params=comm_params(number),
        name="reduce_weights",
    )(matrix, small)


def exchange(blocks):
    return lax.all_to_all(blocks, "fsdp", split_axis=0, concat_axis=0, tiled=True)


def attention_forward(attn_in, segment, w_qkv, w_output):
    query_width = w_output.shape[0]
    key_width = (w_qkv.shape[1] - query_width) // 2
    key_value_heads = key_width // HEAD_SIZE
    count_of_tokens = attn_in.shape[0]
    permitted_mask = allowed_pairs(segment)
    cosine, sine = rope_tables(permitted_mask)
    qkv = jnp.dot(attn_in, w_qkv, preferred_element_type=jnp.float32)
    turned = rotate(
        qkv[:, : query_width + key_width].reshape(count_of_tokens, -1, HEAD_SIZE), cosine, sine
    ).astype(jnp.bfloat16)
    query_rows = turned[:, : query_width // HEAD_SIZE].reshape(
        count_of_tokens, key_value_heads, QUERY_HEADS // KEY_VALUE_HEADS, HEAD_SIZE
    )
    key_matrix = turned[:, query_width // HEAD_SIZE :]
    value_matrix = (
        qkv[:, query_width + key_width :]
        .astype(jnp.bfloat16)
        .reshape(count_of_tokens, key_value_heads, HEAD_SIZE)
    )
    attended = attend(query_rows, key_matrix, value_matrix, permitted_mask)
    mixed_heads = attended.reshape(count_of_tokens, -1)
    partial = jnp.dot(mixed_heads, w_output, preferred_element_type=jnp.float32)
    half = HEAD_SIZE // 2
    beside = jnp.concatenate([turned, turned[..., half:], turned[..., :half]], axis=-1)
    heads = query_width // HEAD_SIZE
    queries = beside[:, :heads].reshape(count_of_tokens, -1)
    keys = beside[:, heads:].reshape(count_of_tokens, -1)
    values = jnp.concatenate([value_matrix, jnp.zeros_like(value_matrix)], axis=-1)
    bias = jnp.where(permitted_mask, 0.0, masked_score).astype(jnp.float32)
    turn = jnp.concatenate([cosine, cosine, sine, -sine], axis=-1)[:, 0]
    kept = (queries, keys, values.reshape(count_of_tokens, -1), bias, turn)
    return (partial.astype(jnp.bfloat16), kept, mixed_heads)


def summed_product(pairs):
    left = jnp.concatenate([pair[0] for pair in pairs], axis=0)
    right = jnp.concatenate([pair[1] for pair in pairs], axis=0)
    return lax.dot_general(
        left, right, (((0,), (0,)), ((), ())), preferred_element_type=jnp.float32
    )


def per_device(
    sizes,
    inputs,
    segment_ids,
    routes,
    w_query,
    key_weight,
    value_weight,
    w_output,
    w_router,
    gain_attn,
    gain_moe,
    w_gate,
    w_up,
    w_down,
    out_grad,
):
    section_count, fsdp_count, tp_count = sizes
    section_index = lax.axis_index("section")
    micro_count, local_rows, model_width = inputs.shape
    depth = w_query.shape[1]
    expert_count = w_router.shape[2]
    hidden_units = w_gate.shape[3]
    own_units = hidden_units // fsdp_count
    hidden = expert_count * own_units
    copies = LANES // expert_count
    query_width = w_query.shape[2]
    key_width = key_weight.shape[2]
    qkv_width = query_width + 2 * key_width
    flat_output = w_output[0].reshape(depth, -1)
    matrix = jnp.concatenate(
        [w_query[0], key_weight[0], value_weight[0], flat_output], axis=1
    )
    few = jnp.concatenate(
        [w_router[0].T, gain_attn.astype(jnp.bfloat16), gain_moe.astype(jnp.bfloat16)], axis=0
    )
    few_rows = -(-few.shape[0] // 16) * 16
    few = jnp.pad(few, ((0, few_rows - few.shape[0]), (0, 0)))
    expert_ids = jnp.arange(expert_count, dtype=jnp.int32)
    chosen_rows = jnp.any(routes[0][..., None] == expert_ids, axis=2).astype(jnp.bfloat16)
    chosen_shape = chosen_rows.shape
    few = jnp.concatenate([few, chosen_rows.reshape(-1, few.shape[1])], axis=0)
    both_out = outgoing_experts(w_gate[0], w_up[0], fsdp_count)
    matrix, few = gather_weights(sizes, matrix, few, 5)
    matrix, few, both_out = lax.optimization_barrier((matrix, few, both_out))
    gate_up = exchange(both_out).reshape(model_width, 2 * hidden)
    matrix = matrix.reshape(model_width, -1)
    chosen_rows = few[:, few_rows:].reshape((fsdp_count,) + chosen_shape)
    few = few[:, :few_rows].transpose(1, 0, 2).reshape(few_rows, model_width)
    w_qkv = matrix[:, :qkv_width]
    out_full = matrix[:, qkv_width:].reshape(-1, model_width)
    out_heads = out_full.reshape(-1, 1, HEAD_SIZE, model_width)
    out_twice = jnp.tile(out_heads, (1, LANES // HEAD_SIZE, 1, 1)).reshape(-1, model_width)
    router = jnp.tile(few[:expert_count].T, (1, copies))
    gain_one = few[expert_count].astype(jnp.float32)[None]
    gain_two = few[expert_count + 1].astype(jnp.float32)[None]
    down = w_down[0].reshape(hidden, model_width)
    lane = jnp.arange(LANES, dtype=jnp.int32)
    owner = jnp.arange(hidden, dtype=jnp.int32) // own_units
    match = (lane % expert_count)[:, None] == owner[None, :]
    spread_map = (match & (lane < 3 * expert_count)[:, None]).astype(jnp.bfloat16)
    pick_map = (match & (lane < 2 * expert_count)[:, None]).astype(jnp.bfloat16).T
    chosen_rows = jnp.tile(chosen_rows, (1, 1, 1, copies))
    segment_rows = segment_ids[:, 0, :]
    tick_count = micro_count + section_count - 1
    outputs = jnp.zeros((micro_count, local_rows, model_width), jnp.bfloat16)
    history = []
    layer_in = jnp.where(section_index == 0, inputs[0], jnp.zeros_like(inputs[0]))
    attn_in = begin_layer(sizes, layer_in, gain_one, 0)
    for tick_step in range(tick_count):
        mb_index = tick_step - section_index
        active = (mb_index >= 0) & (mb_index < micro_count)
        mb_pick = jnp.clip(mb_index, 0, micro_count - 1)
        segment = lax.dynamic_index_in_dim(segment_rows, mb_pick, 0, keepdims=False)
        chosen = lax.dynamic_index_in_dim(chosen_rows, mb_pick, 1, keepdims=False)
        partial, kept, mixed_heads = attention_forward(attn_in, segment, w_qkv, out_full)
        last = tick_step == tick_count - 1
        fresh = None if last else inputs[min(tick_step + 1, micro_count - 1)]
        weights = (router, gain_one, gain_two, gate_up, down, spread_map)
        made = moe_forward(
            sizes, partial, layer_in, chosen, weights, fresh, expert_count, 2 if last else 1
        )
        moe_in, pre, share, state, result = made[:5]
        history.append((attn_in, layer_in, kept, mixed_heads, moe_in, pre, share, state))
        outputs = jnp.where(
            active, lax.dynamic_update_index_in_dim(outputs, result, mb_pick, 0), outputs
        )
        if not last:
            layer_in, attn_in = made[5:]
    input_grads = jnp.zeros((micro_count, local_rows, model_width), jnp.float32)
    gain_sums = None
    all_terms = []
    arrived = None
    place = (lax.axis_index("fsdp"), lax.axis_index("tp") * local_rows, 0)
    for tick_step in range(tick_count):
        mb_index = micro_count + section_count - 2 - tick_step - section_index
        active = (mb_index >= 0) & (mb_index < micro_count)
        mb_pick = jnp.clip(mb_index, 0, micro_count - 1)
        upstream = out_grad[max(micro_count - 1 - tick_step, 0)].astype(jnp.float32)
        if arrived is None:
            arrived = jnp.zeros_like(upstream)
        upstream = jnp.where(
            section_index == section_count - 1, upstream, arrived.astype(jnp.float32)
        )
        upstream = jnp.where(active, upstream, jnp.zeros_like(upstream))
        attn_in, layer_in, kept, mixed_heads, moe_in, pre, share, state = history[tick_count - 1 - tick_step]
        last = tick_step == tick_count - 1
        both_sum, down_sum, logit_grad, gain_two_part, state_grad, attn_grad = moe_backward(
            sizes,
            upstream,
            state,
            share,
            pre,
            moe_in,
            (router, gain_two, gate_up, down, spread_map, pick_map),
            expert_count,
            None if tick_step == 0 else (both_sum, down_sum),
            last,
            7 if tick_step == 0 else 8 if last else 3,
        )
        if last:
            both_sum = exchange(both_sum.reshape(fsdp_count, depth, 2 * hidden))
        grad_out, gain_one_part, arrived, qkv_grad = end_layer(
            sizes, attn_grad, kept, out_twice, w_qkv, layer_in, state_grad, gain_one, 4
        )
        input_grads = jnp.where(
            active, lax.dynamic_update_index_in_dim(input_grads, grad_out, mb_pick, 0), input_grads
        )
        gains = (gain_one_part, gain_two_part)
        gain_sums = gains if gain_sums is None else tuple(a + b for a, b in zip(gain_sums, gains))
        own_rows = lax.dynamic_slice(moe_in, place, (1, local_rows, model_width))[0]
        all_terms.append(
            (
                active,
                (
                    (attn_in, qkv_grad),
                    (mixed_heads, attn_grad),
                    (logit_grad[:, :expert_count], own_rows),
                ),
            )
        )
    chosen_terms = []
    for first in range(micro_count):
        picked = all_terms[first][1]
        for active, terms in all_terms[first + micro_count :: micro_count]:
            picked = jax.tree.map(lambda a, b: jnp.where(active, b, a), picked, terms)
        chosen_terms.append(picked)
    qkv_pairs, output_pairs, router_pairs = zip(*chosen_terms)
    gate_shard, up_shard = incoming_experts(both_sum, expert_count, hidden_units)
    down_shard = down_sum.reshape(expert_count, own_units, model_width)
    small = jnp.concatenate([summed_product(router_pairs)] + list(gain_sums), axis=0)
    small = jnp.pad(small, ((0, few_rows - small.shape[0]), (0, 0)))
    matrix_grad = jnp.concatenate(
        [summed_product(qkv_pairs), summed_product(output_pairs).reshape(model_width, -1)], axis=1
    ).astype(jnp.bfloat16)
    down_sum, matrix_grad = lax.optimization_barrier((plain_copy(down_sum, 4), matrix_grad))
    matrix_grad, few_grad = reduce_weights(
        sizes, matrix_grad.reshape(fsdp_count, depth, -1), small, 6
    )
    shard_sums = (
        matrix_grad[:, :query_width],
        matrix_grad[:, query_width : query_width + key_width],
        matrix_grad[:, query_width + key_width : qkv_width],
        matrix_grad[:, qkv_width:].reshape(-1, model_width),
        few_grad[:expert_count].T,
        few_grad[expert_count],
        few_grad[expert_count + 1],
        gate_shard,
        up_shard,
        down_shard,
    )
    return (outputs[None], input_grads[None]) + tuple((part[None] for part in shard_sums))


def solution(mesh):
    in_specs = (
        P(None, ("fsdp", "tp"), None),
        P(None, "fsdp", None),
        P("section", None, "fsdp", None),
        P("section", "fsdp", "tp"),
        P("section", "fsdp", "tp"),
        P("section", "fsdp", "tp"),
        P("section", ("tp", "fsdp"), None),
        P("section", "fsdp", None),
        P("section", "fsdp"),
        P("section", "fsdp"),
        P("section", None, "fsdp", "tp"),
        P("section", None, "fsdp", "tp"),
        P("section", None, ("tp", "fsdp"), None),
        P(None, ("fsdp", "tp"), None),
    )
    out_specs = (
        P("section", None, ("fsdp", "tp"), None),
        P("section", None, ("fsdp", "tp"), None),
        P("section", "fsdp", "tp"),
        P("section", "fsdp", "tp"),
        P("section", "fsdp", "tp"),
        P("section", ("tp", "fsdp"), None),
        P("section", "fsdp", None),
        P("section", "fsdp"),
        P("section", "fsdp"),
        P("section", None, "fsdp", "tp"),
        P("section", None, "fsdp", "tp"),
        P("section", None, ("tp", "fsdp"), None),
    )
    sizes = tuple(mesh.shape[axis] for axis in ("section", "fsdp", "tp"))
    return jax.shard_map(
        functools.partial(per_device, sizes), mesh=mesh, in_specs=in_specs, out_specs=out_specs, check_vma=False
    )
```
